32 devices in a mesh: dp: 8 (over z, x), mp: 4 (over y, core).
Axes of the slice: x: 2, y: 2, z: 4, core: 2. Of those that a mesh axis runs over, the one named last changes fastest.
Arguments:
- tokens: bfloat16 [8192, 1024], P(('dp', 'mp')), may hold values from -6 to 6
- w_query: bfloat16 [1024, 1024], P(None, 'mp'), may hold values from -0.046875 to 0.046875
- w_key: bfloat16 [1024, 1024], P(None, 'mp'), may hold values from -0.1875 to 0.1875
- w_value: bfloat16 [1024, 1024], P(None, 'mp'), may hold values from -0.1875 to 0.1875
- w_attn_out: bfloat16 [1024, 1024], P('mp'), may hold values from -1 to 1
- w_gate: bfloat16 [1024, 2816], P(None, 'mp'), may hold values from -0.1875 to 0.1875
- w_up: bfloat16 [1024, 2816], P(None, 'mp'), may hold values from -0.1875 to 0.1875
- w_down: bfloat16 [2816, 1024], P('mp'), may hold values from -0.109375 to 0.109375
- norm_attn: float32 [1024], replicated, may hold values from 0.1 to 1.9
- norm_ffn: float32 [1024], replicated, may hold values from 0.1 to 1.9
- rel_table: float32 [32, 16], P(None, 'mp'), may hold values from -3 to 3
- x_table: float32 [32, 16], P(None, 'mp'), may hold values from -3 to 3
- y_table: float32 [32, 16], P(None, 'mp'), may hold values from -3 to 3
- lengths: int32 [8, 2], P('dp'), may hold values from 0 to 1024, as said below
- boxes: int32 [2, 8192], P(None, 'dp'), may hold values from 0 to 127
- cotangent: bfloat16 [8192, 1024], P(('dp', 'mp')), may hold values from -6 to 6
Outputs:
- result: float32 [8192, 1024], P(('dp', 'mp'))
- d_tokens: float32 [8192, 1024], P(('dp', 'mp'))
- grad_query: float32 [1024, 1024], P('dp', 'mp')
- grad_key: float32 [1024, 1024], P('dp', 'mp')
- grad_value: float32 [1024, 1024], P('dp', 'mp')
- grad_attn_out: float32 [1024, 1024], P('mp', 'dp')
- grad_gate: float32 [1024, 2816], P('dp', 'mp')
- grad_up: float32 [1024, 2816], P('dp', 'mp')
- grad_down: float32 [2816, 1024], P('mp', 'dp')
- grad_norm_attn: float32 [1024], P(('dp', 'mp'))
- grad_norm_ffn: float32 [1024], P(('dp', 'mp'))
- grad_rel: float32 [32, 16], P('dp', 'mp')
- grad_x: float32 [32, 16], P('dp', 'mp')
- grad_y: float32 [32, 16], P('dp', 'mp')
The draws below stay inside these ranges and needn't reach their ends.
Inputs may be any that keep to these rules, and one draw needn't show every extreme that they name: `lengths`: in a group whose index modulo 8 is under 5 the odd slots are 0 and the even slots hold 512 to 1024; in the other groups every slot holds 256 to 512. Group 0 has a sequence of 1024 and group 5 one of 512.
All inputs are finite; a program needn't handle non-finite values.
Results may differ from the reference program's by a relative error of at most 0.03.
Values may be sent and summed in bfloat16 or wider, within the bound.
No kernel may reach another device: no remote copies, remote signals or barrier semaphores. Data moves between devices by JAX's collectives and lax.ppermute only.
A program may use at most 832 MiB of HBM per device.

```python
import jax
import jax.numpy as jnp
from jax import lax

D = 1024
HEADS = 16
HEAD = 64
FF = 2816
NB = 32
COORD = 128
LONG = 1024
SHORT = 512
SLOTS = 2
GROUP_TOK = 1024
GROUPS = 8
TOKENS = 8192
N_MP = 4


def draw_lengths(key, part):
    key_long, key_short = jax.random.split(jax.random.fold_in(key, 17))
    group_ids = jnp.arange(GROUPS, dtype=jnp.int32)[:, None]
    slot_ids = jnp.arange(SLOTS, dtype=jnp.int32)[None, :]
    long_len = jax.random.randint(key_long, (GROUPS, SLOTS), SHORT, LONG + 1)
    short_len = jax.random.randint(key_short, (GROUPS, SLOTS), SHORT // 2, SHORT + 1)
    long_len = jnp.where(slot_ids % 2 == 0, long_len, 0)
    long_len = jnp.where((group_ids == 0) & (slot_ids == 0), LONG, long_len)
    short_len = jnp.where((group_ids == 5) & (slot_ids == 0), SHORT, short_len)
    return jnp.where(group_ids % 8 < 5, long_len, short_len).astype(jnp.int32)


def place_ends(result, key, smallest, top_value):
    shape = result.shape
    spot = [jax.random.randint(jax.random.fold_in(key, axis), (), 0, shape[axis]) for axis in range(len(shape))]
    result = result.at[tuple(spot)].set(smallest)
    longest = shape.index(max(shape))
    spot[longest] = (spot[longest] + 1) % shape[longest]
    return result.at[tuple(spot)].set(top_value)


def steps_of(rng, shape, pieces, least, largest):
    level, own = 1.0, jax.random.fold_in(rng, 6)
    for dim, blocks in pieces:
        heights = jnp.exp(jax.random.uniform(jax.random.fold_in(own, dim), (blocks,), jnp.float32, least / len(pieces), largest / len(pieces)))
        level = level * jnp.repeat(heights, shape[dim] // blocks).reshape([-1 if axis == dim else 1 for axis in range(len(shape))])
    return level


def gaussian(stream_key, extent, scale, bound, cuts=(), kind=jnp.bfloat16):
    entries = jax.random.normal(stream_key, extent, jnp.float32) * scale
    if len(cuts) > 0:
        entries = steps_of(stream_key, extent, cuts, -0.22, 0.18) * entries
    return jnp.clip(entries, min=-bound, max=bound).astype(kind)


def setup_inputs(seed: int = 0) -> dict:
    key_of = jax.random.split(jax.random.key(seed), 17)
    tokens = gaussian(key_of[0], (TOKENS, D), 1.0, 6.0, ((0, 32),))
    w_query = gaussian(key_of[1], (D, D), (D * 16) ** -0.5, 0.046875, ((1, 4),))
    w_key = gaussian(key_of[2], (D, D), D ** -0.5, 0.1875, ((1, 4),))
    w_value = gaussian(key_of[3], (D, D), D ** -0.5, 0.1875, ((1, 4),))
    w_attn_out = gaussian(key_of[4], (D, D), (D // 32) ** -0.5, 1.0, ((0, 4),))
    w_gate = gaussian(key_of[5], (D, FF), D ** -0.5, 0.1875, ((1, 4),))
    w_up = gaussian(key_of[6], (D, FF), D ** -0.5, 0.1875, ((1, 4),))
    w_down = gaussian(key_of[7], (FF, D), FF ** -0.5, 0.109375, ((0, 4),))
    norm_attn = jnp.clip(1.0 + 0.18 * jax.random.normal(key_of[8], (D,), jnp.float32), 0.1, 1.9)
    norm_ffn = jnp.clip(1.0 + 0.18 * jax.random.normal(key_of[9], (D,), jnp.float32), 0.1, 1.9)
    rel_table = gaussian(key_of[10], (NB, HEADS), 0.5, 3.0, ((1, 4),), jnp.float32)
    x_table = gaussian(key_of[11], (NB, HEADS), 0.5, 3.0, ((1, 4),), jnp.float32)
    y_table = gaussian(key_of[12], (NB, HEADS), 0.5, 3.0, ((1, 4),), jnp.float32)
    lengths = draw_lengths(jax.random.fold_in(key_of[16], 71), 0)
    boxes = place_ends(jax.random.randint(key_of[14], (2, TOKENS), 0, COORD), jax.random.fold_in(key_of[14], 1), 0, COORD - 1).astype(jnp.int32)
    cotangent = gaussian(key_of[15], (TOKENS, D), 1.0, 6.0, ((0, 32),))
    return {"tokens": tokens, "w_query": w_query, "w_key": w_key, "w_value": w_value, "w_attn_out": w_attn_out, "w_gate": w_gate, "w_up": w_up, "w_down": w_down, "norm_attn": norm_attn, "norm_ffn": norm_ffn, "rel_table": rel_table, "x_table": x_table, "y_table": y_table, "lengths": lengths, "boxes": boxes, "cotangent": cotangent}


thresholds = (1, 2, 3, 4, 5, 6, 7, 8, 12, 16, 23, 32, 46, 64, 91)
norm_eps = 1e-06
masked_score = -1000000000.0
highest = lax.Precision.HIGHEST

@jax.custom_vjp
def low(v):
    return lax.optimization_barrier(v.astype(jnp.bfloat16)).astype(jnp.float32)

@jax.custom_vjp
def low_back(v):
    return v

def low_keep(v):
    return (low(v), None)

def low_pass(kept, grad):
    return (grad,)

def back_keep(v):
    return (v, None)

def back_low(kept, grad):
    return (low(grad),)
low.defvjp(low_keep, low_pass)
low_back.defvjp(back_keep, back_low)

def bucket_of(offsets):
    distance = jnp.abs(offsets)
    bucket_ids = (offsets > 0).astype(jnp.int32) * (NB // 2)
    for threshold in thresholds:
        bucket_ids = bucket_ids + (distance >= threshold).astype(jnp.int32)
    return bucket_ids

def rms_norm(values, gain):
    return values * lax.rsqrt(lax.optimization_barrier(jnp.mean(values * values, axis=-1, keepdims=True)) + norm_eps) * gain

def frame_layout(slot_lengths, group_len):
    positions = jnp.arange(group_len, dtype=jnp.int32)
    slot_ids = jnp.arange(slot_lengths.shape[0], dtype=jnp.int32)
    slot_of = positions // SHORT
    own_length = lax.optimization_barrier(jnp.sum(jnp.where(slot_of[:, None] == slot_ids[None, :], slot_lengths[None, :], 0), axis=1))
    seq_start = jnp.where(own_length > 0, slot_of, slot_of - 1)
    start_length = lax.optimization_barrier(jnp.sum(jnp.where(seq_start[:, None] == slot_ids[None, :], slot_lengths[None, :], 0), axis=1))
    is_valid = positions - seq_start * SHORT < start_length
    return (seq_start, is_valid)

def frame_attention(frame_args, tables):
    queries, keys_in, values_in, seq_start, is_valid, coord_x, coord_y = frame_args
    rel_table, x_table, y_table = tables
    frame_len = queries.shape[0]
    q_heads = queries.reshape(frame_len, HEADS, HEAD)
    k_heads = keys_in.reshape(frame_len, HEADS, HEAD)
    v_heads = values_in.reshape(frame_len, HEADS, HEAD)
    scores = jnp.einsum('qhd,khd->hqk', q_heads, k_heads, precision=highest)
    positions = jnp.arange(frame_len, dtype=jnp.int32)
    bias_all = jnp.take(rel_table, bucket_of(positions[None, :] - positions[:, None]), axis=0)
    bias_all = bias_all + jnp.take(x_table, bucket_of(coord_x[None, :] - coord_x[:, None]), axis=0)
    bias_all = bias_all + jnp.take(y_table, bucket_of(coord_y[None, :] - coord_y[:, None]), axis=0)
    scores = low_back(scores + jnp.transpose(bias_all, (2, 0, 1)))
    allowed = (seq_start[:, None] == seq_start[None, :]) & is_valid[None, :] | (positions[:, None] == positions[None, :])
    scores = jnp.where(allowed[None], scores, masked_score)
    weights = jax.nn.softmax(scores, axis=-1)
    context = jnp.einsum('hqk,khd->qhd', low(weights), v_heads, precision=highest)
    return context.reshape(frame_len, HEADS * HEAD)

def group_forward(inputs, params, seq_start, is_valid, coords):
    w_query, w_key, w_value, w_attn_out, w_gate, w_up, w_down, norm_attn, norm_ffn, rel_table, x_table, y_table = params
    group_len = inputs.shape[0]
    head_cols = D // N_MP
    hidden_cols = FF // N_MP
    normed = low(rms_norm(inputs, norm_attn))
    projected = [[], [], []]
    for member in range(N_MP):
        normed_copy = low_back(normed)
        for which, weight in enumerate((w_query, w_key, w_value)):
            projected[which].append(jnp.dot(normed_copy, weight[:, member * head_cols:(member + 1) * head_cols], precision=highest))
    queries, keys_all, values_all = [low(low_back(jnp.concatenate(parts, axis=1))) for parts in projected]
    frames = group_len // LONG

    def by_frame(array):
        return array.reshape((frames, LONG) + array.shape[1:])
    tables = (rel_table, x_table, y_table)
    context = lax.map(jax.checkpoint(lambda frame_args: frame_attention(frame_args, tables)), (by_frame(queries), by_frame(keys_all), by_frame(values_all), by_frame(seq_start), by_frame(is_valid), by_frame(coords[0]), by_frame(coords[1])))
    context = low(low_back(context.reshape(group_len, D)))
    attn_sum = jnp.zeros_like(inputs)
    for member in range(N_MP):
        lower = member * head_cols
        attn_sum = attn_sum + low(jnp.dot(context[:, lower:lower + head_cols], w_attn_out[lower:lower + head_cols, :], precision=highest))
    mixed = inputs + low_back(attn_sum)
    normed_ffn = low(rms_norm(mixed, norm_ffn))
    ffn_sum = jnp.zeros_like(inputs)
    for member in range(N_MP):
        lower = member * hidden_cols
        normed_copy = low_back(normed_ffn)
        gate_proj = low_back(jnp.dot(normed_copy, w_gate[:, lower:lower + hidden_cols], precision=highest))
        up_proj = low_back(jnp.dot(normed_copy, w_up[:, lower:lower + hidden_cols], precision=highest))
        hidden = low(jax.nn.gelu(gate_proj, approximate=True) * up_proj)
        ffn_sum = ffn_sum + low(jnp.dot(hidden, w_down[lower:lower + hidden_cols, :], precision=highest))
    return mixed + low_back(ffn_sum)

def reference(tokens, w_query, w_key, w_value, w_attn_out, w_gate, w_up, w_down, norm_attn, norm_ffn, rel_table, x_table, y_table, lengths, boxes, cotangent):
    params = tuple((p.astype(jnp.float32) for p in (w_query, w_key, w_value, w_attn_out, w_gate, w_up, w_down, norm_attn, norm_ffn, rel_table, x_table, y_table)))
    token_groups = tokens.astype(jnp.float32).reshape(GROUPS, GROUP_TOK, D)
    grad_groups = cotangent.astype(jnp.float32).reshape(GROUPS, GROUP_TOK, D)
    box_groups = jnp.transpose(boxes.reshape(2, GROUPS, GROUP_TOK), (1, 0, 2))

    def one_group(running, group_args):
        inputs, d_out, slot_lengths, coords = group_args
        seq_start, is_valid = frame_layout(slot_lengths, GROUP_TOK)

        def forward(inputs_in, params_in):
            return group_forward(inputs_in, params_in, seq_start, is_valid, coords)
        output, pull_back = jax.vjp(forward, inputs, params)
        d_inputs, d_params = pull_back(d_out)
        running = jax.tree.map(jnp.add, running, d_params)
        return (running, (output, d_inputs))
    zero_grads = jax.tree.map(jnp.zeros_like, params)
    totals, (outputs, d_inputs) = lax.scan(one_group, zero_grads, (token_groups, grad_groups, lengths, box_groups))
    return (outputs.reshape(TOKENS, D), d_inputs.reshape(TOKENS, D), totals[0], totals[1], totals[2], totals[3], totals[4], totals[5], totals[6], totals[7], totals[8], totals[9], totals[10], totals[11])
```

```python
import functools

import jax
import jax.numpy as jnp
from jax import lax
from jax.experimental import pallas as pl
from jax.experimental.pallas import tpu as pltpu
from jax.sharding import PartitionSpec as P

f32, bf16, i32 = jnp.float32, jnp.bfloat16, jnp.int32
HEAD = 64
NB = 32
COORD = 128
SHORT = 512
NEAR = 3 * COORD
thresholds = (1, 2, 3, 4, 5, 6, 7, 8, 12, 16, 23, 32, 46, 64, 91)
masked_score = -1000000000.0


def dot(a, b):
    return jnp.dot(a, b, preferred_element_type=f32)


def bucket_of(offsets):
    distance = jnp.abs(offsets)
    bucket_ids = jnp.where(offsets > 0, NB // 2, 0)
    for threshold in thresholds:
        bucket_ids = bucket_ids + jnp.where(distance >= threshold, 1, 0)
    return bucket_ids


def offset_hot():
    offsets = lax.broadcasted_iota(i32, (NB, 512), 1) - 256
    return (bucket_of(offsets) == lax.broadcasted_iota(i32, (NB, 512), 0)).astype(f32)


def toeplitz(row, base):
    wide = jnp.broadcast_to(row, (COORD, 512))
    return pltpu.roll(wide, (256 - base) % 512, 1, stride=1, stride_axis=0)


def start_of(len0, len1):
    return jnp.where(len1 > 0, 1, 0), jnp.where(len1 > 0, len1, len0)


def build(lens, tab_ref, box_cols, box_rows, k_ref, b_scr, hot_scr, lut_scr, strip_scr, n_heads):
    n_keys = k_ref.shape[0]
    len0, len1 = lens[0, 0], lens[0, 1]
    start1, start1_len = start_of(len0, len1)
    lane = lax.broadcasted_iota(i32, (n_keys, COORD), 1)
    pos = lax.broadcasted_iota(i32, (n_keys, COORD), 0)
    x_hot = (box_cols[:, 0:1] == lane).astype(bf16)
    y_hot = (box_cols[:, 1:2] == lane).astype(bf16)
    second = pos >= SHORT
    start_k = jnp.where(second, start1, 0)
    limit = jnp.where(second, start1_len, len0)
    valid = pos - start_k * SHORT < limit
    masked0 = jnp.where(valid & (start_k == 0), 0.0, masked_score)
    masked1 = jnp.where(valid & (start_k == start1), 0.0, masked_score)
    extra = jnp.where(lane == 0, masked0, jnp.where(lane == 1, masked1, jnp.where(lane < 5, -1.0, 0.0)))
    extra = extra.astype(bf16)
    for pair in range(n_heads // 2):
        b_scr[pair, :, 0:128] = k_ref[:, pair * 128 : pair * 128 + 128]
        b_scr[pair, :, 128:256] = x_hot
        b_scr[pair, :, 256:384] = y_hot
        b_scr[pair, :, 384:512] = extra
    level = lax.broadcasted_iota(i32, (COORD, n_keys), 0)
    hot_scr[0:128, :] = (box_rows[0:1, :] == level).astype(bf16)
    hot_scr[128:256, :] = (box_rows[1:2, :] == level).astype(bf16)
    vec = jnp.dot(tab_ref[...], offset_hot(), precision=lax.Precision.HIGHEST, preferred_element_type=f32)
    n_strip = strip_scr.shape[1]
    for h in range(n_heads):
        for axis in range(2):
            at = n_heads * (1 + axis) + h
            table = toeplitz(vec[at : at + 1, :], 0)[:, 0:128]
            lut_scr[h, axis] = table.T.astype(bf16)
        near = toeplitz(vec[h : h + 1, :], -128)[:, 0:NEAR]
        mid = (n_strip - NEAR) // 2
        left = jnp.broadcast_to(vec[h : h + 1, 0:1], (mid, COORD))
        right = jnp.broadcast_to(vec[h : h + 1, 511:512], (mid, COORD))
        strip_scr[h, 0:mid, :] = left
        strip_scr[h, mid : mid + NEAR, :] = near.T
        strip_scr[h, mid + NEAR :, :] = right


def query_side(lens, block, qb, h, qt, hot_q, lut_scr, log_rows):
    half = jnp.zeros((HEAD, qb), bf16)
    own = qt[(h % 2) * HEAD : (h % 2) * HEAD + HEAD, :]
    parts = [own, half] if h % 2 == 0 else [half, own]
    x_rows = dot(lut_scr[h, 0], hot_q[0:128, :]).astype(bf16)
    y_rows = dot(lut_scr[h, 1], hot_q[128:256, :]).astype(bf16)
    row = lax.broadcasted_iota(i32, (128, qb), 0)
    q_pos = block * qb + lax.broadcasted_iota(i32, (128, qb), 1)
    slot = jnp.where(q_pos >= SHORT, 1, 0)
    extra = jnp.where(row == slot, 1.0, 0.0)
    if log_rows is not None:
        for piece, value in enumerate(log_rows):
            extra = jnp.where(row == 2 + piece, value, extra)
    return jnp.concatenate(parts + [x_rows, y_rows, extra.astype(bf16)], axis=0)


def pieces(value):
    high = value.astype(bf16).astype(f32)
    rest = value - high
    mid = rest.astype(bf16).astype(f32)
    return high, mid, (rest - mid).astype(bf16).astype(f32)


def scores(lens, block, qb, h, at, b_scr, strip_scr, s_scr):
    n_keys = b_scr.shape[1]
    s = dot(b_scr[h // 2], at)
    blocks = qb // COORD
    top = n_keys // COORD - 1
    for t in range(blocks):
        off = pl.multiple_of((top - (block * blocks + t)) * COORD, COORD)
        s_scr[:, t * 128 : t * 128 + 128] = s[:, t * 128 : t * 128 + 128] + strip_scr[h, pl.ds(off, n_keys), :]
    len0, len1 = lens[0, 0], lens[0, 1]
    start1, start1_len = start_of(len0, len1)
    last = block * qb + qb - 1
    in_second = last >= SHORT
    begin = jnp.where(in_second, start1, 0) * SHORT
    limit = jnp.where(in_second, start1_len, len0)

    @pl.when(last - begin >= limit)
    def _():
        row = lax.broadcasted_iota(i32, at.shape, 0)
        open_at = jnp.where((row == 384) | (row == 385), 0.0, at.astype(f32)).astype(bf16)
        eye = lax.broadcasted_iota(i32, (128, 128), 0) == lax.broadcasted_iota(i32, (128, 128), 1)
        for t in range(blocks):
            rows = pl.ds(pl.multiple_of((block * blocks + t) * 128, 128), 128)
            cols = slice(t * 128, t * 128 + 128)
            own = dot(b_scr[h // 2, rows, :], open_at[:, cols]) + strip_scr[h, top * 128 : top * 128 + 128, :]
            s_scr[rows, cols] = jnp.where(eye, own, s_scr[rows, cols])


def fwd_kernel(n_heads, qb, lens, tab_ref, box_cols, box_rows, q_ref, k_ref, v_ref, ctx_ref, ctxt_ref, lse_ref,
               b_scr, hot_scr, lut_scr, strip_scr, vt_scr, s_scr):
    block = pl.program_id(0)

    @pl.when(block == 0)
    def _():
        build(lens, tab_ref, box_cols, box_rows, k_ref, b_scr, hot_scr, lut_scr, strip_scr, n_heads)
        for pair in range(n_heads // 2):
            vt_scr[pair, 0:128, :] = v_ref[:, pair * 128 : pair * 128 + 128].T
            vt_scr[pair, 128:144, :] = jnp.ones((16, v_ref.shape[0]), bf16)

    hot_q = hot_scr[:, pl.ds(pl.multiple_of(block * qb, qb), qb)]
    for pair in range(n_heads // 2):
        qt = q_ref[:, pair * 128 : pair * 128 + 128].T
        halves = []
        for h in (2 * pair, 2 * pair + 1):
            at = query_side(lens, block, qb, h, qt, hot_q, lut_scr, None)
            scores(lens, block, qb, h, at, b_scr, strip_scr, s_scr)
            s = s_scr[...]
            top = jnp.max(s, axis=0, keepdims=True)
            p = jnp.exp(s - top).astype(bf16)
            out = dot(vt_scr[pair], p)
            total = out[128:129, :]
            halves.append(out[(h % 2) * HEAD : (h % 2) * HEAD + HEAD, :] / total)
            lse_ref[h : h + 1, :] = top + jnp.log(total)
        ctxt = jnp.concatenate(halves, axis=0)
        ctxt_ref[pair * 128 : pair * 128 + 128, :] = ctxt
        ctx_ref[:, pair * 128 : pair * 128 + 128] = ctxt.T.astype(bf16)


def scratch(n_keys, n_heads):
    return [
        pltpu.VMEM((n_heads // 2, n_keys, 512), bf16),
        pltpu.VMEM((256, n_keys), bf16),
        pltpu.VMEM((n_heads, 2, COORD, COORD), bf16),
        pltpu.VMEM((n_heads, 2 * n_keys - COORD, COORD), f32),
    ]


def whole(shape):
    return pl.BlockSpec(shape, lambda i: (0,) * len(shape))


def attend(q, k, v, tables, lengths, box_cols, box_rows, qb=256):
    n_keys, width = k.shape
    n_rows = q.shape[0]
    n_heads = width // HEAD
    return pl.pallas_call(
        functools.partial(fwd_kernel, n_heads, qb),
        out_shape=(
            jax.ShapeDtypeStruct((n_rows, width), bf16),
            jax.ShapeDtypeStruct((width, n_rows), f32),
            jax.ShapeDtypeStruct((8, n_rows), f32),
        ),
        grid=(n_rows // qb,),
        in_specs=[
            pl.BlockSpec(memory_space=pltpu.SMEM),
            whole(tables.shape), whole(box_cols.shape), whole(box_rows.shape),
            pl.BlockSpec((qb, width), lambda i: (i, 0)), whole(k.shape), whole(v.shape),
        ],
        out_specs=(
            pl.BlockSpec((qb, width), lambda i: (i, 0)),
            pl.BlockSpec((width, qb), lambda i: (0, i)),
            pl.BlockSpec((8, qb), lambda i: (0, i)),
        ),
        scratch_shapes=scratch(n_keys, n_heads) + [
            pltpu.VMEM((n_heads // 2, 144, n_keys), bf16),
            pltpu.VMEM((n_keys, qb), f32),
        ],
        compiler_params=pltpu.CompilerParams(dimension_semantics=("arbitrary",), vmem_limit_bytes=56 << 20),
        cost_estimate=pl.CostEstimate(flops=8 * n_heads * n_rows * n_keys * 512, bytes_accessed=4 << 20, transcendentals=n_heads * n_rows * n_keys),
        name="attend",
    )(lengths, tables, box_cols, box_rows, q, k, v)


def skew_sums(tile, base):
    width = tile.shape[1]
    wide = jnp.concatenate([tile, jnp.zeros((128, 512 - width), f32)], axis=1)
    row = lax.broadcasted_iota(i32, (128, 512), 0)
    for bit in range(7):
        wide = jnp.where((row >> bit) & 1 == 1, pltpu.roll(wide, 512 - (1 << bit), 1), wide)
    sums = jnp.sum(wide, axis=0, keepdims=True)
    return pltpu.roll(jnp.broadcast_to(sums, (8, 512)), (256 + base) % 512, 1)[0:1, :]


def bwd_kernel(n_heads, qb, lens, tab_ref, box_cols, box_rows, q_ref, k_ref, v_ref, do_ref, ctxt_ref, lse_ref,
               dq_ref, dk_ref, dv_ref, dtab_ref,
               b_scr, hot_scr, lut_scr, strip_scr, v_scr, kt_scr, s_scr, p_scr, ds_scr, dk_scr, dv_scr, near_scr, lut_acc, far_acc):
    block = pl.program_id(0)
    n_keys = k_ref.shape[0]
    blocks = qb // COORD
    key_blocks = n_keys // COORD

    @pl.when(block == 0)
    def _():
        build(lens, tab_ref, box_cols, box_rows, k_ref, b_scr, hot_scr, lut_scr, strip_scr, n_heads)
        lane = lax.broadcasted_iota(i32, (n_keys, 128), 1)
        minus = jnp.where(lane < 3, -1.0, 0.0).astype(bf16)
        kb = lax.broadcasted_iota(i32, (16, n_keys), 0)
        kp = lax.broadcasted_iota(i32, (16, n_keys), 1)
        for pair in range(n_heads // 2):
            v_scr[pair, :, 0:128] = v_ref[:, pair * 128 : pair * 128 + 128]
            v_scr[pair, :, 128:256] = minus
            kt_scr[pair, 0:128, :] = k_ref[:, pair * 128 : pair * 128 + 128].T
            kt_scr[pair, 128:384, :] = hot_scr[...]
            kt_scr[pair, 384:400, :] = (kp // COORD == kb).astype(bf16)
        dk_scr[...] = jnp.zeros_like(dk_scr)
        dv_scr[...] = jnp.zeros_like(dv_scr)
        near_scr[...] = jnp.zeros_like(near_scr)
        lut_acc[...] = jnp.zeros_like(lut_acc)
        far_acc[...] = jnp.zeros_like(far_acc)
        ds_scr[0:128, :] = jnp.zeros((128, 2 * qb), bf16)
        ds_scr[128 + n_keys :, :] = jnp.zeros((128, 2 * qb), bf16)

    hot_q = hot_scr[:, pl.ds(pl.multiple_of(block * qb, qb), qb)]
    rows_q = pl.ds(pl.multiple_of(block * qb, qb), qb)
    lane_half = lax.broadcasted_iota(i32, (qb, 128), 1) >= HEAD
    for pair in range(n_heads // 2):
        cols = slice(pair * 128, pair * 128 + 128)
        q = q_ref[:, cols]
        do = do_ref[:, cols]
        qt, dot_t = q.T, do.T
        prod = dot_t.astype(f32) * ctxt_ref[cols, :]
        dq_halves = []
        for sub in range(2):
            h = 2 * pair + sub
            mine = slice(sub * HEAD, sub * HEAD + HEAD)
            delta = jnp.sum(prod[mine, :], axis=0, keepdims=True)
            at = query_side(lens, block, qb, h, qt, hot_q, lut_scr, pieces(lse_ref[h : h + 1, :]))
            scores(lens, block, qb, h, at, b_scr, strip_scr, s_scr)
            p = jnp.exp(s_scr[...])
            row = lax.broadcasted_iota(i32, (128, qb), 0)
            extra = jnp.zeros((128, qb), f32)
            for piece, value in enumerate(pieces(delta)):
                extra = jnp.where(row == piece, value, extra)
            none = jnp.zeros((HEAD, qb), bf16)
            own = dot_t[mine, :]
            dat = jnp.concatenate([own, none] if sub == 0 else [none, own], axis=0)
            dp = dot(v_scr[pair], jnp.concatenate([dat, extra.astype(bf16)], axis=0))
            ds = (p * dp).astype(bf16)
            p_scr[:, sub * qb : sub * qb + qb] = p.astype(bf16)
            ds_scr[128 : 128 + n_keys, sub * qb : sub * qb + qb] = ds
            got = dot(kt_scr[pair], ds)
            dq_halves.append(got[mine, :])
            for axis in range(2):
                part = got[128 + 128 * axis : 256 + 128 * axis, :].astype(bf16)
                lut_acc[h, axis] += dot(part, b_scr[pair, rows_q, 128 + 128 * axis : 256 + 128 * axis])
            by_block = got[384:392, :]
            key_block = lax.broadcasted_iota(i32, (8, qb), 0)
            q_block = block * blocks + lax.broadcasted_iota(i32, (8, qb), 1) // COORD
            far_acc[h, 0] += jnp.where(key_block + 1 < q_block, by_block, 0.0)
            far_acc[h, 1] += jnp.where(key_block > q_block + 1, by_block, 0.0)
            for t in range(blocks):
                rows = pl.ds(pl.multiple_of((block * blocks + t) * COORD, COORD), NEAR)
                near_scr[h] += ds_scr[rows, sub * qb + t * 128 : sub * qb + t * 128 + 128].astype(f32)
        dq_ref[:, cols] = jnp.concatenate(dq_halves, axis=0).T.astype(bf16)

        def both(x):
            return jnp.concatenate([jnp.where(lane_half, 0.0, x.astype(f32)), jnp.where(lane_half, x.astype(f32), 0.0)], axis=0).astype(bf16)

        dv_scr[pair] += dot(p_scr[...], both(do))
        dk_scr[pair] += dot(ds_scr[128 : 128 + n_keys, :], both(q))

    @pl.when(block == pl.num_programs(0) - 1)
    def _():
        for pair in range(n_heads // 2):
            cols = slice(pair * 128, pair * 128 + 128)
            dk_ref[:, cols] = dk_scr[pair].astype(bf16)
            dv_ref[:, cols] = dv_scr[pair].astype(bf16)
        offset = lax.broadcasted_iota(i32, (1, 512), 1) - 256
        sums = []
        for h in range(n_heads):
            near = skew_sums(near_scr[h].T, -128)
            left = jnp.sum(far_acc[h, 0], keepdims=True)
            right = jnp.sum(far_acc[h, 1], keepdims=True)
            sums.append(near + jnp.where(offset == -256, left, 0.0) + jnp.where(offset == 255, right, 0.0))
        for axis in range(2):
            for h in range(n_heads):
                sums.append(skew_sums(lut_acc[h, axis].T, 0))
        sums = jnp.concatenate(sums + [jnp.zeros((16 - len(sums), 512), f32)], axis=0)
        dtab_ref[...] = lax.dot_general(offset_hot(), sums, (((1,), (1,)), ((), ())), precision=lax.Precision.HIGHEST, preferred_element_type=f32)


def attend_back(q, k, v, d_ctx, ctxt, lse, tables, lengths, box_cols, box_rows, qb=256):
    n_keys, width = k.shape
    n_rows = q.shape[0]
    n_heads = width // HEAD
    return pl.pallas_call(
        functools.partial(bwd_kernel, n_heads, qb),
        out_shape=(
            jax.ShapeDtypeStruct((n_rows, width), bf16),
            jax.ShapeDtypeStruct((n_keys, width), bf16),
            jax.ShapeDtypeStruct((n_keys, width), bf16),
            jax.ShapeDtypeStruct((NB, 16), f32),
        ),
        grid=(n_rows // qb,),
        in_specs=[
            pl.BlockSpec(memory_space=pltpu.SMEM),
            whole(tables.shape), whole(box_cols.shape), whole(box_rows.shape),
            pl.BlockSpec((qb, width), lambda i: (i, 0)), whole(k.shape), whole(v.shape),
            pl.BlockSpec((qb, width), lambda i: (i, 0)),
            pl.BlockSpec((width, qb), lambda i: (0, i)),
            pl.BlockSpec((8, qb), lambda i: (0, i)),
        ],
        out_specs=(
            pl.BlockSpec((qb, width), lambda i: (i, 0)),
            whole(k.shape), whole(v.shape), whole((NB, 16)),
        ),
        scratch_shapes=scratch(n_keys, n_heads) + [
            pltpu.VMEM((n_heads // 2, n_keys, 256), bf16),
            pltpu.VMEM((n_heads // 2, 400, n_keys), bf16),
            pltpu.VMEM((n_keys, qb), f32),
            pltpu.VMEM((n_keys, 2 * qb), bf16),
            pltpu.VMEM((n_keys + 256, 2 * qb), bf16),
            pltpu.VMEM((n_heads // 2, n_keys, 128), f32),
            pltpu.VMEM((n_heads // 2, n_keys, 128), f32),
            pltpu.VMEM((n_heads, NEAR, COORD), f32),
            pltpu.VMEM((n_heads, 2, COORD, COORD), f32),
            pltpu.VMEM((n_heads, 2, 8, qb), f32),
        ],
        compiler_params=pltpu.CompilerParams(dimension_semantics=("arbitrary",), vmem_limit_bytes=56 << 20),
        cost_estimate=pl.CostEstimate(flops=16 * n_heads * n_rows * n_keys * 512, bytes_accessed=8 << 20, transcendentals=n_heads * n_rows * n_keys),
        name="attend_back",
    )(lengths, tables, box_cols, box_rows, q, k, v, d_ctx, ctxt, lse)


norm_eps = 1e-06


def rms_norm(values, gain):
    return values * lax.rsqrt(jnp.mean(values * values, axis=-1, keepdims=True) + norm_eps) * gain


def contract(left_arr, right_arr, left_dim, right_dim):
    return lax.dot_general(
        left_arr, right_arr, (((left_dim,), (right_dim,)), ((), ())), preferred_element_type=f32
    )


def gated_unit(gate_proj, up_proj):
    return jax.nn.gelu(gate_proj, approximate=True) * up_proj


def local(
    tokens, w_query, w_key, w_value, w_attn_out, w_gate, w_up, w_down, norm_attn, norm_ffn,
    rel_table, x_table, y_table, lengths, boxes, cotangent,
):
    inputs = tokens.astype(f32)
    normed = lax.all_gather(rms_norm(inputs, norm_attn).astype(bf16), "mp", axis=0, tiled=True)
    queries = dot(normed, w_query).astype(bf16)
    keys_all = dot(normed, w_key).astype(bf16)
    values_all = dot(normed, w_value).astype(bf16)
    n_heads = w_query.shape[1] // HEAD
    tables = jnp.concatenate([rel_table.T, x_table.T, y_table.T, jnp.zeros((16 - 3 * n_heads, NB), f32)], axis=0)
    box_cols = boxes.T
    context, ctxt, lse = attend(queries, keys_all, values_all, tables, lengths, box_cols, boxes)
    mixed = inputs + lax.psum_scatter(
        dot(context, w_attn_out).astype(bf16), "mp", scatter_dimension=0, tiled=True
    ).astype(f32)
    normed_ffn = lax.all_gather(rms_norm(mixed, norm_ffn).astype(bf16), "mp", axis=0, tiled=True)
    gate_proj = dot(normed_ffn, w_gate)
    up_proj = dot(normed_ffn, w_up)
    hidden = gated_unit(gate_proj, up_proj).astype(bf16)
    result = mixed + lax.psum_scatter(
        dot(hidden, w_down).astype(bf16), "mp", scatter_dimension=0, tiled=True
    ).astype(f32)
    d_out = cotangent.astype(f32)
    d_full = lax.all_gather(cotangent, "mp", axis=0, tiled=True)
    d_hidden = contract(d_full, w_down, 1, 1)
    grad_down_t = contract(d_full, hidden, 0, 0)
    _, gelu_pull = jax.vjp(gated_unit, gate_proj, up_proj)
    d_gate, d_up = gelu_pull(d_hidden)
    d_gate = d_gate.astype(bf16)
    d_up = d_up.astype(bf16)
    grad_gate = contract(normed_ffn, d_gate, 0, 0)
    grad_up = contract(normed_ffn, d_up, 0, 0)
    ffn_grads = jnp.stack([g.astype(bf16).reshape(lax.axis_size("dp"), -1, g.shape[1]) for g in (grad_gate, grad_up, grad_down_t)], axis=1)
    ffn_sums = lax.psum_scatter(ffn_grads, "dp", scatter_dimension=0, tiled=True)[0].astype(f32)
    d_normed_ffn = lax.psum_scatter(
        (contract(d_gate, w_gate, 1, 1) + contract(d_up, w_up, 1, 1)).astype(bf16),
        "mp", scatter_dimension=0, tiled=True,
    ).astype(f32)
    _, norm_pull = jax.vjp(rms_norm, mixed, norm_ffn)
    d_mixed_part, grad_norm_ffn = norm_pull(d_normed_ffn)
    d_mixed = d_out + d_mixed_part
    d_attn = lax.all_gather(d_mixed.astype(bf16), "mp", axis=0, tiled=True)
    d_context = contract(d_attn, w_attn_out, 1, 1).astype(bf16)
    grad_out_t = contract(d_attn, context, 0, 0)
    d_queries, d_keys, d_values, d_tab = attend_back(
        queries, keys_all, values_all, d_context, ctxt, lse, tables, lengths, box_cols, boxes
    )
    grad_query = contract(normed, d_queries, 0, 0)
    grad_key = contract(normed, d_keys, 0, 0)
    grad_value = contract(normed, d_values, 0, 0)
    attn_grads = jnp.stack([g.astype(bf16).reshape(lax.axis_size("dp"), -1, g.shape[1]) for g in (grad_query, grad_key, grad_value, grad_out_t)], axis=1)
    attn_sums = lax.psum_scatter(attn_grads, "dp", scatter_dimension=0, tiled=True)[0].astype(f32)
    total_rows = contract(d_queries, w_query, 1, 1)
    total_rows = total_rows + contract(d_keys, w_key, 1, 1)
    d_normed = lax.psum_scatter(
        (total_rows + contract(d_values, w_value, 1, 1)).astype(bf16),
        "mp", scatter_dimension=0, tiled=True,
    ).astype(f32)
    _, first_pull = jax.vjp(rms_norm, inputs, norm_attn)
    d_inputs_part, grad_norm_attn = first_pull(d_normed)
    d_tokens = d_mixed + d_inputs_part
    n_dp = lax.axis_size("dp")
    gains = jnp.stack([grad_norm_attn.reshape(n_dp * lax.axis_size("mp"), -1), grad_norm_ffn.reshape(n_dp * lax.axis_size("mp"), -1)], axis=1)
    gains = lax.all_to_all(gains, ("dp", "mp"), split_axis=0, concat_axis=0, tiled=True).sum(axis=0)
    tabs = d_tab[:, : 3 * n_heads].reshape(n_dp, -1, 3, n_heads)
    tabs = lax.all_to_all(tabs, "dp", split_axis=0, concat_axis=0, tiled=True).sum(axis=0)
    return (
        result, d_tokens,
        attn_sums[0], attn_sums[1], attn_sums[2], attn_sums[3].T,
        ffn_sums[0], ffn_sums[1], ffn_sums[2].T,
        gains[0], gains[1], tabs[:, 0], tabs[:, 1], tabs[:, 2],
    )


def solution(mesh):
    in_specs = (
        P(("dp", "mp"), None),
        P(None, "mp"),
        P(None, "mp"),
        P(None, "mp"),
        P("mp", None),
        P(None, "mp"),
        P(None, "mp"),
        P("mp", None),
        P(),
        P(),
        P(None, "mp"),
        P(None, "mp"),
        P(None, "mp"),
        P("dp", None),
        P(None, "dp"),
        P(("dp", "mp"), None),
    )
    out_specs = (
        P(("dp", "mp"), None),
        P(("dp", "mp"), None),
        P("dp", "mp"),
        P("dp", "mp"),
        P("dp", "mp"),
        P("mp", "dp"),
        P("dp", "mp"),
        P("dp", "mp"),
        P("mp", "dp"),
        P(("dp", "mp")),
        P(("dp", "mp")),
        P("dp", "mp"),
        P("dp", "mp"),
        P("dp", "mp"),
    )
    return jax.shard_map(local, mesh=mesh, in_specs=in_specs, out_specs=out_specs, check_vma=False)
```

```python
import functools

import jax
import jax.numpy as jnp
from jax import lax
from jax.experimental import pallas as pl
from jax.experimental.pallas import tpu as pltpu
from jax.sharding import PartitionSpec as P

f32, bf16, i32 = jnp.float32, jnp.bfloat16, jnp.int32
HEAD = 64
NB = 32
COORD = 128
SHORT = 512
NEAR = 3 * COORD
EXTRA = 16
KEYS = 512
thresholds = (1, 2, 3, 4, 5, 6, 7, 8, 12, 16, 23, 32, 46, 64, 91)
masked_score = -1000000000.0


def dot(a, b):
    return jnp.dot(a, b, preferred_element_type=f32)


def dot_nt(a, b):
    return lax.dot_general(a, b, (((1,), (1,)), ((), ())), preferred_element_type=f32)


def dot_tn(a, b):
    return lax.dot_general(a, b, (((0,), (0,)), ((), ())), preferred_element_type=f32)


def bucket_of(offsets):
    distance = jnp.abs(offsets)
    bucket_ids = jnp.where(offsets > 0, NB // 2, 0)
    for threshold in thresholds:
        bucket_ids = bucket_ids + jnp.where(distance >= threshold, 1, 0)
    return bucket_ids


def offset_hot(sign=1):
    offsets = sign * (lax.broadcasted_iota(i32, (NB, 512), 1) - 256)
    return (bucket_of(offsets) == lax.broadcasted_iota(i32, (NB, 512), 0)).astype(f32)


def toeplitz(row, base):
    wide = jnp.broadcast_to(row, (COORD, 512))
    return pltpu.roll(wide, (256 - base) % 512, 1, stride=1, stride_axis=0)


def start_of(len0, len1):
    return jnp.where(len1 > 0, 1, 0), jnp.where(len1 > 0, len1, len0)


def build(lens, tab_ref, box_cols, box_rows, k_ref, b_scr, hot_scr, lut_scr, strip_scr, n_heads):
    n_keys = k_ref.shape[0]
    len0, len1 = lens[0, 0], lens[0, 1]
    start1, start1_len = start_of(len0, len1)
    lane = lax.broadcasted_iota(i32, (n_keys, COORD), 1)
    pos = lax.broadcasted_iota(i32, (n_keys, COORD), 0)
    x_hot = (box_cols[:, 0:1] == lane).astype(bf16)
    y_hot = (box_cols[:, 1:2] == lane).astype(bf16)
    second = pos >= SHORT
    start_k = jnp.where(second, start1, 0)
    limit = jnp.where(second, start1_len, len0)
    valid = pos - start_k * SHORT < limit
    masked0 = jnp.where(valid & (start_k == 0), 0.0, masked_score)
    masked1 = jnp.where(valid & (start_k == start1), 0.0, masked_score)
    extra = jnp.where(lane == 0, masked0, jnp.where(lane == 1, masked1, jnp.where(lane < 5, -1.0, 0.0)))
    extra = extra.astype(bf16)[:, 0:EXTRA]
    for pair in range(n_heads // 2):
        b_scr[pair, :, 0:128] = k_ref[:, pair * 128 : pair * 128 + 128]
        b_scr[pair, :, 128:256] = x_hot
        b_scr[pair, :, 256:384] = y_hot
        b_scr[pair, :, 384 : 384 + EXTRA] = extra
    level = lax.broadcasted_iota(i32, (COORD, n_keys), 0)
    hot_scr[0:128, :] = (box_rows[0:1, :] == level).astype(bf16)
    hot_scr[128:256, :] = (box_rows[1:2, :] == level).astype(bf16)
    vec = jnp.dot(tab_ref[...], offset_hot(), precision=lax.Precision.HIGHEST, preferred_element_type=f32)
    n_strip = strip_scr.shape[1]
    for h in range(n_heads):
        for axis in range(2):
            at = n_heads * (1 + axis) + h
            table = toeplitz(vec[at : at + 1, :], 0)[:, 0:128]
            lut_scr[h, axis] = table.T.astype(bf16)
        near = toeplitz(vec[h : h + 1, :], -128)[:, 0:NEAR]
        mid = (n_strip - NEAR) // 2
        left = jnp.broadcast_to(vec[h : h + 1, 0:1], (mid, COORD))
        right = jnp.broadcast_to(vec[h : h + 1, 511:512], (mid, COORD))
        strip_scr[h, 0:mid, :] = left
        strip_scr[h, mid : mid + NEAR, :] = near.T
        strip_scr[h, mid + NEAR :, :] = right


def query_side(lens, block, qb, h, qt, hot_q, lut_scr, log_rows):
    half = jnp.zeros((HEAD, qb), bf16)
    own = qt[(h % 2) * HEAD : (h % 2) * HEAD + HEAD, :]
    parts = [own, half] if h % 2 == 0 else [half, own]
    x_rows = dot(lut_scr[h, 0], hot_q[0:128, :]).astype(bf16)
    y_rows = dot(lut_scr[h, 1], hot_q[128:256, :]).astype(bf16)
    row = lax.broadcasted_iota(i32, (EXTRA, qb), 0)
    q_pos = block * qb + lax.broadcasted_iota(i32, (EXTRA, qb), 1)
    slot = jnp.where(q_pos >= SHORT, 1, 0)
    extra = jnp.where(row == slot, 1.0, 0.0)
    if log_rows is not None:
        for piece, value in enumerate(log_rows):
            extra = jnp.where(row == 2 + piece, value, extra)
    return jnp.concatenate(parts + [x_rows, y_rows, extra.astype(bf16)], axis=0)


def pieces(value):
    high = value.astype(bf16).astype(f32)
    rest = value - high
    mid = rest.astype(bf16).astype(f32)
    return high, mid, (rest - mid).astype(bf16).astype(f32)


def scores(block, qb, h, at, b_scr, strip_scr, key_at):
    s = dot(b_scr[h // 2, key_at : key_at + KEYS, :], at)
    blocks = qb // COORD
    top = b_scr.shape[1] // COORD - 1
    parts = []
    for t in range(blocks):
        off = pl.multiple_of((top - (block * blocks + t)) * COORD + key_at, COORD)
        parts.append(s[:, t * 128 : t * 128 + 128] + strip_scr[h, pl.ds(off, KEYS), :])
    return jnp.concatenate(parts, axis=1)


def lone(lens, block, qb):
    len0, len1 = lens[0, 0], lens[0, 1]
    start1, start1_len = start_of(len0, len1)
    in_second = block * qb >= SHORT
    begin = jnp.where(in_second, start1, 0) * SHORT
    limit = jnp.where(in_second, start1_len, len0)
    pos = block * qb + lax.broadcasted_iota(i32, (1, qb), 1) - begin
    return block * qb + qb - 1 - begin >= limit, pos >= limit


def own_score(h, qt, kt, strip_scr, lut_scr):
    mine = slice((h % 2) * HEAD, (h % 2) * HEAD + HEAD)
    product = qt[mine, :].astype(f32) * kt[mine, :].astype(f32)
    centre = (strip_scr.shape[1] - COORD) // 2
    bias = strip_scr[h, centre : centre + 1, 0:1] + lut_scr[h, 0, 0:1, 0:1].astype(f32) + lut_scr[h, 1, 0:1, 0:1].astype(f32)
    return jnp.sum(product, axis=0, keepdims=True) + bias


def fwd_kernel(n_heads, qb, base, lens, tab_ref, box_cols, box_rows, q_ref, k_ref, v_ref, *refs):
    ctx_ref, ctxt_ref, lse_ref, out_ref, b_scr, hot_scr, lut_scr, strip_scr, vt_scr, s_scr = refs[-10:]
    n_keys = k_ref.shape[0]
    block = pl.program_id(0) + base

    @pl.when(pl.program_id(0) == 0)
    def _():
        build(lens, tab_ref, box_cols, box_rows, k_ref, b_scr, hot_scr, lut_scr, strip_scr, n_heads)
        for pair in range(n_heads // 2):
            vt_scr[pair, 0:128, :] = v_ref[:, pair * 128 : pair * 128 + 128].T
            vt_scr[pair, 128:144, :] = jnp.ones((16, n_keys), bf16)

    hot_q = hot_scr[:, pl.ds(pl.multiple_of(block * qb, qb), qb)]
    for pair in range(n_heads // 2):
        qt = q_ref[:, pair * 128 : pair * 128 + 128].T
        halves = []
        for h in (2 * pair, 2 * pair + 1):
            at = query_side(lens, block, qb, h, qt, hot_q, lut_scr, None)
            top = None
            for key_at in range(0, n_keys, KEYS):
                s = scores(block, qb, h, at, b_scr, strip_scr, key_at)
                s_scr[h % 2, key_at : key_at + KEYS, :] = s
                high = jnp.max(s, axis=0, keepdims=True)
                top = high if top is None else jnp.maximum(top, high)
            out = None
            for key_at in range(0, n_keys, KEYS):
                p = jnp.exp(s_scr[h % 2, key_at : key_at + KEYS, :] - top).astype(bf16)
                part = dot(vt_scr[pair, :, key_at : key_at + KEYS], p)
                out = part if out is None else out + part
            total = out[128:129, :]
            halves.append(out[(h % 2) * HEAD : (h % 2) * HEAD + HEAD, :] / total)
            lse_ref[h : h + 1, :] = top + jnp.log(total)
        ctxt = jnp.concatenate(halves, axis=0)
        ctxt_ref[pair * 128 : pair * 128 + 128, :] = ctxt
        ctx_ref[:, pair * 128 : pair * 128 + 128] = ctxt.T.astype(bf16)
    some, which = lone(lens, block, qb)

    @pl.when(some)
    def _():
        rows_q = pl.ds(pl.multiple_of(block * qb, qb), qb)
        for pair in range(n_heads // 2):
            cols = slice(pair * 128, pair * 128 + 128)
            qt, kt = q_ref[:, cols].T, k_ref[rows_q, cols].T
            for h in (2 * pair, 2 * pair + 1):
                own = own_score(h, qt, kt, strip_scr, lut_scr)
                log = lse_ref[h : h + 1, :]
                high = jnp.maximum(own, log)
                new = high + jnp.log(jnp.exp(own - high) + jnp.exp(log - high))
                lse_ref[h : h + 1, :] = jnp.where(which, new, log)
                mine = slice(h * HEAD, h * HEAD + HEAD)
                value = vt_scr[pair, (h % 2) * HEAD : (h % 2) * HEAD + HEAD, rows_q].astype(f32)
                old = ctxt_ref[mine, :]
                both = old * jnp.exp(log - new) + value * jnp.exp(own - new)
                ctxt_ref[mine, :] = jnp.where(which, both, old)
            ctx_ref[:, cols] = ctxt_ref[cols, :].T.astype(bf16)

    out_ref[...] = ctx_ref[...]


def scratch(n_keys, n_heads):
    return [
        pltpu.VMEM((n_heads // 2, n_keys, 384 + EXTRA), bf16),
        pltpu.VMEM((256, n_keys), bf16),
        pltpu.VMEM((n_heads, 2, COORD, COORD), bf16),
        pltpu.VMEM((n_heads, 2 * n_keys - COORD, COORD), f32),
    ]


def whole(shape):
    return pl.BlockSpec(shape, lambda *at: (0,) * len(shape))


def params():
    return pltpu.CompilerParams(dimension_semantics=("arbitrary",), vmem_limit_bytes=56 << 20)


def row_block(step, ids):
    return step // 2 * 2 + (step + ids[1]) % 2


def attend(chunk, q, k, v, tables, lengths, box_cols, box_rows, before):
    n_keys, width = k.shape
    qb = n_keys // 4
    n_heads = width // HEAD
    return pl.pallas_call(
        functools.partial(fwd_kernel, n_heads, qb, 2 * chunk),
        out_shape=(
            jax.ShapeDtypeStruct((n_keys, width), bf16),
            jax.ShapeDtypeStruct((width, n_keys), f32),
            jax.ShapeDtypeStruct((8, n_keys), f32),
            jax.ShapeDtypeStruct((2 * qb, width), bf16),
        ),
        grid=(2,),
        in_specs=[
            pl.BlockSpec(memory_space=pltpu.SMEM),
            whole(tables.shape), whole(box_cols.shape), whole(box_rows.shape),
            pl.BlockSpec((qb, width), lambda i: (i + 2 * chunk, 0)), whole(k.shape), whole(v.shape),
        ] + [anywhere()] * len(before),
        out_specs=(
            pl.BlockSpec((qb, width), lambda i: (i + 2 * chunk, 0)),
            pl.BlockSpec((width, qb), lambda i: (0, i + 2 * chunk)),
            pl.BlockSpec((8, qb), lambda i: (0, i + 2 * chunk)),
            pl.BlockSpec((qb, width), lambda i: (i, 0)),
        ),
        scratch_shapes=scratch(n_keys, n_heads) + [
            pltpu.VMEM((n_heads // 2, 144, n_keys), bf16),
            pltpu.VMEM((2, n_keys, qb), f32),
        ],
        input_output_aliases={7 + i: i for i in range(len(before))},
        compiler_params=params(),
        cost_estimate=pl.CostEstimate(flops=7_000_000_000, bytes_accessed=4 << 20, transcendentals=n_heads * 2 * qb * n_keys),
        name="attend",
    )(lengths, tables, box_cols, box_rows, q, k, v, *before)


def skew_sums(tile, base):
    width = tile.shape[1]
    wide = jnp.concatenate([tile, jnp.zeros((128, 512 - width), f32)], axis=1)
    wide = pltpu.roll(wide, (257 - width - base) % 512, 1, stride=1, stride_axis=0)
    return jnp.sum(wide, axis=0, keepdims=True)


def bwd_kernel(n_heads, qb, ids, lens, tab_ref, box_cols, box_rows, q_ref, k_ref, v_ref, d0_ref, d1_ref, d2_ref, d3_ref, wo_ref, ctxt_ref, lse_ref,
               dq_ref, dk_ref, dv_ref, dtab_ref, da_ref,
               b_scr, hot_scr, lut_scr, strip_scr, v_scr, kt_scr, p_scr, ds_scr, dk_scr, dv_scr, near_scr, part_scr, far_acc,
               dot_scr, delta_scr, self_acc):
    step = pl.program_id(0)
    block = row_block(step, ids)
    n_keys = k_ref.shape[0]
    blocks = qb // COORD

    @pl.when(step == 0)
    def _():
        build(lens, tab_ref, box_cols, box_rows, k_ref, b_scr, hot_scr, lut_scr, strip_scr, n_heads)
        lane = lax.broadcasted_iota(i32, (n_keys, 128), 1)
        minus = jnp.where(lane < 3, -1.0, 0.0).astype(bf16)[:, 0:EXTRA]
        level = COORD - 1 - lax.broadcasted_iota(i32, (COORD, n_keys), 0)
        reverse_hot = jnp.concatenate([(box_rows[at : at + 1, :] == level).astype(bf16) for at in (0, 1)], axis=0)
        kb = lax.broadcasted_iota(i32, (16, n_keys), 0)
        kp = lax.broadcasted_iota(i32, (16, n_keys), 1)
        for pair in range(n_heads // 2):
            v_scr[pair, :, 0:128] = v_ref[:, pair * 128 : pair * 128 + 128]
            v_scr[pair, :, 128 : 128 + EXTRA] = minus
            kt_scr[pair, 0:128, :] = k_ref[:, pair * 128 : pair * 128 + 128].T
            kt_scr[pair, 128:384, :] = reverse_hot
            kt_scr[pair, 384:400, :] = (kp // COORD == kb).astype(bf16)
        dk_scr[...] = jnp.zeros_like(dk_scr)
        dv_scr[...] = jnp.zeros_like(dv_scr)
        near_scr[...] = jnp.zeros_like(near_scr)
        far_acc[...] = jnp.zeros_like(far_acc)
        self_acc[...] = jnp.zeros_like(self_acc)
        for pair in range(n_heads // 2):
            ds_scr[pair, 0:128, :] = jnp.zeros((128, 2 * qb), bf16)
            ds_scr[pair, 128 + n_keys :, :] = jnp.zeros((128, 2 * qb), bf16)

    hot_q = hot_scr[:, pl.ds(pl.multiple_of(block * qb, qb), qb)]
    rows_q = pl.ds(pl.multiple_of(block * qb, qb), qb)
    lane_half = lax.broadcasted_iota(i32, (qb, 128), 1) >= HEAD
    for at_step, piece in enumerate((d0_ref, d1_ref, d2_ref, d3_ref)):

        @pl.when(step == at_step)
        def _():
            da_ref[...] = piece[...]

    dot_all = dot_nt(wo_ref[...], da_ref[...]).astype(bf16)
    dot_scr[...] = dot_all
    operands = []
    for pair in range(n_heads // 2):
        cols = slice(pair * 128, pair * 128 + 128)
        dot_t = dot_all[cols, :]
        qt = q_ref[:, cols].T
        prod = dot_t.astype(f32) * ctxt_ref[cols, :]
        for sub in range(2):
            h = 2 * pair + sub
            mine = slice(sub * HEAD, sub * HEAD + HEAD)
            delta = jnp.sum(prod[mine, :], axis=0, keepdims=True)
            delta_scr[h : h + 1, :] = delta
            at = query_side(lens, block, qb, h, qt, hot_q, lut_scr, pieces(lse_ref[h : h + 1, :]))
            row = lax.broadcasted_iota(i32, (EXTRA, qb), 0)
            extra = jnp.zeros((EXTRA, qb), f32)
            for piece, value in enumerate(pieces(delta)):
                extra = jnp.where(row == piece, value, extra)
            none = jnp.zeros((HEAD, qb), bf16)
            own = dot_t[mine, :]
            dat = jnp.concatenate(([own, none] if sub == 0 else [none, own]) + [extra.astype(bf16)], axis=0)
            operands.append((at, dat))
    for h, (at, dat) in enumerate(operands):
        pair, at_q = h // 2, slice(h % 2 * qb, h % 2 * qb + qb)
        for key_at in range(0, n_keys, KEYS):
            p = jnp.exp(scores(block, qb, h, at, b_scr, strip_scr, key_at))
            dp = dot(v_scr[pair, key_at : key_at + KEYS, :], dat)
            p_scr[pair, key_at : key_at + KEYS, at_q] = p.astype(bf16)
            ds_scr[pair, 128 + key_at : 128 + key_at + KEYS, at_q] = (p * dp).astype(bf16)
    key_block = lax.broadcasted_iota(i32, (8, qb), 0)
    q_block = block * blocks + lax.broadcasted_iota(i32, (8, qb), 1) // COORD
    for pair in range(n_heads // 2):
        cols = slice(pair * 128, pair * 128 + 128)
        dq_halves = []
        for sub in range(2):
            h = 2 * pair + sub
            at_q = slice(sub * qb, sub * qb + qb)
            got = dot(kt_scr[pair], ds_scr[pair, 128 : 128 + n_keys, at_q])
            dq_halves.append(got[sub * HEAD : sub * HEAD + HEAD, :])
            part_scr[h, :, rows_q] = got[128:384, :].astype(bf16)
            by_block = got[384:392, :]
            far_acc[h, 0] += jnp.where(key_block + 1 < q_block, by_block, 0.0)
            far_acc[h, 1] += jnp.where(key_block > q_block + 1, by_block, 0.0)
        dq_ref[:, cols] = jnp.concatenate(dq_halves, axis=0).T.astype(bf16)

        def both(x):
            return jnp.concatenate([jnp.where(lane_half, 0.0, x.astype(f32)), jnp.where(lane_half, x.astype(f32), 0.0)], axis=0).astype(bf16)

        dv_scr[pair] += dot(p_scr[pair], both(dot_all[cols, :].T))
        dk_scr[pair] += dot(ds_scr[pair, 128 : 128 + n_keys, :], both(q_ref[:, cols]))
    for h in range(n_heads):
        for t in range(blocks):
            rows = pl.ds(pl.multiple_of((block * blocks + t) * COORD, COORD), NEAR)
            at_q = h % 2 * qb + t * 128
            near_scr[h] += ds_scr[h // 2, rows, at_q : at_q + 128].astype(f32)

    some, which = lone(lens, block, qb)

    @pl.when(some)
    def _():
        for pair in range(n_heads // 2):
            cols = slice(pair * 128, pair * 128 + 128)
            qt, kt, vt = q_ref[:, cols].T, k_ref[rows_q, cols].T, v_ref[rows_q, cols].T
            add_q, add_k, add_v = [], [], []
            for sub in range(2):
                h = 2 * pair + sub
                mine = slice(sub * HEAD, sub * HEAD + HEAD)
                d_out = dot_scr[h * HEAD : h * HEAD + HEAD, :].astype(f32)
                p = jnp.where(which, jnp.exp(own_score(h, qt, kt, strip_scr, lut_scr) - lse_ref[h : h + 1, :]), 0.0)
                dp = jnp.sum(d_out * vt[mine, :].astype(f32), axis=0, keepdims=True) - delta_scr[h : h + 1, :]
                ds = p * dp
                add_q.append(kt[mine, :].astype(f32) * ds)
                add_k.append(qt[mine, :].astype(f32) * ds)
                add_v.append(d_out * p)
                self_acc[h : h + 1, :] += ds
            dq_ref[:, cols] = (dq_ref[:, cols].astype(f32) + jnp.concatenate(add_q, axis=0).T).astype(bf16)
            dk_scr[pair, rows_q, :] += jnp.concatenate(add_k, axis=0).T
            dv_scr[pair, rows_q, :] += jnp.concatenate(add_v, axis=0).T

    @pl.when(step == pl.num_programs(0) - 1)
    def _():
        for pair in range(n_heads // 2):
            cols = slice(pair * 128, pair * 128 + 128)
            dk_ref[:, cols] = dk_scr[pair].astype(bf16)
            dv_ref[:, cols] = dv_scr[pair].astype(bf16)
        offset = 256 - lax.broadcasted_iota(i32, (1, 512), 1)
        row, column = (lax.broadcasted_iota(i32, (NEAR, NEAR), at) for at in (0, 1))
        mirror = (row + column == NEAR - 1).astype(bf16)
        sums = []
        for h in range(n_heads):
            high, rest = pieces(near_scr[h])[0:2]
            near = skew_sums(dot_tn(high.astype(bf16), mirror) + dot_tn(rest.astype(bf16), mirror), -128)
            left = jnp.sum(far_acc[h, 0], keepdims=True)
            right = jnp.sum(far_acc[h, 1], keepdims=True)
            sums.append(near + jnp.where(offset == -255, left, 0.0) + jnp.where(offset == 255, right, 0.0))
        for axis in range(2):
            for h in range(n_heads):
                rows = slice(128 * axis, 128 * axis + 128)
                pairs = dot(part_scr[h, rows, :], b_scr[h // 2, :, 128 + 128 * axis : 256 + 128 * axis])
                sums.append(skew_sums(pairs.T, 0))
        for which_sum in range(len(sums)):
            alone = jnp.sum(self_acc[which_sum % n_heads : which_sum % n_heads + 1, :], keepdims=True)
            sums[which_sum] += jnp.where(offset == 0, alone, 0.0)
        sums = jnp.concatenate(sums + [jnp.zeros((16 - len(sums), 512), f32)], axis=0)
        dtab_ref[...] = lax.dot_general(offset_hot(-1), sums, (((1,), (1,)), ((), ())), precision=lax.Precision.HIGHEST, preferred_element_type=f32)


def attend_back(ids, q, k, v, d_pieces, w_out, ctxt, lse, tables, lengths, box_cols, box_rows):
    n_keys, width = k.shape
    n_rows = q.shape[0]
    n_heads = width // HEAD
    qb = n_rows // 4
    model = w_out.shape[1]
    return pl.pallas_call(
        functools.partial(bwd_kernel, n_heads, qb),
        out_shape=(
            jax.ShapeDtypeStruct((n_rows, width), bf16),
            jax.ShapeDtypeStruct((n_keys, width), bf16),
            jax.ShapeDtypeStruct((n_keys, width), bf16),
            jax.ShapeDtypeStruct((NB, 16), f32),
            jax.ShapeDtypeStruct((n_rows, model), bf16),
        ),
        grid_spec=pltpu.PrefetchScalarGridSpec(
            num_scalar_prefetch=2,
            grid=(4,),
            in_specs=[
                whole(tables.shape), whole(box_cols.shape), whole(box_rows.shape),
                pl.BlockSpec((qb, width), lambda i, ids, lens: (row_block(i, ids), 0)), whole(k.shape), whole(v.shape),
                *[whole(d_pieces[0].shape)] * 4,
                whole(w_out.shape),
                pl.BlockSpec((width, qb), lambda i, ids, lens: (0, row_block(i, ids))),
                pl.BlockSpec((8, qb), lambda i, ids, lens: (0, row_block(i, ids))),
            ],
            out_specs=(
                pl.BlockSpec((qb, width), lambda i, ids, lens: (row_block(i, ids), 0)),
                whole(k.shape), whole(v.shape), whole((NB, 16)),
                pl.BlockSpec((qb, model), lambda i, ids, lens: (row_block(i, ids), 0)),
            ),
            scratch_shapes=scratch(n_keys, n_heads) + [
                pltpu.VMEM((n_heads // 2, n_keys, 128 + EXTRA), bf16),
                pltpu.VMEM((n_heads // 2, 400, n_keys), bf16),
                pltpu.VMEM((n_heads // 2, n_keys, 2 * qb), bf16),
                pltpu.VMEM((n_heads // 2, n_keys + 256, 2 * qb), bf16),
                pltpu.VMEM((n_heads // 2, n_keys, 128), f32),
                pltpu.VMEM((n_heads // 2, n_keys, 128), f32),
                pltpu.VMEM((n_heads, NEAR, COORD), f32),
                pltpu.VMEM((n_heads, 256, n_keys), bf16),
                pltpu.VMEM((n_heads, 2, 8, qb), f32),
                pltpu.VMEM((width, qb), bf16),
                pltpu.VMEM((8, qb), f32),
                pltpu.VMEM((8, qb), f32),
            ],
        ),
        compiler_params=params(),
        cost_estimate=pl.CostEstimate(flops=30_000_000_000, bytes_accessed=8 << 20, transcendentals=n_heads * n_rows * n_keys),
        name="attend_back",
    )(ids, lengths, tables, box_cols, box_rows, q, k, v, *d_pieces, w_out, ctxt, lse)


norm_eps = 1e-06
gelu_scale = 0.7978845608028654
gelu_cube = 0.044715


def scale_of(values):
    return lax.rsqrt(jnp.mean(values * values, axis=-1, keepdims=True) + norm_eps)


def anywhere():
    return pl.BlockSpec(memory_space=pl.ANY)


def estimate(flops, moved):
    return pl.CostEstimate(flops=flops, bytes_accessed=moved, transcendentals=0)


def qkv_kernel(ids, xa_ref, xb_ref, g_ref, wq_ref, wk_ref, wv_ref, *refs):
    xo_ref, n_ref, q_ref, k_ref, v_ref = refs[-5:]
    for at_step, piece in enumerate((xa_ref, xb_ref)):

        @pl.when(pl.program_id(0) == at_step)
        def _():
            xo_ref[...] = piece[...]

    x = xo_ref[...].astype(f32)
    normed = (x * scale_of(x) * g_ref[...]).astype(bf16)
    n_ref[...] = normed
    q_ref[...] = dot(normed, wq_ref[...]).astype(bf16)
    k_ref[...] = dot(normed, wk_ref[...]).astype(bf16)
    v_ref[...] = dot(normed, wv_ref[...]).astype(bf16)


def project(ids, far, pair, gain, weights, before, n_blocks):
    rows, model = pair[0].shape
    width = weights[0].shape[1]

    def row(i, ids):
        chip = 1 - ids[2] if far else ids[2]
        return (2 * chip + (i + ids[1]) % 2, 0)

    shapes = [jax.ShapeDtypeStruct((n_blocks * rows, n), bf16) for n in (model, model, width, width, width)]
    return pl.pallas_call(
        qkv_kernel,
        out_shape=shapes,
        grid_spec=pltpu.PrefetchScalarGridSpec(
            num_scalar_prefetch=1,
            grid=(2,),
            in_specs=[whole(pair[0].shape)] * 2 + [whole(gain.shape)] + [whole(w.shape) for w in weights] + [anywhere()] * len(before),
            out_specs=[pl.BlockSpec((rows, s.shape[1]), row) for s in shapes],
        ),
        input_output_aliases={7 + i: i for i in range(len(before))},
        compiler_params=params(),
        cost_estimate=estimate(12 * rows * model * width, 6 << 20),
        name="project",
    )(ids, *pair, gain, *weights, *before)


def assemble_kernel(ids, *refs):
    for at_step in range(4):

        @pl.when(pl.program_id(0) == at_step)
        def _():
            refs[4][...] = refs[at_step][...]


def assemble(ids, blocks):
    rows, model = blocks[0].shape

    def row(i, ids):
        chip = i // 2
        core = i % 2
        return (2 * ((ids[2] + chip) % 2) + (ids[1] + core) % 2, 0)

    return pl.pallas_call(
        assemble_kernel,
        out_shape=jax.ShapeDtypeStruct((4 * rows, model), bf16),
        grid_spec=pltpu.PrefetchScalarGridSpec(
            num_scalar_prefetch=1,
            grid=(4,),
            in_specs=[whole((rows, model))] * 4,
            out_specs=pl.BlockSpec((rows, model), row),
        ),
        compiler_params=params(),
        cost_estimate=estimate(1, 4 << 20),
        name="assemble",
    )(ids, *blocks)


def ffn_kernel(ids, c0, c1, c2, c3, x_ref, cot_ref, o0, o1, o2, o3, g_ref, wg_ref, wu_ref, wd_ref, *refs):
    mixed_ref, nf_ref, hid_ref, dg_ref, du_ref, dsend, dkeep, rsend, rkeep = refs[-9:]
    mixed = x_ref[...].astype(f32)
    for c, o in ((c0, o0), (c1, o1), (c2, o2), (c3, o3)):
        mixed = mixed + dot(c[...], o[...])
    mixed_ref[...] = mixed
    normed = (mixed * scale_of(mixed) * g_ref[...]).astype(bf16)
    nf_ref[...] = normed
    gate = dot_nt(wg_ref[...], normed)
    up = dot_nt(wu_ref[...], normed)
    d_hidden = dot_nt(wd_ref[...], cot_ref[...])
    square = gate * gate
    t = jnp.tanh(gelu_scale * gate * (1.0 + gelu_cube * square))
    half = 0.5 * (1.0 + t)
    unit = gate * half
    slope = half + 0.5 * gate * (1.0 - t * t) * (gelu_scale * (1.0 + 3.0 * gelu_cube * square))
    hidden = (unit * up).astype(bf16)
    d_gate = (d_hidden * up * slope).astype(bf16)
    d_up = (d_hidden * unit).astype(bf16)
    hid_ref[...] = hidden
    dg_ref[...] = d_gate
    du_ref[...] = d_up
    d_normed = (dot_tn(d_gate, wg_ref[...]) + dot_tn(d_up, wu_ref[...])).astype(bf16)
    down = dot_tn(hidden, wd_ref[...]).astype(bf16)
    step = pl.program_id(0)

    @pl.when(step == 0)
    def _():
        dsend[...] = d_normed
        rsend[...] = down

    @pl.when(step == 1)
    def _():
        dkeep[...] = d_normed
        rkeep[...] = down


def ffn(ids, chunk, contexts, x_all, cot_all, w_outs, gain, w_gate_t, w_up_t, w_down, before):
    total, model = x_all.shape
    rows = total // 4
    width, hidden = contexts[0].shape[1], w_down.shape[0]

    def local_row(i, ids):
        return (i + 1 + ids[1]) % 2

    def row(i, ids):
        return 2 * chunk + local_row(i, ids)

    rows_spec = pl.BlockSpec((rows, model), lambda i, ids: (row(i, ids), 0))
    units_spec = pl.BlockSpec((hidden, rows), lambda i, ids: (0, row(i, ids)))
    kept = [((total, model), f32), ((total, model), bf16)] + [((hidden, total), bf16)] * 3
    sent = [((rows, model), bf16)] * 4
    weights = (*w_outs, gain, w_gate_t, w_up_t, w_down)
    return pl.pallas_call(
        ffn_kernel,
        out_shape=[jax.ShapeDtypeStruct(*s) for s in kept + sent],
        grid_spec=pltpu.PrefetchScalarGridSpec(
            num_scalar_prefetch=1,
            grid=(2,),
            in_specs=[pl.BlockSpec((rows, width), lambda i, ids: (local_row(i, ids), 0))] * 4
            + [rows_spec, rows_spec]
            + [whole(w.shape) for w in weights]
            + [anywhere()] * len(before),
            out_specs=[rows_spec] * 2 + [units_spec] * 3 + [whole(s[0]) for s in sent],
        ),
        input_output_aliases={15 + i: i for i in range(len(before))},
        compiler_params=params(),
        cost_estimate=estimate(4 * rows * model * (model + 6 * hidden), 16 << 20),
        name="ffn",
    )(ids, *contexts, x_all, cot_all, *weights, *before)


def norm_back(total, values, gain):
    r = scale_of(values)
    n = values * r
    e = gain * total
    return r * (e - n * jnp.mean(n * e, axis=-1, keepdims=True)), jnp.sum(total * n, axis=0, keepdims=True)


def mid_kernel(chunk, ids, a_ref, b_ref, mixed_ref, cot_ref, g_ref, dm_ref, da_ref, sum_ref):
    total = a_ref[...].astype(f32) + b_ref[...].astype(f32)
    grad, gain_sum = norm_back(total, mixed_ref[...], g_ref[...])
    d_mixed = cot_ref[...].astype(f32) + grad
    dm_ref[...] = d_mixed
    da_ref[...] = d_mixed.astype(bf16)
    sum_ref[...] = jnp.where(ids[2] == chunk, gain_sum, 0.0)


def mid(ids, chunk, a, b, mixed, cot_all, gain):
    rows, model = a.shape
    spec = pl.BlockSpec((rows, model), lambda i, ids: (2 * chunk + ids[1], 0))
    return pl.pallas_call(
        functools.partial(mid_kernel, chunk),
        out_shape=[
            jax.ShapeDtypeStruct((rows, model), f32),
            jax.ShapeDtypeStruct((rows, model), bf16),
            jax.ShapeDtypeStruct((1, model), f32),
        ],
        grid_spec=pltpu.PrefetchScalarGridSpec(
            num_scalar_prefetch=1,
            grid=(1,),
            in_specs=[whole(a.shape), whole(b.shape), spec, spec, whole(gain.shape)],
            out_specs=[whole((rows, model)), whole((rows, model)), whole((1, model))],
        ),
        compiler_params=params(),
        cost_estimate=estimate(1 << 20, 5 << 20),
        name="mid",
    )(ids, a, b, mixed, cot_all, gain)


def back_kernel(ids, dq_ref, dk_ref, dv_ref, wq_ref, wk_ref, wv_ref, send_ref, keep_ref):
    total = dot_nt(dq_ref[...], wq_ref[...]) + dot_nt(dk_ref[...], wk_ref[...]) + dot_nt(dv_ref[...], wv_ref[...])
    step = pl.program_id(0)

    @pl.when(step == 0)
    def _():
        send_ref[...] = total.astype(bf16)

    @pl.when(step == 1)
    def _():
        keep_ref[...] = total


def project_back(ids, far, grads, weights):
    total, width = grads[0].shape
    rows, model = total // 4, weights[0].shape[0]

    def row(i, ids):
        chip = 1 - ids[2] if far else ids[2]
        return 2 * chip + (i + 1 + ids[1]) % 2

    return pl.pallas_call(
        back_kernel,
        out_shape=[jax.ShapeDtypeStruct((rows, model), bf16), jax.ShapeDtypeStruct((rows, model), f32)],
        grid_spec=pltpu.PrefetchScalarGridSpec(
            num_scalar_prefetch=1,
            grid=(2,),
            in_specs=[pl.BlockSpec((rows, width), lambda i, ids: (row(i, ids), 0))] * 3 + [whole(w.shape) for w in weights],
            out_specs=[whole((rows, model))] * 2,
        ),
        compiler_params=params(),
        cost_estimate=estimate(12 * rows * model * width, 4 << 20),
        name="project_back",
    )(ids, *grads, *weights)


def last_kernel(ids, keep_ref, core_ref, y_ref, x_ref, g_ref, da_ref, db_ref, out_ref, sum_ref):
    total = keep_ref[...] + core_ref[...].astype(f32) + y_ref[...].astype(f32)
    grad, gain_sum = norm_back(total, x_ref[...].astype(f32), g_ref[...])
    out_ref[...] = jnp.where(ids[2] == 0, da_ref[...], db_ref[...]) + grad
    sum_ref[...] = gain_sum


def last(ids, keep, core, far, x, gain, d_mixed):
    shapes = [keep.shape, (1, keep.shape[1])]
    ins = (keep, core, far, x, gain, *d_mixed)
    return pl.pallas_call(
        last_kernel,
        out_shape=[jax.ShapeDtypeStruct(s, f32) for s in shapes],
        grid_spec=pltpu.PrefetchScalarGridSpec(
            num_scalar_prefetch=1,
            grid=(1,),
            in_specs=[whole(a.shape) for a in ins],
            out_specs=[whole(s) for s in shapes],
        ),
        compiler_params=params(),
        cost_estimate=estimate(1 << 20, 6 << 20),
        name="last",
    )(ids, *ins)


def unit_sums_kernel(n, split, *refs):
    out_ref = refs[-1]
    for i in range(n):
        out = dot(refs[i][...], refs[n + i][...]).astype(bf16)
        width = out.shape[1] // split
        for part in range(split):
            out_ref[part, i] = out[:, part * width : part * width + width]


def unit_sums(lefts, rights, shards):
    n = len(lefts)
    total, model = rights[0].shape
    hidden = lefts[0].shape[0]
    cut = model // shards
    step = 256
    split = step // cut if cut % 128 == 0 else 1
    out = pl.pallas_call(
        functools.partial(unit_sums_kernel, n, split),
        out_shape=jax.ShapeDtypeStruct((model // step * split, n, hidden, step // split), bf16),
        grid=(model // step,),
        in_specs=[whole(a.shape) for a in lefts] + [pl.BlockSpec((total, step), lambda i: (0, i))] * n,
        out_specs=pl.BlockSpec((split, n, hidden, step // split), lambda i: (i, 0, 0, 0)),
        compiler_params=params(),
        cost_estimate=estimate(2 * n * total * model * hidden, 16 << 20),
        name="unit_sums",
    )(*lefts, *rights)
    if split == 1:
        out = out.reshape(model // step, n, hidden, step // cut, cut)
        out = out.transpose(0, 3, 1, 2, 4).reshape(shards, n, hidden, cut)
    return out


def bit_orders(shards):
    bits = list(range(shards.bit_length() - 1))
    return bits, bits[1:] + bits[:1]


def slot_of(flip, order):
    place = 0
    for bit in order[1:]:
        place = 2 * place + (flip >> bit) % 2
    return (flip >> order[0]) % 2, place


def head_sums_kernel(shards, groups, ids, *refs):
    n = sum(groups)
    outs, acc = refs[2 * n : -1], refs[-1]
    cut = acc.shape[0] // shards
    at = 0
    for group, (size, order) in enumerate(zip(groups, bit_orders(shards), strict=True)):
        for i in range(size):
            left, right = refs[at], refs[n + at]
            same = at > 0 and i > 0
            acc[...] = dot_tn(left[...], right[...])
            for flip in range(shards):
                sent, place = slot_of(flip, order)
                rows = pl.ds(pl.multiple_of((ids[3] ^ flip) * cut, cut), cut)
                outs[2 * group + sent][place, i] = acc[rows, :].astype(bf16)
            at += 1


def head_sums(ids, lefts, rights, groups, shards):
    total, model = lefts[0].shape
    width = rights[0].shape[1]
    shapes = [(shards // 2, size, model // shards, width) for size in groups for _ in range(2)]
    return pl.pallas_call(
        functools.partial(head_sums_kernel, shards, groups),
        out_shape=[jax.ShapeDtypeStruct(s, bf16) for s in shapes],
        grid_spec=pltpu.PrefetchScalarGridSpec(
            num_scalar_prefetch=1,
            grid=(1,),
            in_specs=[whole(a.shape) for a in (*lefts, *rights)],
            out_specs=[whole(s) for s in shapes],
            scratch_shapes=[pltpu.VMEM((model, width), f32)],
        ),
        compiler_params=params(),
        cost_estimate=estimate(2 * len(lefts) * total * model * width, 8 << 20),
        name="head_sums",
    )(ids, *lefts, *rights)


def exchange_sums(kept, sent, order, n_dp):
    kept = kept.astype(f32)
    for step, bit in enumerate(order):
        came = lax.ppermute(sent, "dp", [(i, i ^ (1 << bit)) for i in range(n_dp)])
        total = kept + came.astype(f32)
        half = total.shape[0] // 2
        if step + 1 < len(order):
            kept, sent = total[:half], total[half:].astype(bf16)
    return total[0]


def local(
    tokens, w_query, w_key, w_value, w_attn_out, w_gate, w_up, w_down, norm_attn, norm_ffn,
    rel_table, x_table, y_table, lengths, boxes, cotangent,
):
    n_mp, n_dp = lax.axis_size("mp"), lax.axis_size("dp")
    me = lax.axis_index("mp")
    core, chip = me % 2, me // 2
    ids = jnp.stack([me, core, chip, lax.axis_index("dp")]).astype(i32)
    rows, model = tokens.shape

    def by_core(a):
        return lax.ppermute(a, "mp", [(i, i ^ 1) for i in range(n_mp)])

    def by_chip(a):
        return lax.ppermute(a, "mp", [(i, i ^ 2) for i in range(n_mp)])

    def after(a, *earlier):
        return lax.optimization_barrier((a, *earlier))[0]

    n_heads = w_query.shape[1] // HEAD
    tables = jnp.concatenate([rel_table.T, x_table.T, y_table.T, jnp.zeros((16 - 3 * n_heads, NB), f32)], axis=0)
    box_cols = boxes.T
    gain_attn, gain_ffn = norm_attn.reshape(1, model), norm_ffn.reshape(1, model)
    weights = (w_query, w_key, w_value)
    w_gate_t, w_up_t = w_gate.T, w_up.T

    x_chip = by_chip(tokens)
    group = project(ids, False, (tokens, by_core(tokens)), gain_attn, weights, [], n_mp)
    x_chip = after(x_chip, group[0])
    x_both = by_core(x_chip)
    w_chip = by_chip(after(w_attn_out, x_chip))
    c_chip = by_chip(after(cotangent, x_chip))
    group = project(ids, True, (x_chip, x_both), gain_attn, weights, group, n_mp)
    x_all, normed, queries, keys_all, values_all = group

    kept, contexts = [], []
    for chunk in range(2):
        *kept, own = attend(chunk, queries, keys_all, values_all, tables, lengths, box_cols, boxes, kept)
        far = by_chip(own)
        contexts.append((own, far))
        if chunk == 0:
            queries = after(queries, own)
    context, ctxt, lse = kept
    w_chip = after(w_chip, own)
    c_chip = after(c_chip, own)
    w_outs = (w_attn_out, by_core(w_attn_out), w_chip, by_core(w_chip))
    cot_all = assemble(ids, (cotangent, by_core(cotangent), c_chip, by_core(c_chip)))

    kept, halves = [], []
    for chunk in range(2):
        own, far = contexts[chunk]
        pieces_in = (own, by_core(own), far, by_core(far))
        out = ffn(ids, chunk, pieces_in, x_all, cot_all, w_outs, gain_ffn, w_gate_t, w_up_t, w_down, kept)
        kept = out[:5]
        halves.append(out[5:])
    mixed_all, normed_ffn, hidden, d_gate, d_up = kept

    d_mixed, d_pieces, gain_sums, sums, fars = [], [], [], [], []
    for chunk in range(2):
        d_send, d_keep, _, _ = halves[chunk]
        chip_sum = (d_keep.astype(f32) + by_core(d_send).astype(f32)).astype(bf16)
        sums.append(chip_sum)
        fars.append(by_chip(chip_sum))
    ffn_grads = unit_sums((d_gate, d_up, hidden), (normed_ffn, normed_ffn, after(cot_all, sums[1])), n_dp)
    for chunk in range(2):
        far = after(fars[chunk], ffn_grads) if chunk else fars[chunk]
        dm, da, gs = mid(ids, chunk, sums[chunk], far, mixed_all, cot_all, gain_ffn)
        d_mixed.append(dm)
        d_pieces += [da, by_core(da)]
        gain_sums.append(gs)
    ffn_sums = lax.psum_scatter(ffn_grads, "dp", scatter_dimension=0, tiled=True)[0].astype(f32)

    chip_sums = []
    for chunk in range(2):
        r_send = after(halves[chunk][2], ffn_grads)
        chip_sums.append((halves[chunk][3].astype(f32) + by_core(r_send).astype(f32)).astype(bf16))
    r_out = after(jnp.where(chip == 0, chip_sums[1], chip_sums[0]), fars[1])
    r_far = by_chip(r_out)
    d_pieces[3] = after(d_pieces[3], r_out)

    d_queries, d_keys, d_values, d_tab, d_attn = attend_back(
        ids, queries, keys_all, values_all, d_pieces, w_attn_out, ctxt, lse, tables, lengths, box_cols, boxes
    )
    d_queries, r_far = lax.optimization_barrier((d_queries, r_far))
    mixed_own = lax.dynamic_slice_in_dim(mixed_all, me * rows, rows, 0)
    result = mixed_own + jnp.where(chip == 0, chip_sums[0], chip_sums[1]).astype(f32) + r_far.astype(f32)
    d_heads = (d_queries, d_keys, d_values)
    attn_grads = head_sums(ids, (normed, normed, normed, d_attn), (*d_heads, context), (2, 2), n_dp)
    f_send, f_keep = project_back(ids, True, d_heads, weights)
    f_sum = (f_keep + by_core(f_send).astype(f32)).astype(bf16)
    far = by_chip(f_sum)
    n_send, n_keep = project_back(ids, False, d_heads, weights)
    d_tokens, gain_first = last(ids, n_keep, by_core(n_send), far, tokens, gain_attn, d_mixed)
    attn_sums = [
        exchange_sums(attn_grads[2 * i], attn_grads[2 * i + 1], order, n_dp) for i, order in enumerate(bit_orders(n_dp))
    ]

    gains = jnp.concatenate([gain_first, gain_sums[0] + gain_sums[1]], axis=0).reshape(2, n_dp, n_mp, -1).transpose(1, 2, 0, 3)
    n_gain = gains.shape[3]
    tabs = d_tab[:, : 3 * n_heads].reshape(n_dp, 1, -1)
    tabs = jnp.where(lax.broadcasted_iota(i32, (1, n_mp, 1), 1) == me, tabs, 0.0)
    small = jnp.concatenate([gains.reshape(n_dp, n_mp, 2 * n_gain), tabs], axis=2).reshape(n_dp * n_mp, -1)
    small = lax.all_to_all(small, ("dp", "mp"), split_axis=0, concat_axis=0, tiled=True).sum(axis=0)
    tabs = small[2 * n_gain :].reshape(-1, 3, n_heads)
    return (
        result, d_tokens,
        attn_sums[0][0], attn_sums[0][1], attn_sums[1][0], attn_sums[1][1].T,
        ffn_sums[0].T, ffn_sums[1].T, ffn_sums[2],
        small[:n_gain], small[n_gain : 2 * n_gain], tabs[:, 0], tabs[:, 1], tabs[:, 2],
    )


def solution(mesh):
    in_specs = (
        P(("dp", "mp"), None),
        P(None, "mp"),
        P(None, "mp"),
        P(None, "mp"),
        P("mp", None),
        P(None, "mp"),
        P(None, "mp"),
        P("mp", None),
        P(),
        P(),
        P(None, "mp"),
        P(None, "mp"),
        P(None, "mp"),
        P("dp", None),
        P(None, "dp"),
        P(("dp", "mp"), None),
    )
    out_specs = (
        P(("dp", "mp"), None),
        P(("dp", "mp"), None),
        P("dp", "mp"),
        P("dp", "mp"),
        P("dp", "mp"),
        P("mp", "dp"),
        P("dp", "mp"),
        P("dp", "mp"),
        P("mp", "dp"),
        P(("dp", "mp")),
        P(("dp", "mp")),
        P("dp", "mp"),
        P("dp", "mp"),
        P("dp", "mp"),
    )
    return jax.shard_map(local, mesh=mesh, in_specs=in_specs, out_specs=out_specs, check_vma=False)
```

```python
import functools

import jax
import jax.numpy as jnp
from jax import lax
from jax.experimental import pallas as pl
from jax.experimental.pallas import tpu as pltpu
from jax.sharding import PartitionSpec as P

f32, bf16, i32 = jnp.float32, jnp.bfloat16, jnp.int32
HEAD = 64
NB = 32
COORD = 128
SHORT = 512
NEAR = 3 * COORD
EXTRA = 16
KEYS = 512
thresholds = (1, 2, 3, 4, 5, 6, 7, 8, 12, 16, 23, 32, 46, 64, 91)
masked_score = -1000000000.0


def dot(a, b):
    return jnp.dot(a, b, preferred_element_type=f32)


def dot_nt(a, b):
    return lax.dot_general(a, b, (((1,), (1,)), ((), ())), preferred_element_type=f32)


def dot_tn(a, b):
    return lax.dot_general(a, b, (((0,), (0,)), ((), ())), preferred_element_type=f32)


def bucket_of(offsets):
    distance = jnp.abs(offsets)
    bucket_ids = jnp.where(offsets > 0, NB // 2, 0)
    for threshold in thresholds:
        bucket_ids = bucket_ids + jnp.where(distance >= threshold, 1, 0)
    return bucket_ids


def offset_hot(sign=1):
    offsets = sign * (lax.broadcasted_iota(i32, (NB, 512), 1) - 256)
    return (bucket_of(offsets) == lax.broadcasted_iota(i32, (NB, 512), 0)).astype(f32)


def toeplitz(row, base):
    wide = jnp.broadcast_to(row, (COORD, 512))
    return pltpu.roll(wide, (256 - base) % 512, 1, stride=1, stride_axis=0)


def start_of(len0, len1):
    return jnp.where(len1 > 0, 1, 0), jnp.where(len1 > 0, len1, len0)


def build(lens, tab_ref, box_cols, box_rows, k_ref, b_scr, hot_scr, lut_scr, strip_scr, n_heads, first=0, in_all=None):
    n_keys = k_ref.shape[0]
    len0, len1 = lens[0, 0], lens[0, 1]
    start1, start1_len = start_of(len0, len1)
    lane = lax.broadcasted_iota(i32, (n_keys, COORD), 1)
    pos = lax.broadcasted_iota(i32, (n_keys, COORD), 0)
    x_hot = (box_cols[:, 0:1] == lane).astype(bf16)
    y_hot = (box_cols[:, 1:2] == lane).astype(bf16)
    second = pos >= SHORT
    start_k = jnp.where(second, start1, 0)
    limit = jnp.where(second, start1_len, len0)
    valid = pos - start_k * SHORT < limit
    masked0 = jnp.where(valid & (start_k == 0), 0.0, masked_score)
    masked1 = jnp.where(valid & (start_k == start1), 0.0, masked_score)
    extra = jnp.where(lane == 0, masked0, jnp.where(lane == 1, masked1, jnp.where(lane < 5, -1.0, 0.0)))
    extra = extra.astype(bf16)[:, 0:EXTRA]
    for pair in range(n_heads // 2):
        b_scr[pair, :, 0:128] = k_ref[:, pair * 128 : pair * 128 + 128]
        b_scr[pair, :, 128:256] = x_hot
        b_scr[pair, :, 256:384] = y_hot
        b_scr[pair, :, 384 : 384 + EXTRA] = extra
    level = lax.broadcasted_iota(i32, (COORD, n_keys), 0)
    hot_scr[0:128, :] = (box_rows[0:1, :] == level).astype(bf16)
    hot_scr[128:256, :] = (box_rows[1:2, :] == level).astype(bf16)
    vec = jnp.dot(tab_ref[...], offset_hot(), precision=lax.Precision.HIGHEST, preferred_element_type=f32)
    n_strip = strip_scr.shape[1]
    for h in range(n_heads):
        for axis in range(2):
            at = (in_all or n_heads) * (1 + axis) + first + h
            table = toeplitz(vec[at : at + 1, :], 0)[:, 0:128]
            lut_scr[h, axis] = table.T.astype(bf16)
        row = vec[first + h : first + h + 1, :]
        near = toeplitz(row, -128)[:, 0:NEAR]
        mid = (n_strip - NEAR) // 2
        left = jnp.broadcast_to(row[:, 0:1], (mid, COORD))
        right = jnp.broadcast_to(row[:, 511:512], (mid, COORD))
        strip_scr[h, 0:mid, :] = left
        strip_scr[h, mid : mid + NEAR, :] = near.T
        strip_scr[h, mid + NEAR :, :] = right


def query_side(lens, block, qb, h, qt, hot_q, lut_scr, log_rows):
    half = jnp.zeros((HEAD, qb), bf16)
    own = qt[(h % 2) * HEAD : (h % 2) * HEAD + HEAD, :]
    parts = [own, half] if h % 2 == 0 else [half, own]
    x_rows = dot(lut_scr[h, 0], hot_q[0:128, :]).astype(bf16)
    y_rows = dot(lut_scr[h, 1], hot_q[128:256, :]).astype(bf16)
    row = lax.broadcasted_iota(i32, (EXTRA, qb), 0)
    q_pos = block * qb + lax.broadcasted_iota(i32, (EXTRA, qb), 1)
    slot = jnp.where(q_pos >= SHORT, 1, 0)
    extra = jnp.where(row == slot, 1.0, 0.0)
    if log_rows is not None:
        for piece, value in enumerate(log_rows):
            extra = jnp.where(row == 2 + piece, value, extra)
    return jnp.concatenate(parts + [x_rows, y_rows, extra.astype(bf16)], axis=0)


def pieces(value):
    high = value.astype(bf16).astype(f32)
    rest = value - high
    mid = rest.astype(bf16).astype(f32)
    return high, mid, (rest - mid).astype(bf16).astype(f32)


def scores(block, qb, h, at, b_scr, strip_scr, key_at):
    s = dot(b_scr[h // 2, key_at : key_at + KEYS, :], at)
    blocks = qb // COORD
    top = b_scr.shape[1] // COORD - 1
    parts = []
    for t in range(blocks):
        off = pl.multiple_of((top - (block * blocks + t)) * COORD + key_at, COORD)
        parts.append(s[:, t * 128 : t * 128 + 128] + strip_scr[h, pl.ds(off, KEYS), :])
    return jnp.concatenate(parts, axis=1)


def lone(lens, block, qb):
    len0, len1 = lens[0, 0], lens[0, 1]
    start1, start1_len = start_of(len0, len1)
    in_second = block * qb >= SHORT
    begin = jnp.where(in_second, start1, 0) * SHORT
    limit = jnp.where(in_second, start1_len, len0)
    pos = block * qb + lax.broadcasted_iota(i32, (1, qb), 1) - begin
    return block * qb + qb - 1 - begin >= limit, pos >= limit


def own_score(h, qt, kt, strip_scr, lut_scr):
    mine = slice((h % 2) * HEAD, (h % 2) * HEAD + HEAD)
    product = qt[mine, :].astype(f32) * kt[mine, :].astype(f32)
    centre = (strip_scr.shape[1] - COORD) // 2
    bias = strip_scr[h, centre : centre + 1, 0:1] + lut_scr[h, 0, 0:1, 0:1].astype(f32) + lut_scr[h, 1, 0:1, 0:1].astype(f32)
    return jnp.sum(product, axis=0, keepdims=True) + bias


def fwd_kernel(n_heads, qb, base, lens, tab_ref, box_cols, box_rows, q_ref, k_ref, v_ref, *refs):
    ctx_ref, ctxt_ref, lse_ref, out_ref, b_scr, hot_scr, lut_scr, strip_scr, vt_scr, s_scr = refs[-10:]
    n_keys = k_ref.shape[0]
    block = pl.program_id(0) + base

    @pl.when(pl.program_id(0) == 0)
    def _():
        build(lens, tab_ref, box_cols, box_rows, k_ref, b_scr, hot_scr, lut_scr, strip_scr, n_heads)
        for pair in range(n_heads // 2):
            vt_scr[pair, 0:128, :] = v_ref[:, pair * 128 : pair * 128 + 128].T
            vt_scr[pair, 128:144, :] = jnp.ones((16, n_keys), bf16)

    hot_q = hot_scr[:, pl.ds(pl.multiple_of(block * qb, qb), qb)]
    for pair in range(n_heads // 2):
        qt = q_ref[:, pair * 128 : pair * 128 + 128].T
        halves = []
        for h in (2 * pair, 2 * pair + 1):
            at = query_side(lens, block, qb, h, qt, hot_q, lut_scr, None)
            top = None
            for key_at in range(0, n_keys, KEYS):
                s = scores(block, qb, h, at, b_scr, strip_scr, key_at)
                s_scr[h % 2, key_at : key_at + KEYS, :] = s
                high = jnp.max(s, axis=0, keepdims=True)
                top = high if top is None else jnp.maximum(top, high)
            out = None
            for key_at in range(0, n_keys, KEYS):
                p = jnp.exp(s_scr[h % 2, key_at : key_at + KEYS, :] - top).astype(bf16)
                part = dot(vt_scr[pair, :, key_at : key_at + KEYS], p)
                out = part if out is None else out + part
            total = out[128:129, :]
            halves.append(out[(h % 2) * HEAD : (h % 2) * HEAD + HEAD, :] / total)
            lse_ref[h : h + 1, :] = top + jnp.log(total)
        ctxt = jnp.concatenate(halves, axis=0)
        ctxt_ref[pair * 128 : pair * 128 + 128, :] = ctxt
        ctx_ref[:, pair * 128 : pair * 128 + 128] = ctxt.T.astype(bf16)
    some, which = lone(lens, block, qb)

    @pl.when(some)
    def _():
        rows_q = pl.ds(pl.multiple_of(block * qb, qb), qb)
        for pair in range(n_heads // 2):
            cols = slice(pair * 128, pair * 128 + 128)
            qt, kt = q_ref[:, cols].T, k_ref[rows_q, cols].T
            for h in (2 * pair, 2 * pair + 1):
                own = own_score(h, qt, kt, strip_scr, lut_scr)
                log = lse_ref[h : h + 1, :]
                high = jnp.maximum(own, log)
                new = high + jnp.log(jnp.exp(own - high) + jnp.exp(log - high))
                lse_ref[h : h + 1, :] = jnp.where(which, new, log)
                mine = slice(h * HEAD, h * HEAD + HEAD)
                value = vt_scr[pair, (h % 2) * HEAD : (h % 2) * HEAD + HEAD, rows_q].astype(f32)
                old = ctxt_ref[mine, :]
                both = old * jnp.exp(log - new) + value * jnp.exp(own - new)
                ctxt_ref[mine, :] = jnp.where(which, both, old)
            ctx_ref[:, cols] = ctxt_ref[cols, :].T.astype(bf16)

    out_ref[...] = ctx_ref[...]


def scratch(n_keys, n_heads):
    return [
        pltpu.VMEM((n_heads // 2, n_keys, 384 + EXTRA), bf16),
        pltpu.VMEM((256, n_keys), bf16),
        pltpu.VMEM((n_heads, 2, COORD, COORD), bf16),
        pltpu.VMEM((n_heads, 2 * n_keys - COORD, COORD), f32),
    ]


def whole(shape):
    return pl.BlockSpec(shape, lambda *at: (0,) * len(shape))


def params():
    return pltpu.CompilerParams(dimension_semantics=("arbitrary",), vmem_limit_bytes=62 << 20)


def row_block(step, ids):
    return step // 2 * 2 + (step + ids[1]) % 2


def attend(chunk, q, k, v, tables, lengths, box_cols, box_rows, before):
    n_keys, width = k.shape
    qb = n_keys // 4
    n_heads = width // HEAD
    return pl.pallas_call(
        functools.partial(fwd_kernel, n_heads, qb, 2 * chunk),
        out_shape=(
            jax.ShapeDtypeStruct((n_keys, width), bf16),
            jax.ShapeDtypeStruct((width, n_keys), f32),
            jax.ShapeDtypeStruct((8, n_keys), f32),
            jax.ShapeDtypeStruct((2 * qb, width), bf16),
        ),
        grid=(2,),
        in_specs=[
            pl.BlockSpec(memory_space=pltpu.SMEM),
            whole(tables.shape), whole(box_cols.shape), whole(box_rows.shape),
            pl.BlockSpec((qb, width), lambda i: (i + 2 * chunk, 0)), whole(k.shape), whole(v.shape),
        ] + [anywhere()] * len(before),
        out_specs=(
            pl.BlockSpec((qb, width), lambda i: (i + 2 * chunk, 0)),
            pl.BlockSpec((width, qb), lambda i: (0, i + 2 * chunk)),
            pl.BlockSpec((8, qb), lambda i: (0, i + 2 * chunk)),
            pl.BlockSpec((qb, width), lambda i: (i, 0)),
        ),
        scratch_shapes=scratch(n_keys, n_heads) + [
            pltpu.VMEM((n_heads // 2, 144, n_keys), bf16),
            pltpu.VMEM((2, n_keys, qb), f32),
        ],
        input_output_aliases={7 + i: i for i in range(len(before))},
        compiler_params=params(),
        cost_estimate=estimate(),
        name="attend",
    )(lengths, tables, box_cols, box_rows, q, k, v, *before)


def skew_sums(tile, base):
    width = tile.shape[1]
    wide = jnp.concatenate([tile, jnp.zeros((128, 512 - width), f32)], axis=1)
    wide = pltpu.roll(wide, (257 - width - base) % 512, 1, stride=1, stride_axis=0)
    return jnp.sum(wide, axis=0, keepdims=True)


def bwd_kernel(pair, in_all, qb, ids, lens, tab_ref, box_cols, box_rows, q_ref, k_ref, v_ref, d0_ref, d1_ref, d2_ref, d3_ref, wo_ref, ctxt_ref, lse_ref, *refs):
    out_ref, dtab_ref, da_ref = refs[:3]
    (b_scr, hot_scr, lut_scr, strip_scr, v_scr, kt_scr, p_scr, ds_scr, dk_scr, dv_scr, near_scr, part_scr, far_acc,
     delta_scr, self_acc) = refs[-15:]
    step = pl.program_id(0)
    block = row_block(step, ids)
    n_keys = k_ref.shape[0]
    blocks = qb // COORD
    heads = range(2)

    @pl.when(step == 0)
    def _():
        build(lens, tab_ref, box_cols, box_rows, k_ref, b_scr, hot_scr, lut_scr, strip_scr, 2, 2 * pair, in_all)
        lane = lax.broadcasted_iota(i32, (n_keys, 128), 1)
        level = COORD - 1 - lax.broadcasted_iota(i32, (COORD, n_keys), 0)
        kb = lax.broadcasted_iota(i32, (16, n_keys), 0)
        kp = lax.broadcasted_iota(i32, (16, n_keys), 1)
        v_scr[:, 0:128] = v_ref[...]
        v_scr[:, 128 : 128 + EXTRA] = jnp.where(lane < 3, -1.0, 0.0).astype(bf16)[:, 0:EXTRA]
        kt_scr[0:128, :] = k_ref[...].T
        for axis in range(2):
            kt_scr[128 + 128 * axis : 256 + 128 * axis, :] = (box_rows[axis : axis + 1, :] == level).astype(bf16)
        kt_scr[384:400, :] = (kp // COORD == kb).astype(bf16)
        dk_scr[...] = jnp.zeros_like(dk_scr)
        dv_scr[...] = jnp.zeros_like(dv_scr)
        near_scr[...] = jnp.zeros_like(near_scr)
        far_acc[...] = jnp.zeros_like(far_acc)
        self_acc[...] = jnp.zeros_like(self_acc)
        ds_scr[0:128, :] = jnp.zeros((128, 2 * qb), bf16)
        ds_scr[128 + n_keys :, :] = jnp.zeros((128, 2 * qb), bf16)

    rows_q = pl.ds(pl.multiple_of(block * qb, qb), qb)
    hot_q = hot_scr[:, rows_q]
    lane_half = lax.broadcasted_iota(i32, (qb, 128), 1) >= HEAD
    for at_step, piece in enumerate((d0_ref, d1_ref, d2_ref, d3_ref)):

        @pl.when(step == at_step)
        def _():
            da_ref[...] = piece[...]

    dot_t = dot_nt(wo_ref[...], da_ref[...]).astype(bf16)
    qt = q_ref[...].T
    prod = dot_t.astype(f32) * ctxt_ref[...]
    operands = []
    for h in heads:
        mine = slice(h * HEAD, h * HEAD + HEAD)
        delta = jnp.sum(prod[mine, :], axis=0, keepdims=True)
        delta_scr[h : h + 1, :] = delta
        log = lse_ref[2 * pair + h : 2 * pair + h + 1, :]
        at = query_side(lens, block, qb, h, qt, hot_q, lut_scr, pieces(log))
        row = lax.broadcasted_iota(i32, (EXTRA, qb), 0)
        extra = jnp.zeros((EXTRA, qb), f32)
        for piece, value in enumerate(pieces(delta)):
            extra = jnp.where(row == piece, value, extra)
        none = jnp.zeros((HEAD, qb), bf16)
        own = dot_t[mine, :]
        dat = jnp.concatenate(([own, none] if h == 0 else [none, own]) + [extra.astype(bf16)], axis=0)
        operands.append((at, dat))
    for h, (at, dat) in enumerate(operands):
        at_q = slice(h * qb, h * qb + qb)
        for key_at in range(0, n_keys, KEYS):
            p = jnp.exp(scores(block, qb, h, at, b_scr, strip_scr, key_at))
            dp = dot(v_scr[key_at : key_at + KEYS, :], dat)
            p_scr[key_at : key_at + KEYS, at_q] = p.astype(bf16)
            ds_scr[128 + key_at : 128 + key_at + KEYS, at_q] = (p * dp).astype(bf16)
    key_block = lax.broadcasted_iota(i32, (8, qb), 0)
    q_block = block * blocks + lax.broadcasted_iota(i32, (8, qb), 1) // COORD
    dq_halves = []
    for h in heads:
        at_q = slice(h * qb, h * qb + qb)
        got = dot(kt_scr[...], ds_scr[128 : 128 + n_keys, at_q])
        dq_halves.append(got[h * HEAD : h * HEAD + HEAD, :])
        part_scr[h, :, rows_q] = got[128:384, :].astype(bf16)
        by_block = got[384:392, :]
        far_acc[h, 0] += jnp.where(key_block + 1 < q_block, by_block, 0.0)
        far_acc[h, 1] += jnp.where(key_block > q_block + 1, by_block, 0.0)
    out_ref[rows_q, 0:128] = jnp.concatenate(dq_halves, axis=0).T.astype(bf16)

    def both(x):
        return jnp.concatenate([jnp.where(lane_half, 0.0, x.astype(f32)), jnp.where(lane_half, x.astype(f32), 0.0)], axis=0).astype(bf16)

    dv_scr[...] += dot(p_scr[...], both(dot_t.T))
    dk_scr[...] += dot(ds_scr[128 : 128 + n_keys, :], both(q_ref[...]))
    for h in heads:
        for t in range(blocks):
            rows = pl.ds(pl.multiple_of((block * blocks + t) * COORD, COORD), NEAR)
            at_q = h * qb + t * 128
            near_scr[h] += ds_scr[rows, at_q : at_q + 128].astype(f32)

    some, which = lone(lens, block, qb)

    @pl.when(some)
    def _():
        kt, vt = k_ref[rows_q, :].T, v_ref[rows_q, :].T
        d_out = dot_nt(wo_ref[...], da_ref[...]).astype(bf16).astype(f32)
        q_t = q_ref[...].T
        add_q, add_k, add_v = [], [], []
        for h in heads:
            mine = slice(h * HEAD, h * HEAD + HEAD)
            log = lse_ref[2 * pair + h : 2 * pair + h + 1, :]
            p = jnp.where(which, jnp.exp(own_score(h, q_t, kt, strip_scr, lut_scr) - log), 0.0)
            dp = jnp.sum(d_out[mine, :] * vt[mine, :].astype(f32), axis=0, keepdims=True) - delta_scr[h : h + 1, :]
            ds = p * dp
            add_q.append(kt[mine, :].astype(f32) * ds)
            add_k.append(q_t[mine, :].astype(f32) * ds)
            add_v.append(d_out[mine, :] * p)
            self_acc[h : h + 1, :] += ds
        out_ref[rows_q, 0:128] = (out_ref[rows_q, 0:128].astype(f32) + jnp.concatenate(add_q, axis=0).T).astype(bf16)
        dk_scr[rows_q, :] += jnp.concatenate(add_k, axis=0).T
        dv_scr[rows_q, :] += jnp.concatenate(add_v, axis=0).T

    @pl.when(step == pl.num_programs(0) - 1)
    def _():
        out_ref[:, 128:256] = dk_scr[...].astype(bf16)
        out_ref[:, 256:384] = dv_scr[...].astype(bf16)
        offset = 256 - lax.broadcasted_iota(i32, (1, 512), 1)
        row, column = (lax.broadcasted_iota(i32, (NEAR, NEAR), at) for at in (0, 1))
        mirror = (row + column == NEAR - 1).astype(bf16)
        sums = [jnp.zeros((1, 512), f32)] * 16
        for h in heads:
            high, rest = pieces(near_scr[h])[0:2]
            near = skew_sums(dot_tn(high.astype(bf16), mirror) + dot_tn(rest.astype(bf16), mirror), -128)
            left = jnp.sum(far_acc[h, 0], keepdims=True)
            right = jnp.sum(far_acc[h, 1], keepdims=True)
            alone = jnp.where(offset == 0, jnp.sum(self_acc[h : h + 1, :], keepdims=True), 0.0)
            far = jnp.where(offset == -255, left, 0.0) + jnp.where(offset == 255, right, 0.0)
            sums[2 * pair + h] = near + far + alone
            for axis in range(2):
                rows = slice(128 * axis, 128 * axis + 128)
                pairs = dot(part_scr[h, rows, :], b_scr[0, :, 128 + 128 * axis : 256 + 128 * axis])
                sums[in_all * (1 + axis) + 2 * pair + h] = skew_sums(pairs.T, 0) + alone
        sums = jnp.concatenate(sums, axis=0)
        dtab_ref[...] = lax.dot_general(offset_hot(-1), sums, (((1,), (1,)), ((), ())), precision=lax.Precision.HIGHEST, preferred_element_type=f32)


def attend_back(pair, ids, q, k, v, d_pieces, w_out, ctxt, lse, tables, lengths, box_cols, box_rows):
    n_keys, width = k.shape
    n_rows = q.shape[0]
    qb = n_rows // 4
    model = w_out.shape[1]
    column = pl.BlockSpec((n_keys, 128), lambda i, ids, lens: (0, pair))
    shapes = [((n_rows, 384), bf16, whole((n_rows, 384))), ((NB, 16), f32, whole((NB, 16)))]
    if pair == 0:
        shapes.append(((n_rows, model), bf16, pl.BlockSpec((qb, model), lambda i, ids, lens: (row_block(i, ids), 0))))
    return pl.pallas_call(
        functools.partial(bwd_kernel, pair, width // HEAD, qb),
        out_shape=[jax.ShapeDtypeStruct(shape, kind) for shape, kind, _ in shapes],
        grid_spec=pltpu.PrefetchScalarGridSpec(
            num_scalar_prefetch=2,
            grid=(4,),
            in_specs=[
                whole(tables.shape), whole(box_cols.shape), whole(box_rows.shape),
                pl.BlockSpec((qb, 128), lambda i, ids, lens: (row_block(i, ids), pair)), column, column,
                *[pl.BlockSpec((qb, model), lambda i, ids, lens, at=at: (at, 0)) for at in (0, 0, 1, 1)],
                pl.BlockSpec((128, model), lambda i, ids, lens: (pair, 0)),
                pl.BlockSpec((128, qb), lambda i, ids, lens: (pair, row_block(i, ids))),
                pl.BlockSpec((8, qb), lambda i, ids, lens: (0, row_block(i, ids))),
            ],
            out_specs=[spec for _, _, spec in shapes],
            scratch_shapes=([] if pair == 0 else [pltpu.VMEM((qb, model), bf16)]) + scratch(n_keys, 2) + [
                pltpu.VMEM((n_keys, 128 + EXTRA), bf16),
                pltpu.VMEM((400, n_keys), bf16),
                pltpu.VMEM((n_keys, 2 * qb), bf16),
                pltpu.VMEM((n_keys + 256, 2 * qb), bf16),
                pltpu.VMEM((n_keys, 128), f32),
                pltpu.VMEM((n_keys, 128), f32),
                pltpu.VMEM((2, NEAR, COORD), f32),
                pltpu.VMEM((2, 256, n_keys), bf16),
                pltpu.VMEM((2, 2, 8, qb), f32),
                pltpu.VMEM((8, qb), f32),
                pltpu.VMEM((8, qb), f32),
            ],
        ),
        compiler_params=params(),
        cost_estimate=estimate(),
        name="attend_back",
    )(ids, lengths, tables, box_cols, box_rows, q, k, v, *d_pieces, w_out, ctxt, lse)


norm_eps = 1e-06
gelu_scale = 0.7978845608028654
gelu_cube = 0.044715


def scale_of(values):
    return lax.rsqrt(jnp.mean(values * values, axis=-1, keepdims=True) + norm_eps)


def anywhere():
    return pl.BlockSpec(memory_space=pl.ANY)


def estimate():
    return pl.CostEstimate(flops=1_000, bytes_accessed=1_000, transcendentals=0)


def qkv_kernel(ids, xa_ref, xb_ref, g_ref, wq_ref, wk_ref, wv_ref, *refs):
    xo_ref, n_ref, q_ref, k_ref, v_ref = refs[-5:]
    for at_step, piece in enumerate((xa_ref, xb_ref)):

        @pl.when(pl.program_id(0) == at_step)
        def _():
            xo_ref[...] = piece[...]

    x = xo_ref[...].astype(f32)
    normed = (x * scale_of(x) * g_ref[...]).astype(bf16)
    n_ref[...] = normed
    q_ref[...] = dot(normed, wq_ref[...]).astype(bf16)
    k_ref[...] = dot(normed, wk_ref[...]).astype(bf16)
    v_ref[...] = dot(normed, wv_ref[...]).astype(bf16)


def project(ids, far, pair, gain, weights, before, n_blocks):
    rows, model = pair[0].shape
    width = weights[0].shape[1]

    def row(i, ids):
        chip = 1 - ids[2] if far else ids[2]
        return (2 * chip + (i + ids[1]) % 2, 0)

    shapes = [jax.ShapeDtypeStruct((n_blocks * rows, n), bf16) for n in (model, model, width, width, width)]
    return pl.pallas_call(
        qkv_kernel,
        out_shape=shapes,
        grid_spec=pltpu.PrefetchScalarGridSpec(
            num_scalar_prefetch=1,
            grid=(2,),
            in_specs=[whole(pair[0].shape)] * 2 + [whole(gain.shape)] + [whole(w.shape) for w in weights] + [anywhere()] * len(before),
            out_specs=[pl.BlockSpec((rows, s.shape[1]), row) for s in shapes],
        ),
        input_output_aliases={7 + i: i for i in range(len(before))},
        compiler_params=params(),
        cost_estimate=estimate(),
        name="project",
    )(ids, *pair, gain, *weights, *before)


def assemble_kernel(ids, *refs):
    for at_step in range(4):

        @pl.when(pl.program_id(0) == at_step)
        def _():
            refs[4][...] = refs[at_step][...]


def assemble(ids, blocks):
    rows, model = blocks[0].shape

    def row(i, ids):
        chip = i // 2
        core = i % 2
        return (2 * ((ids[2] + chip) % 2) + (ids[1] + core) % 2, 0)

    return pl.pallas_call(
        assemble_kernel,
        out_shape=jax.ShapeDtypeStruct((4 * rows, model), bf16),
        grid_spec=pltpu.PrefetchScalarGridSpec(
            num_scalar_prefetch=1,
            grid=(4,),
            in_specs=[whole((rows, model))] * 4,
            out_specs=pl.BlockSpec((rows, model), row),
        ),
        compiler_params=params(),
        cost_estimate=estimate(),
        name="assemble",
    )(ids, *blocks)


def ffn_kernel(ids, a0, a1, a2, a3, b0, b1, b2, b3, x_ref, cot_ref, o0, o1, o2, o3, g_ref, wg_ref, wu_ref, wd_ref,
               mixed_ref, nf_ref, hid_ref, dg_ref, du_ref, dsend, dkeep, rsend, rkeep):
    first = pl.program_id(0) < 2
    mixed = x_ref[...].astype(f32)
    for a, b, o in ((a0, b0, o0), (a1, b1, o1), (a2, b2, o2), (a3, b3, o3)):
        mixed = mixed + dot(jnp.where(first, a[...], b[...]), o[...])
    normed = (mixed * scale_of(mixed) * g_ref[...]).astype(bf16)
    nf_ref[...] = normed
    gate = dot_nt(wg_ref[...], normed)
    up = dot_nt(wu_ref[...], normed)
    d_hidden = dot_nt(wd_ref[...], cot_ref[...])
    square = gate * gate
    t = jnp.tanh(gelu_scale * gate * (1.0 + gelu_cube * square))
    half = 0.5 * (1.0 + t)
    unit = gate * half
    slope = half + 0.5 * gate * (1.0 - t * t) * (gelu_scale * (1.0 + 3.0 * gelu_cube * square))
    hidden = (unit * up).astype(bf16)
    d_gate = (d_hidden * up * slope).astype(bf16)
    d_up = (d_hidden * unit).astype(bf16)
    hid_ref[...] = hidden
    dg_ref[...] = d_gate
    du_ref[...] = d_up
    d_normed = (dot_tn(d_gate, wg_ref[...]) + dot_tn(d_up, wu_ref[...])).astype(bf16)
    down = dot_tn(hidden, wd_ref[...]).astype(bf16)
    half = pl.program_id(0) % 2

    @pl.when(half == 0)
    def _():
        dsend[...] = d_normed
        rsend[...] = down

    @pl.when(half == 1)
    def _():
        dkeep[...] = d_normed
        rkeep[...] = down
        mixed_ref[...] = mixed


def ffn(ids, contexts, x_all, cot_all, w_outs, gain, w_gate_t, w_up_t, w_down):
    total, model = x_all.shape
    rows = total // 4
    width, hidden = contexts[0][0].shape[1], w_down.shape[0]

    def local_row(i, ids):
        return (i + 1 + ids[1]) % 2

    def row(i, ids):
        return i // 2 * 2 + local_row(i, ids)

    def part(chunk):
        return pl.BlockSpec((rows, width), lambda i, ids: (jnp.where(i // 2 == chunk, local_row(i, ids), ids[1] if chunk == 0 else 1 - ids[1]), 0))

    rows_spec = pl.BlockSpec((rows, model), lambda i, ids: (row(i, ids), 0))
    units_spec = pl.BlockSpec((hidden, rows), lambda i, ids: (0, row(i, ids)))
    half_spec = pl.BlockSpec((rows, model), lambda i, ids: (i // 2, 0))
    outs = [((2 * rows, model), f32, half_spec), ((total, model), bf16, rows_spec)]
    outs += [((hidden, total), bf16, units_spec)] * 3
    outs += [((2 * rows, model), bf16, half_spec)] * 4
    ins = [(a, part(chunk)) for chunk in range(2) for a in contexts[chunk]]
    ins += [(x_all, rows_spec), (cot_all, rows_spec)]
    ins += [(w, whole(w.shape)) for w in (*w_outs, gain, w_gate_t, w_up_t, w_down)]
    return call(ffn_kernel, ids, ins, outs, (4,), "ffn")


def norm_back(total, values, gain):
    r = scale_of(values)
    n = values * r
    e = gain * total
    return r * (e - n * jnp.mean(n * e, axis=-1, keepdims=True)), jnp.sum(total * n, axis=0, keepdims=True)


def mid_kernel(ids, a_ref, b_ref, mixed_ref, cot_ref, g_ref, dm_ref, da_ref, sum_ref):
    total = a_ref[...].astype(f32) + b_ref[...].astype(f32)
    grad, gain_sum = norm_back(total, mixed_ref[...], g_ref[...])
    d_mixed = cot_ref[...].astype(f32) + grad
    dm_ref[...] = d_mixed
    da_ref[...] = d_mixed.astype(bf16)
    step = pl.program_id(0)
    gain_sum = jnp.where(ids[2] == step // 2, gain_sum, 0.0)

    @pl.when(step == 0)
    def _():
        sum_ref[...] = gain_sum

    @pl.when(step > 0)
    def _():
        sum_ref[...] += gain_sum


def mid(ids, own, far, mixed, cot_all, gain):
    total, model = own.shape
    rows = total // 4
    spec = pl.BlockSpec((rows, model), lambda i, ids: (i, 0))
    cot_spec = pl.BlockSpec((rows, model), lambda i, ids: (i // 2 * 4 + 2 * ids[1] + i % 2, 0))
    ins = [(own, spec), (far, spec), (mixed, spec), (cot_all, cot_spec), (gain, whole(gain.shape))]
    outs = [((total, model), f32, spec), ((total, model), bf16, spec), ((1, model), f32, whole((1, model)))]
    return call(mid_kernel, ids, ins, outs, (4,), "mid")


def back_kernel(ids, a_ref, b_ref, wa_ref, wb_ref, *outs):
    total = dot_nt(a_ref[...], wa_ref[...]) + dot_nt(b_ref[...], wb_ref[...])
    for at_step, out in enumerate(outs):

        @pl.when(pl.program_id(0) == at_step)
        def _():
            out[...] = total.astype(out.dtype)


def project_back(ids, grads, weights):
    total, width = grads[0].shape
    rows, model = total // 4, weights[0].shape[0]

    def row(i, ids):
        return (2 * ((1 - i // 2 + ids[2]) % 2) + (i + 1 + ids[1]) % 2, 0)

    ins = [(g, pl.BlockSpec((rows, width), row)) for g in grads] + [(w, whole(w.shape)) for w in weights]
    outs = [((rows, model), kind, whole((rows, model))) for kind in (bf16, f32, bf16, f32)]
    return call(back_kernel, ids, ins, outs, (4,), "project_back")


def last_kernel(ids, keep_ref, core_ref, y_ref, x_ref, g_ref, dm_ref, out_ref, sum_ref):
    total = keep_ref[...] + core_ref[...].astype(f32) + y_ref[...].astype(f32)
    grad, gain_sum = norm_back(total, x_ref[...].astype(f32), g_ref[...])
    out_ref[...] = dm_ref[...] + grad
    sum_ref[...] = gain_sum


def last(ids, keep, core, far, x, gain, d_mixed):
    ins = [(a, whole(a.shape)) for a in (keep, core, far, x, gain)]
    ins.append((d_mixed, pl.BlockSpec(keep.shape, lambda i, ids: (ids[2], 0))))
    outs = [(shape, f32, whole(shape)) for shape in (keep.shape, (1, keep.shape[1]))]
    return call(last_kernel, ids, ins, outs, (1,), "last")


def bit_orders(shards):
    bits = list(range(shards.bit_length() - 1))
    return bits, bits[1:] + bits[:1]


def slot_of(flip, order):
    place = 0
    for bit in order[1:]:
        place = 2 * place + (flip >> bit) % 2
    return (flip >> order[0]) % 2, place


def unit_parts_kernel(ids, *refs):
    n = 3
    kept_a, sent_a, kept_b, sent_b = refs[2 * n :]
    step = pl.program_id(0)
    low, high = step % 2, step // 2
    even = ids[3] % 2 == 0
    nears, fars = [], []
    for i in range(n):
        out = dot(refs[i][...], refs[n + i][...]).astype(bf16)
        width, cut = out.shape[1] // 2, out.shape[0] // 2
        first, second = out[:, :width], out[:, width:]
        nears.append(jnp.where(even, first, second))
        fars.append(jnp.where(even, second, first))
        kept_a[2 * low + high, i] = nears[i][:cut]
        sent_a[2 * low + high, i] = fars[i][:cut]

    @pl.when(low == 0)
    def _():
        for i in range(n):
            kept_b[2 * high, i] = nears[i][cut:]
            kept_b[2 * high + 1, i] = fars[i][cut:]

    @pl.when(low == 1)
    def _():
        for i in range(n):
            sent_b[2 * high, i] = nears[i][cut:]
            sent_b[2 * high + 1, i] = fars[i][cut:]


def unit_parts(ids, lefts, rights):
    n = len(lefts)
    total, model = rights[0].shape
    hidden = lefts[0].shape[0]
    shape = (4, n, hidden // 2, model // 8)
    return pl.pallas_call(
        unit_parts_kernel,
        out_shape=[jax.ShapeDtypeStruct(shape, bf16)] * 4,
        grid_spec=pltpu.PrefetchScalarGridSpec(
            num_scalar_prefetch=1,
            grid=(4,),
            in_specs=[whole(a.shape) for a in lefts] + [pl.BlockSpec((total, model // 4), lambda i, ids: (0, i ^ (ids[3] // 2)))] * n,
            out_specs=[whole(shape)] * 4,
        ),
        compiler_params=params(),
        cost_estimate=estimate(),
        name="unit_parts",
    )(ids, *lefts, *rights)


def unit_sums_kernel(n, split, *refs):
    out_ref = refs[-1]
    for i in range(n):
        out = dot(refs[i][...], refs[n + i][...]).astype(bf16)
        width = out.shape[1] // split
        for part in range(split):
            out_ref[part, i] = out[:, part * width : part * width + width]


def unit_sums(lefts, rights, shards):
    n = len(lefts)
    total, model = rights[0].shape
    hidden = lefts[0].shape[0]
    cut = model // shards
    step = 256
    split = step // cut if cut % 128 == 0 else 1
    out = pl.pallas_call(
        functools.partial(unit_sums_kernel, n, split),
        out_shape=jax.ShapeDtypeStruct((model // step * split, n, hidden, step // split), bf16),
        grid=(model // step,),
        in_specs=[whole(a.shape) for a in lefts] + [pl.BlockSpec((total, step), lambda i: (0, i))] * n,
        out_specs=pl.BlockSpec((split, n, hidden, step // split), lambda i: (i, 0, 0, 0)),
        compiler_params=params(),
        cost_estimate=estimate(),
        name="unit_sums",
    )(*lefts, *rights)
    if split == 1:
        out = out.reshape(model // step, n, hidden, step // cut, cut)
        out = out.transpose(0, 3, 1, 2, 4).reshape(shards, n, hidden, cut)
    return out


def head_sums_kernel(shards, ids, normed_ref, da_ref, g0_ref, g1_ref, ctx_ref, ka_ref, sa_ref, kb_ref, sb_ref, acc, turned):
    outs = ((ka_ref, sa_ref), (kb_ref, sb_ref))
    cut = acc.shape[0] // shards
    turned[...] = normed_ref[...].T
    acc[:, 0:384] = dot(turned[...], g0_ref[...])
    acc[:, 384:768] = dot(turned[...], g1_ref[...])
    turned[...] = da_ref[...].T
    acc[:, 768:] = dot(turned[...], ctx_ref[...])
    for group, order in enumerate(bit_orders(shards)):
        for flip in range(shards):
            sent, place = slot_of(flip, order)
            at = (ids[3] ^ flip) * cut + group * (cut // 2)
            rows = pl.ds(pl.multiple_of(at, cut // 2), cut // 2)
            outs[group][sent][place] = acc[rows, :].astype(bf16)


def head_sums(ids, normed, d_attn, grads, context, shards):
    total, model = normed.shape
    columns = 2 * grads[0].shape[1] + context.shape[1]
    shape = (shards // 2, model // shards // 2, columns)
    ins = [(a, whole(a.shape)) for a in (normed, d_attn, *grads, context)]
    return pl.pallas_call(
        functools.partial(head_sums_kernel, shards),
        out_shape=[jax.ShapeDtypeStruct(shape, bf16)] * 4,
        grid_spec=pltpu.PrefetchScalarGridSpec(
            num_scalar_prefetch=1,
            grid=(1,),
            in_specs=[spec for _, spec in ins],
            out_specs=[whole(shape)] * 4,
            scratch_shapes=[pltpu.VMEM((model, columns), f32), pltpu.VMEM((model, total), bf16)],
        ),
        compiler_params=params(),
        cost_estimate=estimate(),
        name="head_sums",
    )(ids, *(a for a, _ in ins))


def swap(sent, bit, n_dp):
    return lax.ppermute(sent, "dp", [(i, i ^ (1 << bit)) for i in range(n_dp)])


def call(kernel, ids, ins, outs, grid, name):
    return pl.pallas_call(
        kernel,
        out_shape=[jax.ShapeDtypeStruct(shape, kind) for shape, kind, _ in outs],
        grid_spec=pltpu.PrefetchScalarGridSpec(
            num_scalar_prefetch=1,
            grid=grid,
            in_specs=[spec for _, spec in ins],
            out_specs=[spec for _, _, spec in outs],
        ),
        compiler_params=params(),
        cost_estimate=estimate(),
        name=name,
    )(ids, *(array for array, _ in ins))


def out_kernel(ids, ka_ref, ca_ref, kb_ref, cb_ref, send_ref, own_ref):
    sum_a = ka_ref[...].astype(f32) + ca_ref[...].astype(f32)
    sum_b = kb_ref[...].astype(f32) + cb_ref[...].astype(f32)
    first = ids[2] == 0
    send_ref[...] = jnp.where(first, sum_b, sum_a).astype(bf16)
    own_ref[...] = jnp.where(first, sum_a, sum_b)


def out_sums(ids, keep, core):
    rows, model = keep.shape[0] // 2, keep.shape[1]
    low = pl.BlockSpec((rows // 2, model), lambda i, ids: (i, 0))
    high = pl.BlockSpec((rows // 2, model), lambda i, ids: (2 + i, 0))
    ins = [(keep, low), (core, low), (keep, high), (core, high)]
    return call(out_kernel, ids, ins, [((rows, model), bf16, low), ((rows, model), f32, low)], (2,), "out_sums")


def result_kernel(ids, mixed_ref, own_ref, far_ref, out_ref):
    out_ref[...] = mixed_ref[...] + own_ref[...] + far_ref[...].astype(f32)


def result_of(ids, mixed, own, far):
    rows, model = own.shape
    spec = pl.BlockSpec((rows // 2, model), lambda i, ids: (i, 0))
    ins = [(mixed, pl.BlockSpec((rows // 2, model), lambda i, ids: (2 * ids[2] + i, 0))), (own, spec), (far, spec)]
    return call(result_kernel, ids, ins, [(own.shape, f32, spec)], (2,), "result_of")[0]


def onward_kernel(n, ids, *refs):
    for i in range(n):
        low, high, came_low, came_high = refs[4 * i : 4 * i + 4]
        keep, send = refs[4 * n + 2 * i : 4 * n + 2 * i + 2]
        keep[...] = (low[...].astype(f32) + came_low[...].astype(f32)).astype(bf16)
        send[...] = (high[...].astype(f32) + came_high[...].astype(f32)).astype(bf16)


def onward(ids, kept, came):
    ins, outs = [], []
    half = kept[0].shape[0] // 2
    for k, c in zip(kept, came, strict=True):
        block = (1,) + k.shape[1:]
        rest = (0,) * (k.ndim - 1)
        low = pl.BlockSpec(block, lambda i, ids, rest=rest: (i,) + rest)
        high = pl.BlockSpec(block, lambda i, ids, rest=rest: (half + i,) + rest)
        ins += [(k, low), (k, high), (c, low), (c, high)]
        outs += [((half,) + k.shape[1:], bf16, low)] * 2
    got = call(functools.partial(onward_kernel, len(kept)), ids, ins, outs, (half,), "onward")
    return got[0::2], got[1::2]


def unit_last_kernel(ids, ka, ca, kb, cb, *outs):
    cut = ka.shape[2]
    for i, out in enumerate(outs):
        out[0:cut, :] = ka[0, i].astype(f32) + ca[0, i].astype(f32)
        out[cut:, :] = kb[0, i].astype(f32) + cb[0, i].astype(f32)


def unit_last(ids, kept, came):
    _, n, cut, columns = kept[0].shape
    ins = [(a, whole(a.shape)) for a in (kept[0], came[0], kept[1], came[1])]
    outs = [((2 * cut, columns), f32, whole((2 * cut, columns)))] * n
    return call(unit_last_kernel, ids, ins, outs, (1,), "unit_last")


def head_last_kernel(ids, ka, ca, kb, cb, *outs):
    rows = ka.shape[1]
    both = jnp.concatenate([k[0].astype(f32) + c[0].astype(f32) for k, c in ((ka, ca), (kb, cb))], axis=0)
    for i, out in enumerate(outs[:3]):
        out[:, 0:128] = both[:, 128 * i : 128 * i + 128]
        out[:, 128:256] = both[:, 384 + 128 * i : 512 + 128 * i]
    outs[3][...] = both[:, 768:].T


def head_last(ids, kept, came):
    _, rows, columns = kept[0].shape
    ins = [(a, whole(a.shape)) for a in (kept[0], came[0], kept[1], came[1])]
    outs = [((2 * rows, 256), f32, whole((2 * rows, 256)))] * 3 + [((256, 2 * rows), f32, whole((256, 2 * rows)))]
    return call(head_last_kernel, ids, ins, outs, (1,), "head_last")


def local(
    tokens, w_query, w_key, w_value, w_attn_out, w_gate, w_up, w_down, norm_attn, norm_ffn,
    rel_table, x_table, y_table, lengths, boxes, cotangent,
):
    n_mp, n_dp = lax.axis_size("mp"), lax.axis_size("dp")
    me = lax.axis_index("mp")
    core, chip = me % 2, me // 2
    ids = jnp.stack([me, core, chip, lax.axis_index("dp")]).astype(i32)
    rows, model = tokens.shape

    def by_core(a):
        return lax.ppermute(a, "mp", [(i, i ^ 1) for i in range(n_mp)])

    def by_chip(a):
        return lax.ppermute(a, "mp", [(i, i ^ 2) for i in range(n_mp)])

    def together(*arrays):
        return lax.optimization_barrier(arrays)

    def after(a, *earlier):
        return lax.optimization_barrier((a, *earlier))[0]

    def exchange_small(a):
        return lax.all_to_all(a, ("dp", "mp"), split_axis=0, concat_axis=0, tiled=True)

    n_heads = w_query.shape[1] // HEAD
    tables = jnp.concatenate([rel_table.T, x_table.T, y_table.T, jnp.zeros((16 - 3 * n_heads, NB), f32)], axis=0)
    box_cols = boxes.T
    gain_attn, gain_ffn = norm_attn.reshape(1, model), norm_ffn.reshape(1, model)
    weights = (w_query, w_key, w_value)
    w_gate_t, w_up_t = w_gate.T, w_up.T

    x_chip = by_chip(tokens)
    group = project(ids, False, (tokens, by_core(tokens)), gain_attn, weights, [], n_mp)
    w_pairs = [jnp.concatenate([w[:, at : at + 128] for w in weights], axis=1) for at in (0, 128)]
    x_chip, _, box_cols, tables, *w_pairs = together(x_chip, group[0], box_cols, tables, *w_pairs)
    x_both = by_core(x_chip)
    w_chip = by_chip(after(w_attn_out, x_chip))
    c_chip = by_chip(after(cotangent, x_chip))
    group = project(ids, True, (x_chip, x_both), gain_attn, weights, group, n_mp)
    x_all, normed, queries, keys_all, values_all = group

    *kept, own_a = attend(0, queries, keys_all, values_all, tables, lengths, box_cols, boxes, [])
    core_a, far_a = by_core(own_a), by_chip(own_a)
    *kept, own_b = attend(1, after(queries, own_a), keys_all, values_all, tables, lengths, box_cols, boxes, kept)
    context, ctxt, lse = kept
    own_b, core_a, far_a, w_chip, c_chip = together(own_b, core_a, far_a, w_chip, c_chip)
    core_b, far_b = by_core(own_b), by_chip(own_b)
    w_outs = (w_attn_out, by_core(w_attn_out), w_chip, by_core(w_chip))
    cot_all = assemble(ids, (cotangent, by_core(cotangent), c_chip, by_core(c_chip)))
    both_a = by_core(far_a)
    cot_all, far_b = together(cot_all, far_b)
    contexts = ((own_a, core_a, far_a, both_a), (own_b, core_b, far_b, by_core(far_b)))

    out = ffn(ids, contexts, x_all, cot_all, w_outs, gain_ffn, w_gate_t, w_up_t, w_down)
    mixed, normed_ffn, hidden, d_gate, d_up, d_send, d_keep, r_send, r_keep = out
    d_core = by_core(d_send)
    sums = (d_keep.astype(f32) + d_core.astype(f32)).astype(bf16)
    far_sums = by_chip(sums)
    r_core = by_core(after(r_send, sums))

    orders = bit_orders(n_dp)
    pairwise = n_dp == 8 and model == 1024
    unit_args = ((d_gate, d_up, hidden), (normed_ffn, normed_ffn, after(cot_all, sums)))
    if pairwise:
        unit = list(unit_parts(ids, *unit_args))
        unit[0], unit[2], far_sums, r_core = together(unit[0], unit[2], far_sums, r_core)
        unit_came = [swap(unit[2 * i + 1], order[0], n_dp) for i, order in enumerate(orders)]
    else:
        unit = [unit_sums(*unit_args, n_dp)]
        *unit, far_sums, r_core = together(*unit, far_sums, r_core)
        ffn_sums = lax.psum_scatter(unit[0], "dp", scatter_dimension=0, tiled=True)[0].astype(f32)
    d_mixed, d_own, gain_mid = mid(ids, sums, far_sums, mixed, cot_all, gain_ffn)
    d_core = by_core(d_own)

    d_pieces = (d_own, d_core, d_own, d_core)
    back_args = (d_pieces, w_attn_out, ctxt, lse, tables, lengths, box_cols, boxes)
    heads_0, tab_0, d_attn = attend_back(0, ids, queries, keys_all, values_all, *back_args)

    def swaps(sends, step):
        return [swap(send, order[step], n_dp) for send, order in zip(sends, orders, strict=True)]

    queries_1 = after(queries, heads_0)
    if pairwise:
        unit_came = together(*unit_came, heads_0)[:2]
        unit_kept, sends = onward(ids, unit[0::2], unit_came)
        unit_came = swaps(sends, 1)
        queries_1 = after(queries_1, *sends)
    heads_1, tab_1 = attend_back(1, ids, queries_1, keys_all, values_all, *back_args)

    f_send, f_keep, n_send, n_keep = project_back(ids, (heads_0, heads_1), w_pairs)
    f_core, n_core = by_core(f_send), by_core(n_send)
    if pairwise:
        attn = head_sums(ids, normed, d_attn, (heads_0, after(heads_1, f_keep)), context, n_dp)
        f_core, n_core, *attn = together(f_core, n_core, *attn)
        unit_came = together(*unit_came, attn[0])[:2]
        unit_kept, sends = onward(ids, unit_kept, unit_came)
        unit_came = swaps(sends, 2)
        f_core = after(f_core, *sends)
        came = swaps(attn[1::2], 0)
    f_sum = (f_keep + f_core.astype(f32)).astype(bf16)
    far = by_chip(f_sum)
    if pairwise:
        r_out, r_own = out_sums(ids, r_keep, after(r_core, f_sum))
        came[0], came[1], far, r_out = together(*came, far, r_out)
        r_far = by_chip(r_out)
        kept, sends = onward(ids, attn[0::2], came)
        came = swaps(sends, 1)
        far = after(far, *sends)
    else:
        r_out, r_own = out_sums(ids, r_keep, r_core)
        result = result_of(ids, mixed, r_own, by_chip(r_out))
    d_tokens, gain_first = last(ids, n_keep, n_core, far, tokens, gain_attn, d_mixed)

    gains = jnp.concatenate([gain_first, gain_mid], axis=0).reshape(2, n_dp, n_mp, -1).transpose(1, 2, 0, 3)
    n_gain = gains.shape[3]
    d_tab = tab_0 + tab_1
    tabs = d_tab[:, : 3 * n_heads].reshape(n_dp, 1, -1)
    tabs = jnp.where(lax.broadcasted_iota(i32, (1, n_mp, 1), 1) == me, tabs, 0.0)
    small = jnp.concatenate([gains.reshape(n_dp, n_mp, 2 * n_gain), tabs], axis=2).reshape(n_dp * n_mp, -1)
    if pairwise:
        unit_came[0], unit_came[1], small = together(*unit_came, small)
        small = exchange_small(small)
        ffn_sums = unit_last(ids, unit_kept, unit_came)
        came[0], came[1], *ffn_sums = together(*came, *ffn_sums)
        kept, sends = onward(ids, kept, came)
        came = swaps(sends, 2)
        small = after(small, *sends).sum(axis=0)
        result = result_of(ids, mixed, r_own, after(r_far, *sends))
        came[0], came[1], result = together(*came, result)
        attn_sums = head_last(ids, kept, came)
    else:
        grads = [heads[:, 128 * i : 128 * i + 128] for i in range(3) for heads in (heads_0, heads_1)]
        wide = [dot_tn(normed, grad) for grad in grads]
        wide = [jnp.concatenate(wide[2 * i : 2 * i + 2], axis=1) for i in range(3)] + [dot_tn(d_attn, context)]
        wide = jnp.concatenate(wide, axis=1).astype(bf16)
        wide = lax.psum_scatter(wide, "dp", scatter_dimension=0, tiled=True).astype(f32)
        attn_sums = [wide[:, 256 * i : 256 * i + 256] for i in range(4)]
        attn_sums[3] = attn_sums[3].T
        small = exchange_small(small).sum(axis=0)
    tabs = small[2 * n_gain :].reshape(-1, 3, n_heads)
    return (
        result, d_tokens,
        *attn_sums,
        ffn_sums[0].T, ffn_sums[1].T, ffn_sums[2],
        small[:n_gain], small[n_gain : 2 * n_gain], tabs[:, 0], tabs[:, 1], tabs[:, 2],
    )


def solution(mesh):
    in_specs = (
        P(("dp", "mp"), None),
        P(None, "mp"),
        P(None, "mp"),
        P(None, "mp"),
        P("mp", None),
        P(None, "mp"),
        P(None, "mp"),
        P("mp", None),
        P(),
        P(),
        P(None, "mp"),
        P(None, "mp"),
        P(None, "mp"),
        P("dp", None),
        P(None, "dp"),
        P(("dp", "mp"), None),
    )
    out_specs = (
        P(("dp", "mp"), None),
        P(("dp", "mp"), None),
        P("dp", "mp"),
        P("dp", "mp"),
        P("dp", "mp"),
        P("mp", "dp"),
        P("dp", "mp"),
        P("dp", "mp"),
        P("mp", "dp"),
        P(("dp", "mp")),
        P(("dp", "mp")),
        P("dp", "mp"),
        P("dp", "mp"),
        P("dp", "mp"),
    )
    return jax.shard_map(local, mesh=mesh, in_specs=in_specs, out_specs=out_specs, check_vma=False)
```

```python
import functools

import jax
import jax.numpy as jnp
from jax import lax
from jax.experimental import pallas as pl
from jax.experimental.pallas import tpu as pltpu
from jax.sharding import PartitionSpec as P

f32, bf16, i32 = jnp.float32, jnp.bfloat16, jnp.int32
HEAD = 64
NB = 32
COORD = 128
SHORT = 512
NEAR = 3 * COORD
EXTRA = 16
KEYS = 512
thresholds = (1, 2, 3, 4, 5, 6, 7, 8, 12, 16, 23, 32, 46, 64, 91)
masked_score = -1000000000.0


def dot(a, b):
    return jnp.dot(a, b, preferred_element_type=f32)


def dot_nt(a, b):
    return lax.dot_general(a, b, (((1,), (1,)), ((), ())), preferred_element_type=f32)


def dot_tn(a, b):
    return lax.dot_general(a, b, (((0,), (0,)), ((), ())), preferred_element_type=f32)


def bucket_of(offsets):
    distance = jnp.abs(offsets)
    bucket_ids = jnp.where(offsets > 0, NB // 2, 0)
    for threshold in thresholds:
        bucket_ids = bucket_ids + jnp.where(distance >= threshold, 1, 0)
    return bucket_ids


def offset_hot(sign=1):
    offsets = sign * (lax.broadcasted_iota(i32, (NB, 512), 1) - 256)
    return (bucket_of(offsets) == lax.broadcasted_iota(i32, (NB, 512), 0)).astype(f32)


def toeplitz(row, base):
    wide = jnp.broadcast_to(row, (COORD, 512))
    return pltpu.roll(wide, (256 - base) % 512, 1, stride=1, stride_axis=0)


def start_of(len0, len1):
    return jnp.where(len1 > 0, 1, 0), jnp.where(len1 > 0, len1, len0)


def build(lens, tab_ref, box_cols, box_rows, k_ref, b_scr, hot_scr, lut_scr, strip_scr, n_heads):
    n_keys = k_ref.shape[0]
    len0, len1 = lens[0, 0], lens[0, 1]
    start1, start1_len = start_of(len0, len1)
    lane = lax.broadcasted_iota(i32, (n_keys, COORD), 1)
    pos = lax.broadcasted_iota(i32, (n_keys, COORD), 0)
    x_hot = (box_cols[:, 0:1] == lane).astype(bf16)
    y_hot = (box_cols[:, 1:2] == lane).astype(bf16)
    second = pos >= SHORT
    start_k = jnp.where(second, start1, 0)
    limit = jnp.where(second, start1_len, len0)
    valid = pos - start_k * SHORT < limit
    masked0 = jnp.where(valid & (start_k == 0), 0.0, masked_score)
    masked1 = jnp.where(valid & (start_k == start1), 0.0, masked_score)
    extra = jnp.where(lane == 0, masked0, jnp.where(lane == 1, masked1, 0.0))
    extra = extra.astype(bf16)[:, 0:EXTRA]
    for pair in range(n_heads // 2):
        b_scr[pair, :, 0:128] = k_ref[:, pair * 128 : pair * 128 + 128]
        b_scr[pair, :, 128:256] = x_hot
        b_scr[pair, :, 256:384] = y_hot
        b_scr[pair, :, 384 : 384 + EXTRA] = extra
    level = lax.broadcasted_iota(i32, (COORD, n_keys), 0)
    hot_scr[0:128, :] = (box_rows[0:1, :] == level).astype(bf16)
    hot_scr[128:256, :] = (box_rows[1:2, :] == level).astype(bf16)
    vec = jnp.dot(tab_ref[...], offset_hot(), precision=lax.Precision.HIGHEST, preferred_element_type=f32)
    n_strip = strip_scr.shape[1]
    for h in range(n_heads):
        for axis in range(2):
            at = n_heads * (1 + axis) + h
            table = toeplitz(vec[at : at + 1, :], 0)[:, 0:128]
            lut_scr[h, axis] = table.T.astype(bf16)
        row = vec[h : h + 1, :]
        near = toeplitz(row, -128)[:, 0:NEAR]
        mid = (n_strip - NEAR) // 2
        left = jnp.broadcast_to(row[:, 0:1], (mid, COORD))
        right = jnp.broadcast_to(row[:, 511:512], (mid, COORD))
        strip_scr[h, 0:mid, :] = left
        strip_scr[h, mid : mid + NEAR, :] = near.T
        strip_scr[h, mid + NEAR :, :] = right


def query_side(lens, block, qb, h, qt, hot_q, lut_scr):
    half = jnp.zeros((HEAD, qb), bf16)
    own = qt[(h % 2) * HEAD : (h % 2) * HEAD + HEAD, :]
    parts = [own, half] if h % 2 == 0 else [half, own]
    x_rows = dot(lut_scr[h, 0], hot_q[0:128, :]).astype(bf16)
    y_rows = dot(lut_scr[h, 1], hot_q[128:256, :]).astype(bf16)
    row = lax.broadcasted_iota(i32, (EXTRA, qb), 0)
    q_pos = block * qb + lax.broadcasted_iota(i32, (EXTRA, qb), 1)
    extra = jnp.where(row == jnp.where(q_pos >= SHORT, 1, 0), 1.0, 0.0)
    return jnp.concatenate(parts + [x_rows, y_rows, extra.astype(bf16)], axis=0)


def pieces(value):
    high = value.astype(bf16).astype(f32)
    rest = value - high
    mid = rest.astype(bf16).astype(f32)
    return high, mid, (rest - mid).astype(bf16).astype(f32)


def scores(block, qb, h, at, b_scr, strip_scr, key_at):
    s = dot(b_scr[h // 2, key_at : key_at + KEYS, :], at)
    blocks = qb // COORD
    top = b_scr.shape[1] // COORD - 1
    parts = []
    for t in range(blocks):
        off = pl.multiple_of((top - (block * blocks + t)) * COORD + key_at, COORD)
        parts.append(s[:, t * 128 : t * 128 + 128] + strip_scr[h, pl.ds(off, KEYS), :])
    return jnp.concatenate(parts, axis=1)


def lone(lens, block, qb):
    len0, len1 = lens[0, 0], lens[0, 1]
    start1, start1_len = start_of(len0, len1)
    in_second = block * qb >= SHORT
    begin = jnp.where(in_second, start1, 0) * SHORT
    limit = jnp.where(in_second, start1_len, len0)
    pos = block * qb + lax.broadcasted_iota(i32, (1, qb), 1) - begin
    return block * qb + qb - 1 - begin >= limit, pos >= limit


def own_score(h, qt, kt, strip_scr, lut_scr):
    mine = slice((h % 2) * HEAD, (h % 2) * HEAD + HEAD)
    product = qt[mine, :].astype(f32) * kt[mine, :].astype(f32)
    centre = (strip_scr.shape[1] - COORD) // 2
    bias = strip_scr[h, centre : centre + 1, 0:1] + lut_scr[h, 0, 0:1, 0:1].astype(f32) + lut_scr[h, 1, 0:1, 0:1].astype(f32)
    return jnp.sum(product, axis=0, keepdims=True) + bias


def fwd_kernel(n_heads, qb, base, lens, tab_ref, box_cols, box_rows, q_ref, k_ref, v_ref, *refs):
    ctx_ref, ctxt_ref, rows_ref, p_ref, out_ref, b_scr, hot_scr, lut_scr, strip_scr, vt_scr, s_scr, top_scr, log_scr = refs[-13:]
    n_keys = k_ref.shape[0]
    block = pl.program_id(0) + base

    @pl.when(pl.program_id(0) == 0)
    def _():
        build(lens, tab_ref, box_cols, box_rows, k_ref, b_scr, hot_scr, lut_scr, strip_scr, n_heads)
        for pair in range(n_heads // 2):
            vt_scr[pair, 0:128, :] = v_ref[:, pair * 128 : pair * 128 + 128].T
            vt_scr[pair, 128:144, :] = jnp.ones((16, n_keys), bf16)

    hot_q = hot_scr[:, pl.ds(pl.multiple_of(block * qb, qb), qb)]
    for pair in range(n_heads // 2):
        qt = q_ref[:, pair * 128 : pair * 128 + 128].T
        halves = []
        for h in (2 * pair, 2 * pair + 1):
            at = query_side(lens, block, qb, h, qt, hot_q, lut_scr)
            top = None
            for key_at in range(0, n_keys, KEYS):
                s = scores(block, qb, h, at, b_scr, strip_scr, key_at)
                s_scr[h % 2, key_at : key_at + KEYS, :] = s
                high = jnp.max(s, axis=0, keepdims=True)
                top = high if top is None else jnp.maximum(top, high)
            out = None
            for key_at in range(0, n_keys, KEYS):
                p = jnp.exp(s_scr[h % 2, key_at : key_at + KEYS, :] - top).astype(bf16)
                p_ref[h, key_at : key_at + KEYS, :] = p
                part = dot(vt_scr[pair, :, key_at : key_at + KEYS], p)
                out = part if out is None else out + part
            total = out[128:129, :]
            factor = 1.0 / total
            halves.append(out[(h % 2) * HEAD : (h % 2) * HEAD + HEAD, :] * factor)
            rows_ref[h : h + 1, :] = factor
            rows_ref[n_heads + h : n_heads + h + 1, :] = jnp.zeros((1, qb), f32)
            top_scr[h : h + 1, :] = top
            log_scr[h : h + 1, :] = top + jnp.log(total)
        ctxt = jnp.concatenate(halves, axis=0)
        ctxt_ref[pair * 128 : pair * 128 + 128, :] = ctxt
        ctx_ref[:, pair * 128 : pair * 128 + 128] = ctxt.T.astype(bf16)
    some, which = lone(lens, block, qb)

    @pl.when(some)
    def _():
        rows_q = pl.ds(pl.multiple_of(block * qb, qb), qb)
        for pair in range(n_heads // 2):
            cols = slice(pair * 128, pair * 128 + 128)
            qt, kt = q_ref[:, cols].T, k_ref[rows_q, cols].T
            for h in (2 * pair, 2 * pair + 1):
                own = own_score(h, qt, kt, strip_scr, lut_scr)
                log = log_scr[h : h + 1, :]
                high = jnp.maximum(own, log)
                new = high + jnp.log(jnp.exp(own - high) + jnp.exp(log - high))
                mine = slice(h * HEAD, h * HEAD + HEAD)
                value = vt_scr[pair, (h % 2) * HEAD : (h % 2) * HEAD + HEAD, rows_q].astype(f32)
                old = ctxt_ref[mine, :]
                alone = jnp.exp(own - new)
                ctxt_ref[mine, :] = jnp.where(which, old * jnp.exp(log - new) + value * alone, old)
                factor = rows_ref[h : h + 1, :]
                rows_ref[h : h + 1, :] = jnp.where(which, jnp.exp(top_scr[h : h + 1, :] - new), factor)
                rows_ref[n_heads + h : n_heads + h + 1, :] = jnp.where(which, alone, 0.0)
            ctx_ref[:, cols] = ctxt_ref[cols, :].T.astype(bf16)

    out_ref[...] = ctx_ref[...]


def scratch(n_keys, n_heads):
    return [
        pltpu.VMEM((n_heads // 2, n_keys, 384 + EXTRA), bf16),
        pltpu.VMEM((256, n_keys), bf16),
        pltpu.VMEM((n_heads, 2, COORD, COORD), bf16),
        pltpu.VMEM((n_heads, 2 * n_keys - COORD, COORD), f32),
    ]


def whole(shape):
    return pl.BlockSpec(shape, lambda *at: (0,) * len(shape))


def params():
    return pltpu.CompilerParams(dimension_semantics=("arbitrary",), vmem_limit_bytes=62 << 20)


def row_block(step, ids):
    return step // 2 * 2 + (step + ids[1]) % 2


def attend(chunk, q, k, v, tables, lengths, box_cols, box_rows, before):
    n_keys, width = k.shape
    qb = n_keys // 4
    n_heads = width // HEAD
    return pl.pallas_call(
        functools.partial(fwd_kernel, n_heads, qb, 2 * chunk),
        out_shape=(
            jax.ShapeDtypeStruct((n_keys, width), bf16),
            jax.ShapeDtypeStruct((width, n_keys), f32),
            jax.ShapeDtypeStruct((8, n_keys), f32),
            jax.ShapeDtypeStruct((n_heads, n_keys, n_keys), bf16),
            jax.ShapeDtypeStruct((2 * qb, width), bf16),
        ),
        grid=(2,),
        in_specs=[
            pl.BlockSpec(memory_space=pltpu.SMEM),
            whole(tables.shape), whole(box_cols.shape), whole(box_rows.shape),
            pl.BlockSpec((qb, width), lambda i: (i + 2 * chunk, 0)), whole(k.shape), whole(v.shape),
        ] + [anywhere()] * len(before),
        out_specs=(
            pl.BlockSpec((qb, width), lambda i: (i + 2 * chunk, 0)),
            pl.BlockSpec((width, qb), lambda i: (0, i + 2 * chunk)),
            pl.BlockSpec((8, qb), lambda i: (0, i + 2 * chunk)),
            pl.BlockSpec((n_heads, n_keys, qb), lambda i: (0, 0, i + 2 * chunk)),
            pl.BlockSpec((qb, width), lambda i: (i, 0)),
        ),
        scratch_shapes=scratch(n_keys, n_heads) + [
            pltpu.VMEM((n_heads // 2, 144, n_keys), bf16),
            pltpu.VMEM((2, n_keys, qb), f32),
            pltpu.VMEM((8, qb), f32),
            pltpu.VMEM((8, qb), f32),
        ],
        input_output_aliases={7 + i: i for i in range(len(before))},
        compiler_params=params(),
        cost_estimate=estimate(),
        name="attend",
    )(lengths, tables, box_cols, box_rows, q, k, v, *before)


def skew_sums(tile, base):
    width = tile.shape[1]
    wide = jnp.concatenate([tile, jnp.zeros((128, 512 - width), f32)], axis=1)
    wide = pltpu.roll(wide, (257 - width - base) % 512, 1, stride=1, stride_axis=0)
    return jnp.sum(wide, axis=0, keepdims=True)


def bwd_kernel(n_heads, qb, ids, lens, box_cols, box_rows, q_ref, k_ref, v_ref, d0_ref, d1_ref, d2_ref, d3_ref, wo_ref, ctxt_ref, rows_ref, p_ref,
               out_ref, dtab_ref, da_ref, v_scr, kt_scr, ds_scr, dk_scr, dv_scr, near_scr, part_scr, far_acc, self_acc):
    step = pl.program_id(0)
    block = row_block(step, ids)
    n_keys = k_ref.shape[0]
    blocks = qb // COORD

    @pl.when(step == 0)
    def _():
        lane = lax.broadcasted_iota(i32, (n_keys, 128), 1)
        level = COORD - 1 - lax.broadcasted_iota(i32, (COORD, n_keys), 0)
        kb = lax.broadcasted_iota(i32, (16, n_keys), 0)
        kp = lax.broadcasted_iota(i32, (16, n_keys), 1)
        for pair in range(n_heads // 2):
            cols = slice(pair * 128, pair * 128 + 128)
            v_scr[pair, :, 0:128] = v_ref[:, cols]
            v_scr[pair, :, 128 : 128 + EXTRA] = jnp.where(lane < 3, -1.0, 0.0).astype(bf16)[:, 0:EXTRA]
            kt_scr[pair, 0:128, :] = k_ref[:, cols].T
            for axis in range(2):
                kt_scr[pair, 128 + 128 * axis : 256 + 128 * axis, :] = (box_rows[axis : axis + 1, :] == level).astype(bf16)
            kt_scr[pair, 384:400, :] = (kp // COORD == kb).astype(bf16)
        dk_scr[...] = jnp.zeros_like(dk_scr)
        dv_scr[...] = jnp.zeros_like(dv_scr)
        near_scr[...] = jnp.zeros_like(near_scr)
        far_acc[...] = jnp.zeros_like(far_acc)
        self_acc[...] = jnp.zeros_like(self_acc)
        for h in range(n_heads):
            ds_scr[h, 0:128, :] = jnp.zeros((128, qb), bf16)
            ds_scr[h, 128 + n_keys :, :] = jnp.zeros((128, qb), bf16)

    rows_q = pl.ds(pl.multiple_of(block * qb, qb), qb)
    lane_half = lax.broadcasted_iota(i32, (qb, 128), 1) >= HEAD
    for at_step, piece in enumerate((d0_ref, d1_ref, d2_ref, d3_ref)):

        @pl.when(step == at_step)
        def _():
            da_ref[...] = piece[...]

    d_ctx = dot_nt(wo_ref[...], da_ref[...])
    prod = d_ctx * ctxt_ref[...]
    scaled = []
    operands = []
    for h in range(n_heads):
        mine = slice(h * HEAD, h * HEAD + HEAD)
        factor = rows_ref[h : h + 1, :]
        delta = jnp.sum(prod[mine, :], axis=0, keepdims=True) * factor
        row = lax.broadcasted_iota(i32, (EXTRA, qb), 0)
        extra = jnp.zeros((EXTRA, qb), f32)
        for piece, value in enumerate(pieces(delta)):
            extra = jnp.where(row == piece, value, extra)
        none = jnp.zeros((HEAD, qb), bf16)
        own = (d_ctx[mine, :] * factor).astype(bf16)
        scaled.append(own)
        operands.append(jnp.concatenate(([own, none] if h % 2 == 0 else [none, own]) + [extra.astype(bf16)], axis=0))
    for h, dat in enumerate(operands):
        for key_at in range(0, n_keys, KEYS):
            dp = dot(v_scr[h // 2, key_at : key_at + KEYS, :], dat)
            p = p_ref[h, key_at : key_at + KEYS, :].astype(f32)
            ds_scr[h, 128 + key_at : 128 + key_at + KEYS, :] = (p * dp).astype(bf16)
    key_block = lax.broadcasted_iota(i32, (8, qb), 0)
    q_block = block * blocks + lax.broadcasted_iota(i32, (8, qb), 1) // COORD

    def of_head(x, h):
        return jnp.where(lane_half, x if h else 0.0, 0.0 if h else x).astype(bf16)

    for pair in range(n_heads // 2):
        dq_halves = []
        for h in (2 * pair, 2 * pair + 1):
            got = dot(kt_scr[pair], ds_scr[h, 128 : 128 + n_keys, :])
            dq_halves.append(got[h % 2 * HEAD : h % 2 * HEAD + HEAD, :])
            part_scr[h, :, rows_q] = got[128:384, :].astype(bf16)
            by_block = got[384:392, :]
            far_acc[h, 0] += jnp.where(key_block + 1 < q_block, by_block, 0.0)
            far_acc[h, 1] += jnp.where(key_block > q_block + 1, by_block, 0.0)
        out_ref[rows_q, 384 * pair : 384 * pair + 128] = jnp.concatenate(dq_halves, axis=0).T.astype(bf16)
        do = jnp.concatenate(scaled[2 * pair : 2 * pair + 2], axis=0).T.astype(f32)
        q = q_ref[:, 128 * pair : 128 * pair + 128].astype(f32)
        dv_scr[pair] += dot(p_ref[2 * pair], of_head(do, 0)) + dot(p_ref[2 * pair + 1], of_head(do, 1))
        ds = [ds_scr[2 * pair + h, 128 : 128 + n_keys, :] for h in range(2)]
        dk_scr[pair] += dot(ds[0], of_head(q, 0)) + dot(ds[1], of_head(q, 1))
    for h in range(n_heads):
        for t in range(blocks):
            rows = pl.ds(pl.multiple_of((block * blocks + t) * COORD, COORD), NEAR)
            near_scr[h] += ds_scr[h, rows, t * 128 : t * 128 + 128].astype(f32)

    some, _ = lone(lens, block, qb)

    @pl.when(some)
    def _():
        d_out = dot_nt(wo_ref[...], da_ref[...])
        product = d_out * ctxt_ref[...]
        for pair in range(n_heads // 2):
            cols = slice(pair * 128, pair * 128 + 128)
            q_t, kt, vt = q_ref[:, cols].T, k_ref[rows_q, cols].T, v_ref[rows_q, cols].T
            add_q, add_k, add_v = [], [], []
            for h in (2 * pair, 2 * pair + 1):
                mine = slice(h % 2 * HEAD, h % 2 * HEAD + HEAD)
                d_own = d_out[h * HEAD : h * HEAD + HEAD, :]
                p = rows_ref[n_heads + h : n_heads + h + 1, :]
                dp = jnp.sum(d_own * vt[mine, :].astype(f32) - product[h * HEAD : h * HEAD + HEAD, :], axis=0, keepdims=True)
                ds = p * dp
                add_q.append(kt[mine, :].astype(f32) * ds)
                add_k.append(q_t[mine, :].astype(f32) * ds)
                add_v.append(d_own * p)
                self_acc[h : h + 1, :] += ds
            at = slice(384 * pair, 384 * pair + 128)
            out_ref[rows_q, at] = (out_ref[rows_q, at].astype(f32) + jnp.concatenate(add_q, axis=0).T).astype(bf16)
            dk_scr[pair, rows_q, :] += jnp.concatenate(add_k, axis=0).T
            dv_scr[pair, rows_q, :] += jnp.concatenate(add_v, axis=0).T

    @pl.when(step == pl.num_programs(0) - 1)
    def _():
        for pair in range(n_heads // 2):
            out_ref[:, 384 * pair + 128 : 384 * pair + 256] = dk_scr[pair].astype(bf16)
            out_ref[:, 384 * pair + 256 : 384 * pair + 384] = dv_scr[pair].astype(bf16)
        offset = 256 - lax.broadcasted_iota(i32, (1, 512), 1)
        row, column = (lax.broadcasted_iota(i32, (NEAR, NEAR), at) for at in (0, 1))
        mirror = (row + column == NEAR - 1).astype(bf16)
        lane = lax.broadcasted_iota(i32, (n_keys, 128), 1)
        hots = [(box_cols[:, axis : axis + 1] == lane).astype(bf16) for axis in range(2)]
        sums = [jnp.zeros((1, 512), f32)] * 16
        for h in range(n_heads):
            high, rest = pieces(near_scr[h])[0:2]
            near = skew_sums(dot_tn(high.astype(bf16), mirror) + dot_tn(rest.astype(bf16), mirror), -128)
            left = jnp.sum(far_acc[h, 0], keepdims=True)
            right = jnp.sum(far_acc[h, 1], keepdims=True)
            alone = jnp.where(offset == 0, jnp.sum(self_acc[h : h + 1, :], keepdims=True), 0.0)
            far = jnp.where(offset == -255, left, 0.0) + jnp.where(offset == 255, right, 0.0)
            sums[h] = near + far + alone
            for axis in range(2):
                pairs = dot(part_scr[h, 128 * axis : 128 * axis + 128, :], hots[axis])
                sums[n_heads * (1 + axis) + h] = skew_sums(pairs.T, 0) + alone
        sums = jnp.concatenate(sums, axis=0)
        dtab_ref[...] = lax.dot_general(offset_hot(-1), sums, (((1,), (1,)), ((), ())), precision=lax.Precision.HIGHEST, preferred_element_type=f32)


def attend_back(ids, q, k, v, d_own, d_core, w_out, ctxt, rows, probs, lengths, box_cols, box_rows):
    n_keys, width = k.shape
    n_heads = width // HEAD
    qb = n_keys // 4
    model = w_out.shape[1]
    n_pairs = n_heads // 2
    at_rows = lambda i, ids, lens: (row_block(i, ids), 0)
    at_columns = lambda i, ids, lens: (0, row_block(i, ids))
    pieces_in = [(d, at) for at in range(2) for d in (d_own, d_core)]
    return pl.pallas_call(
        functools.partial(bwd_kernel, n_heads, qb),
        out_shape=[
            jax.ShapeDtypeStruct((n_keys, 384 * n_pairs), bf16),
            jax.ShapeDtypeStruct((NB, 16), f32),
            jax.ShapeDtypeStruct((n_keys, model), bf16),
        ],
        grid_spec=pltpu.PrefetchScalarGridSpec(
            num_scalar_prefetch=2,
            grid=(4,),
            in_specs=[
                whole(box_cols.shape), whole(box_rows.shape),
                pl.BlockSpec((qb, width), at_rows), whole(k.shape), whole(v.shape),
                *[pl.BlockSpec((qb, model), lambda i, ids, lens, at=at: (at, 0)) for _, at in pieces_in],
                whole(w_out.shape),
                pl.BlockSpec((width, qb), at_columns),
                pl.BlockSpec((8, qb), at_columns),
                pl.BlockSpec((n_heads, n_keys, qb), lambda i, ids, lens: (0, 0, row_block(i, ids))),
            ],
            out_specs=[whole((n_keys, 384 * n_pairs)), whole((NB, 16)), pl.BlockSpec((qb, model), at_rows)],
            scratch_shapes=[
                pltpu.VMEM((n_pairs, n_keys, 128 + EXTRA), bf16),
                pltpu.VMEM((n_pairs, 400, n_keys), bf16),
                pltpu.VMEM((n_heads, n_keys + 256, qb), bf16),
                pltpu.VMEM((n_pairs, n_keys, 128), f32),
                pltpu.VMEM((n_pairs, n_keys, 128), f32),
                pltpu.VMEM((n_heads, NEAR, COORD), f32),
                pltpu.VMEM((n_heads, 256, n_keys), bf16),
                pltpu.VMEM((n_heads, 2, 8, qb), f32),
                pltpu.VMEM((8, qb), f32),
            ],
        ),
        compiler_params=params(),
        cost_estimate=estimate(),
        name="attend_back",
    )(ids, lengths, box_cols, box_rows, q, k, v, *(d for d, _ in pieces_in), w_out, ctxt, rows, probs)


norm_eps = 1e-06
gelu_scale = 0.7978845608028654
gelu_cube = 0.044715


def scale_of(values):
    return lax.rsqrt(jnp.mean(values * values, axis=-1, keepdims=True) + norm_eps)


def anywhere():
    return pl.BlockSpec(memory_space=pl.ANY)


def estimate():
    return pl.CostEstimate(flops=1_000, bytes_accessed=1_000, transcendentals=0)


def qkv_kernel(ids, xa_ref, xb_ref, g_ref, wq_ref, wk_ref, wv_ref, *refs):
    xo_ref, n_ref, q_ref, k_ref, v_ref = refs[-5:]
    for at_step, piece in enumerate((xa_ref, xb_ref)):

        @pl.when(pl.program_id(0) == at_step)
        def _():
            xo_ref[...] = piece[...]

    x = xo_ref[...].astype(f32)
    normed = (x * scale_of(x) * g_ref[...]).astype(bf16)
    n_ref[...] = normed
    q_ref[...] = dot(normed, wq_ref[...]).astype(bf16)
    k_ref[...] = dot(normed, wk_ref[...]).astype(bf16)
    v_ref[...] = dot(normed, wv_ref[...]).astype(bf16)


def project(ids, far, pair, gain, weights, before, n_blocks):
    rows, model = pair[0].shape
    width = weights[0].shape[1]

    def row(i, ids):
        chip = 1 - ids[2] if far else ids[2]
        return (2 * chip + (i + ids[1]) % 2, 0)

    shapes = [jax.ShapeDtypeStruct((n_blocks * rows, n), bf16) for n in (model, model, width, width, width)]
    return pl.pallas_call(
        qkv_kernel,
        out_shape=shapes,
        grid_spec=pltpu.PrefetchScalarGridSpec(
            num_scalar_prefetch=1,
            grid=(2,),
            in_specs=[whole(pair[0].shape)] * 2 + [whole(gain.shape)] + [whole(w.shape) for w in weights] + [anywhere()] * len(before),
            out_specs=[pl.BlockSpec((rows, s.shape[1]), row) for s in shapes],
        ),
        input_output_aliases={7 + i: i for i in range(len(before))},
        compiler_params=params(),
        cost_estimate=estimate(),
        name="project",
    )(ids, *pair, gain, *weights, *before)


def assemble_kernel(ids, *refs):
    for at_step in range(4):

        @pl.when(pl.program_id(0) == at_step)
        def _():
            refs[4][...] = refs[at_step][...]


def assemble(ids, blocks):
    rows, model = blocks[0].shape

    def row(i, ids):
        chip = i // 2
        core = i % 2
        return (2 * ((ids[2] + chip) % 2) + (ids[1] + core) % 2, 0)

    return pl.pallas_call(
        assemble_kernel,
        out_shape=jax.ShapeDtypeStruct((4 * rows, model), bf16),
        grid_spec=pltpu.PrefetchScalarGridSpec(
            num_scalar_prefetch=1,
            grid=(4,),
            in_specs=[whole((rows, model))] * 4,
            out_specs=pl.BlockSpec((rows, model), row),
        ),
        compiler_params=params(),
        cost_estimate=estimate(),
        name="assemble",
    )(ids, *blocks)


def ffn_kernel(ids, a0, a1, a2, a3, b0, b1, b2, b3, x_ref, cot_ref, o0, o1, o2, o3, g_ref, wg_ref, wu_ref, wd_ref,
               mixed_ref, nf_ref, hid_ref, dg_ref, du_ref, dsend, dkeep, rsend, rkeep):
    first = pl.program_id(0) < 2
    mixed = x_ref[...].astype(f32)
    for a, b, o in ((a0, b0, o0), (a1, b1, o1), (a2, b2, o2), (a3, b3, o3)):
        mixed = mixed + dot(jnp.where(first, a[...], b[...]), o[...])
    normed = (mixed * scale_of(mixed) * g_ref[...]).astype(bf16)
    nf_ref[...] = normed
    gate = dot_nt(wg_ref[...], normed)
    up = dot_nt(wu_ref[...], normed)
    d_hidden = dot_nt(wd_ref[...], cot_ref[...])
    square = gate * gate
    t = jnp.tanh(gelu_scale * gate * (1.0 + gelu_cube * square))
    half = 0.5 * (1.0 + t)
    unit = gate * half
    slope = half + 0.5 * gate * (1.0 - t * t) * (gelu_scale * (1.0 + 3.0 * gelu_cube * square))
    hidden = (unit * up).astype(bf16)
    d_gate = (d_hidden * up * slope).astype(bf16)
    d_up = (d_hidden * unit).astype(bf16)
    hid_ref[...] = hidden
    dg_ref[...] = d_gate
    du_ref[...] = d_up
    d_normed = (dot_tn(d_gate, wg_ref[...]) + dot_tn(d_up, wu_ref[...])).astype(bf16)
    down = dot_tn(hidden, wd_ref[...]).astype(bf16)
    half = pl.program_id(0) % 2

    @pl.when(half == 0)
    def _():
        dsend[...] = d_normed
        rsend[...] = down

    @pl.when(half == 1)
    def _():
        dkeep[...] = d_normed
        rkeep[...] = down
        mixed_ref[...] = mixed


def ffn(ids, contexts, x_all, cot_all, w_outs, gain, w_gate_t, w_up_t, w_down):
    total, model = x_all.shape
    rows = total // 4
    width, hidden = contexts[0][0].shape[1], w_down.shape[0]

    def local_row(i, ids):
        return (i + 1 + ids[1]) % 2

    def row(i, ids):
        return i // 2 * 2 + local_row(i, ids)

    def part(chunk):
        return pl.BlockSpec((rows, width), lambda i, ids: (jnp.where(i // 2 == chunk, local_row(i, ids), ids[1] if chunk == 0 else 1 - ids[1]), 0))

    rows_spec = pl.BlockSpec((rows, model), lambda i, ids: (row(i, ids), 0))
    units_spec = pl.BlockSpec((hidden, rows), lambda i, ids: (0, row(i, ids)))
    half_spec = pl.BlockSpec((rows, model), lambda i, ids: (i // 2, 0))
    outs = [((2 * rows, model), f32, half_spec), ((total, model), bf16, rows_spec)]
    outs += [((hidden, total), bf16, units_spec)] * 3
    outs += [((2 * rows, model), bf16, half_spec)] * 4
    ins = [(a, part(chunk)) for chunk in range(2) for a in contexts[chunk]]
    ins += [(x_all, rows_spec), (cot_all, rows_spec)]
    ins += [(w, whole(w.shape)) for w in (*w_outs, gain, w_gate_t, w_up_t, w_down)]
    return call(ffn_kernel, ids, ins, outs, (4,), "ffn")


def norm_back(total, values, gain):
    r = scale_of(values)
    n = values * r
    e = gain * total
    return r * (e - n * jnp.mean(n * e, axis=-1, keepdims=True)), jnp.sum(total * n, axis=0, keepdims=True)


def mid_kernel(ids, a_ref, b_ref, mixed_ref, cot_ref, g_ref, dm_ref, da_ref, sum_ref):
    total = a_ref[...].astype(f32) + b_ref[...].astype(f32)
    grad, gain_sum = norm_back(total, mixed_ref[...], g_ref[...])
    d_mixed = cot_ref[...].astype(f32) + grad
    dm_ref[...] = d_mixed
    da_ref[...] = d_mixed.astype(bf16)
    step = pl.program_id(0)
    gain_sum = jnp.where(ids[2] == step // 2, gain_sum, 0.0)

    @pl.when(step == 0)
    def _():
        sum_ref[...] = gain_sum

    @pl.when(step > 0)
    def _():
        sum_ref[...] += gain_sum


def mid(ids, own, far, mixed, cot_all, gain):
    total, model = own.shape
    rows = total // 4
    spec = pl.BlockSpec((rows, model), lambda i, ids: (i, 0))
    cot_spec = pl.BlockSpec((rows, model), lambda i, ids: (i // 2 * 4 + 2 * ids[1] + i % 2, 0))
    ins = [(own, spec), (far, spec), (mixed, spec), (cot_all, cot_spec), (gain, whole(gain.shape))]
    outs = [((total, model), f32, spec), ((total, model), bf16, spec), ((1, model), f32, whole((1, model)))]
    return call(mid_kernel, ids, ins, outs, (4,), "mid")


def back_kernel(ids, a_ref, b_ref, wa_ref, wb_ref, *outs):
    total = dot_nt(a_ref[...], wa_ref[...]) + dot_nt(b_ref[...], wb_ref[...])
    for at_step, out in enumerate(outs):

        @pl.when(pl.program_id(0) == at_step)
        def _():
            out[...] = total.astype(out.dtype)


def project_back(ids, grads, weights):
    total = grads.shape[0]
    rows, (model, width) = total // 4, weights[0].shape

    def row(i, ids):
        return 2 * ((1 - i // 2 + ids[2]) % 2) + (i + 1 + ids[1]) % 2

    ins = [(grads, pl.BlockSpec((rows, width), lambda i, ids, at=at: (row(i, ids), at))) for at in range(2)]
    ins += [(w, whole(w.shape)) for w in weights]
    outs = [((rows, model), kind, whole((rows, model))) for kind in (bf16, f32, bf16, f32)]
    return call(back_kernel, ids, ins, outs, (4,), "project_back")


def last_kernel(ids, keep_ref, core_ref, y_ref, x_ref, g_ref, dm_ref, out_ref, sum_ref):
    total = keep_ref[...] + core_ref[...].astype(f32) + y_ref[...].astype(f32)
    grad, gain_sum = norm_back(total, x_ref[...].astype(f32), g_ref[...])
    out_ref[...] = dm_ref[...] + grad
    sum_ref[...] = gain_sum


def last(ids, keep, core, far, x, gain, d_mixed):
    ins = [(a, whole(a.shape)) for a in (keep, core, far, x, gain)]
    ins.append((d_mixed, pl.BlockSpec(keep.shape, lambda i, ids: (ids[2], 0))))
    outs = [(shape, f32, whole(shape)) for shape in (keep.shape, (1, keep.shape[1]))]
    return call(last_kernel, ids, ins, outs, (1,), "last")


def bit_orders(shards):
    bits = list(range(shards.bit_length() - 1))
    return bits, bits[1:] + bits[:1]


def slot_of(flip, order):
    place = 0
    for bit in order[1:]:
        place = 2 * place + (flip >> bit) % 2
    return (flip >> order[0]) % 2, place


def unit_parts_kernel(ids, *refs):
    n = 3
    kept_a, sent_a, kept_b, sent_b = refs[2 * n :]
    step = pl.program_id(0)
    low, high = step % 2, step // 2
    even = ids[3] % 2 == 0
    nears, fars = [], []
    for i in range(n):
        out = dot(refs[i][...], refs[n + i][...]).astype(bf16)
        width, cut = out.shape[1] // 2, out.shape[0] // 2
        first, second = out[:, :width], out[:, width:]
        nears.append(jnp.where(even, first, second))
        fars.append(jnp.where(even, second, first))
        kept_a[2 * low + high, i] = nears[i][:cut]
        sent_a[2 * low + high, i] = fars[i][:cut]

    @pl.when(low == 0)
    def _():
        for i in range(n):
            kept_b[2 * high, i] = nears[i][cut:]
            kept_b[2 * high + 1, i] = fars[i][cut:]

    @pl.when(low == 1)
    def _():
        for i in range(n):
            sent_b[2 * high, i] = nears[i][cut:]
            sent_b[2 * high + 1, i] = fars[i][cut:]


def unit_parts(ids, lefts, rights):
    n = len(lefts)
    total, model = rights[0].shape
    hidden = lefts[0].shape[0]
    shape = (4, n, hidden // 2, model // 8)
    return pl.pallas_call(
        unit_parts_kernel,
        out_shape=[jax.ShapeDtypeStruct(shape, bf16)] * 4,
        grid_spec=pltpu.PrefetchScalarGridSpec(
            num_scalar_prefetch=1,
            grid=(4,),
            in_specs=[whole(a.shape) for a in lefts] + [pl.BlockSpec((total, model // 4), lambda i, ids: (0, i ^ (ids[3] // 2)))] * n,
            out_specs=[whole(shape)] * 4,
        ),
        compiler_params=params(),
        cost_estimate=estimate(),
        name="unit_parts",
    )(ids, *lefts, *rights)


def unit_sums_kernel(n, split, *refs):
    out_ref = refs[-1]
    for i in range(n):
        out = dot(refs[i][...], refs[n + i][...]).astype(bf16)
        width = out.shape[1] // split
        for part in range(split):
            out_ref[part, i] = out[:, part * width : part * width + width]


def unit_sums(lefts, rights, shards):
    n = len(lefts)
    total, model = rights[0].shape
    hidden = lefts[0].shape[0]
    cut = model // shards
    step = 256
    split = step // cut if cut % 128 == 0 else 1
    out = pl.pallas_call(
        functools.partial(unit_sums_kernel, n, split),
        out_shape=jax.ShapeDtypeStruct((model // step * split, n, hidden, step // split), bf16),
        grid=(model // step,),
        in_specs=[whole(a.shape) for a in lefts] + [pl.BlockSpec((total, step), lambda i: (0, i))] * n,
        out_specs=pl.BlockSpec((split, n, hidden, step // split), lambda i: (i, 0, 0, 0)),
        compiler_params=params(),
        cost_estimate=estimate(),
        name="unit_sums",
    )(*lefts, *rights)
    if split == 1:
        out = out.reshape(model // step, n, hidden, step // cut, cut)
        out = out.transpose(0, 3, 1, 2, 4).reshape(shards, n, hidden, cut)
    return out


def head_sums_kernel(shards, ids, normed_ref, da_ref, g_ref, ctx_ref, ka_ref, sa_ref, kb_ref, sb_ref, acc, turned):
    outs = ((ka_ref, sa_ref), (kb_ref, sb_ref))
    cut = acc.shape[0] // shards
    turned[...] = normed_ref[...].T
    acc[:, 0:768] = dot(turned[...], g_ref[...])
    turned[...] = da_ref[...].T
    acc[:, 768:] = dot(turned[...], ctx_ref[...])
    for group, order in enumerate(bit_orders(shards)):
        for flip in range(shards):
            sent, place = slot_of(flip, order)
            at = (ids[3] ^ flip) * cut + group * (cut // 2)
            rows = pl.ds(pl.multiple_of(at, cut // 2), cut // 2)
            outs[group][sent][place] = acc[rows, :].astype(bf16)


def head_sums(ids, normed, d_attn, grads, context, shards):
    total, model = normed.shape
    columns = grads.shape[1] + context.shape[1]
    shape = (shards // 2, model // shards // 2, columns)
    ins = [(a, whole(a.shape)) for a in (normed, d_attn, grads, context)]
    return pl.pallas_call(
        functools.partial(head_sums_kernel, shards),
        out_shape=[jax.ShapeDtypeStruct(shape, bf16)] * 4,
        grid_spec=pltpu.PrefetchScalarGridSpec(
            num_scalar_prefetch=1,
            grid=(1,),
            in_specs=[spec for _, spec in ins],
            out_specs=[whole(shape)] * 4,
            scratch_shapes=[pltpu.VMEM((model, columns), f32), pltpu.VMEM((model, total), bf16)],
        ),
        compiler_params=params(),
        cost_estimate=estimate(),
        name="head_sums",
    )(ids, *(a for a, _ in ins))


def swap(sent, bit, n_dp):
    return lax.ppermute(sent, "dp", [(i, i ^ (1 << bit)) for i in range(n_dp)])


def call(kernel, ids, ins, outs, grid, name):
    return pl.pallas_call(
        kernel,
        out_shape=[jax.ShapeDtypeStruct(shape, kind) for shape, kind, _ in outs],
        grid_spec=pltpu.PrefetchScalarGridSpec(
            num_scalar_prefetch=1,
            grid=grid,
            in_specs=[spec for _, spec in ins],
            out_specs=[spec for _, _, spec in outs],
        ),
        compiler_params=params(),
        cost_estimate=estimate(),
        name=name,
    )(ids, *(array for array, _ in ins))


def out_kernel(ids, ka_ref, ca_ref, kb_ref, cb_ref, send_ref, own_ref):
    sum_a = ka_ref[...].astype(f32) + ca_ref[...].astype(f32)
    sum_b = kb_ref[...].astype(f32) + cb_ref[...].astype(f32)
    first = ids[2] == 0
    send_ref[...] = jnp.where(first, sum_b, sum_a).astype(bf16)
    own_ref[...] = jnp.where(first, sum_a, sum_b)


def out_sums(ids, keep, core):
    rows, model = keep.shape[0] // 2, keep.shape[1]
    low = pl.BlockSpec((rows // 2, model), lambda i, ids: (i, 0))
    high = pl.BlockSpec((rows // 2, model), lambda i, ids: (2 + i, 0))
    ins = [(keep, low), (core, low), (keep, high), (core, high)]
    return call(out_kernel, ids, ins, [((rows, model), bf16, low), ((rows, model), f32, low)], (2,), "out_sums")


def result_kernel(ids, mixed_ref, own_ref, far_ref, out_ref):
    out_ref[...] = mixed_ref[...] + own_ref[...] + far_ref[...].astype(f32)


def result_of(ids, mixed, own, far):
    rows, model = own.shape
    spec = pl.BlockSpec((rows // 2, model), lambda i, ids: (i, 0))
    ins = [(mixed, pl.BlockSpec((rows // 2, model), lambda i, ids: (2 * ids[2] + i, 0))), (own, spec), (far, spec)]
    return call(result_kernel, ids, ins, [(own.shape, f32, spec)], (2,), "result_of")[0]


def onward_kernel(n, ids, *refs):
    for i in range(n):
        low, high, came_low, came_high = refs[4 * i : 4 * i + 4]
        keep, send = refs[4 * n + 2 * i : 4 * n + 2 * i + 2]
        keep[...] = (low[...].astype(f32) + came_low[...].astype(f32)).astype(bf16)
        send[...] = (high[...].astype(f32) + came_high[...].astype(f32)).astype(bf16)


def onward(ids, kept, came):
    ins, outs = [], []
    half = kept[0].shape[0] // 2
    for k, c in zip(kept, came, strict=True):
        block = (1,) + k.shape[1:]
        rest = (0,) * (k.ndim - 1)
        low = pl.BlockSpec(block, lambda i, ids, rest=rest: (i,) + rest)
        high = pl.BlockSpec(block, lambda i, ids, rest=rest: (half + i,) + rest)
        ins += [(k, low), (k, high), (c, low), (c, high)]
        outs += [((half,) + k.shape[1:], bf16, low)] * 2
    got = call(functools.partial(onward_kernel, len(kept)), ids, ins, outs, (half,), "onward")
    return got[0::2], got[1::2]


def unit_last_kernel(ids, ka, ca, kb, cb, *outs):
    cut = ka.shape[2]
    for i, out in enumerate(outs):
        out[0:cut, :] = ka[0, i].astype(f32) + ca[0, i].astype(f32)
        out[cut:, :] = kb[0, i].astype(f32) + cb[0, i].astype(f32)


def unit_last(ids, kept, came):
    _, n, cut, columns = kept[0].shape
    ins = [(a, whole(a.shape)) for a in (kept[0], came[0], kept[1], came[1])]
    outs = [((2 * cut, columns), f32, whole((2 * cut, columns)))] * n
    return call(unit_last_kernel, ids, ins, outs, (1,), "unit_last")


def head_last_kernel(ids, ka, ca, kb, cb, *outs):
    rows = ka.shape[1]
    both = jnp.concatenate([k[0].astype(f32) + c[0].astype(f32) for k, c in ((ka, ca), (kb, cb))], axis=0)
    for i, out in enumerate(outs[:3]):
        out[:, 0:128] = both[:, 128 * i : 128 * i + 128]
        out[:, 128:256] = both[:, 384 + 128 * i : 512 + 128 * i]
    outs[3][...] = both[:, 768:].T


def head_last(ids, kept, came):
    _, rows, columns = kept[0].shape
    ins = [(a, whole(a.shape)) for a in (kept[0], came[0], kept[1], came[1])]
    outs = [((2 * rows, 256), f32, whole((2 * rows, 256)))] * 3 + [((256, 2 * rows), f32, whole((256, 2 * rows)))]
    return call(head_last_kernel, ids, ins, outs, (1,), "head_last")


def local(
    tokens, w_query, w_key, w_value, w_attn_out, w_gate, w_up, w_down, norm_attn, norm_ffn,
    rel_table, x_table, y_table, lengths, boxes, cotangent,
):
    n_mp, n_dp = lax.axis_size("mp"), lax.axis_size("dp")
    me = lax.axis_index("mp")
    core, chip = me % 2, me // 2
    ids = jnp.stack([me, core, chip, lax.axis_index("dp")]).astype(i32)
    rows, model = tokens.shape

    def by_core(a):
        return lax.ppermute(a, "mp", [(i, i ^ 1) for i in range(n_mp)])

    def by_chip(a):
        return lax.ppermute(a, "mp", [(i, i ^ 2) for i in range(n_mp)])

    def together(*arrays):
        return lax.optimization_barrier(arrays)

    def after(a, *earlier):
        return lax.optimization_barrier((a, *earlier))[0]

    def exchange_small(a):
        return lax.all_to_all(a, ("dp", "mp"), split_axis=0, concat_axis=0, tiled=True)

    n_heads = w_query.shape[1] // HEAD
    tables = jnp.concatenate([rel_table.T, x_table.T, y_table.T, jnp.zeros((16 - 3 * n_heads, NB), f32)], axis=0)
    box_cols = boxes.T
    gain_attn, gain_ffn = norm_attn.reshape(1, model), norm_ffn.reshape(1, model)
    weights = (w_query, w_key, w_value)
    w_gate_t, w_up_t = w_gate.T, w_up.T

    x_chip = by_chip(tokens)
    group = project(ids, False, (tokens, by_core(tokens)), gain_attn, weights, [], n_mp)
    w_pairs = [jnp.concatenate([w[:, at : at + 128] for w in weights], axis=1) for at in (0, 128)]
    x_chip, _, box_cols, tables, *w_pairs = together(x_chip, group[0], box_cols, tables, *w_pairs)
    x_both = by_core(x_chip)
    w_chip = by_chip(after(w_attn_out, x_chip))
    c_chip = by_chip(after(cotangent, x_chip))
    group = project(ids, True, (x_chip, x_both), gain_attn, weights, group, n_mp)
    x_all, normed, queries, keys_all, values_all = group

    *kept, own_a = attend(0, queries, keys_all, values_all, tables, lengths, box_cols, boxes, [])
    core_a, far_a = by_core(own_a), by_chip(own_a)
    *kept, own_b = attend(1, after(queries, own_a), keys_all, values_all, tables, lengths, box_cols, boxes, kept)
    context, ctxt, factors, probs = kept
    own_b, core_a, far_a, w_chip, c_chip = together(own_b, core_a, far_a, w_chip, c_chip)
    core_b, far_b = by_core(own_b), by_chip(own_b)
    w_outs = (w_attn_out, by_core(w_attn_out), w_chip, by_core(w_chip))
    cot_all = assemble(ids, (cotangent, by_core(cotangent), c_chip, by_core(c_chip)))
    both_a = by_core(far_a)
    cot_all, far_b = together(cot_all, far_b)
    contexts = ((own_a, core_a, far_a, both_a), (own_b, core_b, far_b, by_core(far_b)))

    out = ffn(ids, contexts, x_all, cot_all, w_outs, gain_ffn, w_gate_t, w_up_t, w_down)
    mixed, normed_ffn, hidden, d_gate, d_up, d_send, d_keep, r_send, r_keep = out
    d_core = by_core(d_send)
    sums = (d_keep.astype(f32) + d_core.astype(f32)).astype(bf16)
    far_sums = by_chip(sums)
    r_core = by_core(after(r_send, sums))

    orders = bit_orders(n_dp)
    pairwise = n_dp == 8 and model == 1024
    unit_args = ((d_gate, d_up, hidden), (normed_ffn, normed_ffn, after(cot_all, sums)))
    if pairwise:
        unit = list(unit_parts(ids, *unit_args))
        r_out, r_own = out_sums(ids, r_keep, r_core)
        unit[0], unit[2], far_sums, r_out = together(unit[0], unit[2], far_sums, r_out)
        unit_came = [swap(unit[2 * i + 1], order[0], n_dp) for i, order in enumerate(orders)]
    else:
        unit = [unit_sums(*unit_args, n_dp)]
        r_out, r_own = out_sums(ids, r_keep, r_core)
        *unit, far_sums, r_out = together(*unit, far_sums, r_out)
        ffn_sums = lax.psum_scatter(unit[0], "dp", scatter_dimension=0, tiled=True)[0].astype(f32)
    d_mixed, d_own, gain_mid = mid(ids, sums, far_sums, mixed, cot_all, gain_ffn)
    d_core = by_core(d_own)

    r_far = by_chip(r_out)
    d_heads, d_tab, d_attn = attend_back(
        ids, queries, keys_all, values_all, d_own, d_core, w_attn_out, ctxt, factors, probs, lengths, box_cols, boxes
    )
    d_heads, r_far = together(d_heads, r_far)

    def swaps(sends, step):
        return [swap(send, order[step], n_dp) for send, order in zip(sends, orders, strict=True)]

    d_first = d_heads
    if pairwise:
        unit_came = together(*unit_came, d_heads)[:2]
        unit_kept, sends = onward(ids, unit[0::2], unit_came)
        unit_came = swaps(sends, 1)
        d_first = after(d_heads, *sends)
    f_send, f_keep, n_send, n_keep = project_back(ids, d_first, w_pairs)
    f_core, n_core = by_core(f_send), by_core(n_send)
    if pairwise:
        attn = head_sums(ids, normed, d_attn, after(d_heads, f_keep), context, n_dp)
        f_core, n_core, *attn = together(f_core, n_core, *attn)
        unit_came = together(*unit_came, attn[0])[:2]
        unit_kept, sends = onward(ids, unit_kept, unit_came)
        unit_came = swaps(sends, 2)
        f_core = after(f_core, *sends)
        came = swaps(attn[1::2], 0)
    f_sum = (f_keep + f_core.astype(f32)).astype(bf16)
    far = by_chip(f_sum)
    if pairwise:
        came[0], came[1], f_sum = together(*came, f_sum)
        kept, sends = onward(ids, attn[0::2], came)
        came = swaps(sends, 1)
        far = after(far, *sends)
    d_tokens, gain_first = last(ids, n_keep, n_core, far, tokens, gain_attn, d_mixed)

    gains = jnp.concatenate([gain_first, gain_mid], axis=0).reshape(2, n_dp, n_mp, -1).transpose(1, 2, 0, 3)
    n_gain = gains.shape[3]
    tabs = d_tab[:, : 3 * n_heads].reshape(n_dp, 1, -1)
    tabs = jnp.where(lax.broadcasted_iota(i32, (1, n_mp, 1), 1) == me, tabs, 0.0)
    small = jnp.concatenate([gains.reshape(n_dp, n_mp, 2 * n_gain), tabs], axis=2).reshape(n_dp * n_mp, -1)
    if pairwise:
        unit_came[0], unit_came[1], small = together(*unit_came, small)
        small = exchange_small(small)
        ffn_sums = unit_last(ids, unit_kept, unit_came)
        came[0], came[1], *ffn_sums = together(*came, *ffn_sums)
        kept, sends = onward(ids, kept, came)
        came = swaps(sends, 2)
        small = after(small, *sends).sum(axis=0)
        result = result_of(ids, mixed, r_own, after(r_far, *sends))
        came[0], came[1], result = together(*came, result)
        attn_sums = head_last(ids, kept, came)
    else:
        result = result_of(ids, mixed, r_own, r_far)
        wide = dot_tn(normed, d_heads)
        parts = [wide[:, 384 * pair + 128 * i : 384 * pair + 128 * i + 128] for i in range(3) for pair in range(2)]
        wide = [*parts, dot_tn(d_attn, context)]
        wide = jnp.concatenate(wide, axis=1).astype(bf16)
        wide = lax.psum_scatter(wide, "dp", scatter_dimension=0, tiled=True).astype(f32)
        attn_sums = [wide[:, 256 * i : 256 * i + 256] for i in range(4)]
        attn_sums[3] = attn_sums[3].T
        small = exchange_small(small).sum(axis=0)
    tabs = small[2 * n_gain :].reshape(-1, 3, n_heads)
    return (
        result, d_tokens,
        *attn_sums,
        ffn_sums[0].T, ffn_sums[1].T, ffn_sums[2],
        small[:n_gain], small[n_gain : 2 * n_gain], tabs[:, 0], tabs[:, 1], tabs[:, 2],
    )


def solution(mesh):
    in_specs = (
        P(("dp", "mp"), None),
        P(None, "mp"),
        P(None, "mp"),
        P(None, "mp"),
        P("mp", None),
        P(None, "mp"),
        P(None, "mp"),
        P("mp", None),
        P(),
        P(),
        P(None, "mp"),
        P(None, "mp"),
        P(None, "mp"),
        P("dp", None),
        P(None, "dp"),
        P(("dp", "mp"), None),
    )
    out_specs = (
        P(("dp", "mp"), None),
        P(("dp", "mp"), None),
        P("dp", "mp"),
        P("dp", "mp"),
        P("dp", "mp"),
        P("mp", "dp"),
        P("dp", "mp"),
        P("dp", "mp"),
        P("mp", "dp"),
        P(("dp", "mp")),
        P(("dp", "mp")),
        P("dp", "mp"),
        P("dp", "mp"),
        P("dp", "mp"),
    )
    return jax.shard_map(local, mesh=mesh, in_specs=in_specs, out_specs=out_specs, check_vma=False)
```

```python
import functools

import jax
import jax.numpy as jnp
from jax import lax
from jax.experimental import pallas as pl
from jax.experimental.pallas import tpu as pltpu
from jax.sharding import PartitionSpec as P

f32, bf16, i32 = jnp.float32, jnp.bfloat16, jnp.int32
HEAD = 64
NB = 32
COORD = 128
SHORT = 512
NEAR = 3 * COORD
EXTRA = 16
KEYS = 512
thresholds = (1, 2, 3, 4, 5, 6, 7, 8, 12, 16, 23, 32, 46, 64, 91)
masked_score = -1000000000.0


def dot(a, b):
    return jnp.dot(a, b, preferred_element_type=f32)


def dot_nt(a, b):
    return lax.dot_general(a, b, (((1,), (1,)), ((), ())), preferred_element_type=f32)


def dot_tn(a, b):
    return lax.dot_general(a, b, (((0,), (0,)), ((), ())), preferred_element_type=f32)


def bucket_of(offsets):
    distance = jnp.abs(offsets)
    bucket_ids = jnp.where(offsets > 0, NB // 2, 0)
    for threshold in thresholds:
        bucket_ids = bucket_ids + jnp.where(distance >= threshold, 1, 0)
    return bucket_ids


def offset_hot(sign=1):
    offsets = sign * (lax.broadcasted_iota(i32, (NB, 512), 1) - 256)
    return (bucket_of(offsets) == lax.broadcasted_iota(i32, (NB, 512), 0)).astype(f32)


def toeplitz(row, base):
    wide = jnp.broadcast_to(row, (COORD, 512))
    return pltpu.roll(wide, (256 - base) % 512, 1, stride=1, stride_axis=0)


def start_of(len0, len1):
    return jnp.where(len1 > 0, 1, 0), jnp.where(len1 > 0, len1, len0)


def build(lens, tab_ref, box_cols, box_rows, k_ref, b_scr, hot_scr, lut_scr, strip_scr, n_heads):
    n_keys = k_ref.shape[0]
    len0, len1 = lens[0, 0], lens[0, 1]
    start1, start1_len = start_of(len0, len1)
    lane = lax.broadcasted_iota(i32, (n_keys, COORD), 1)
    pos = lax.broadcasted_iota(i32, (n_keys, COORD), 0)
    x_hot = (box_cols[:, 0:1] == lane).astype(bf16)
    y_hot = (box_cols[:, 1:2] == lane).astype(bf16)
    second = pos >= SHORT
    start_k = jnp.where(second, start1, 0)
    limit = jnp.where(second, start1_len, len0)
    valid = pos - start_k * SHORT < limit
    masked0 = jnp.where(valid & (start_k == 0), 0.0, masked_score)
    masked1 = jnp.where(valid & (start_k == start1), 0.0, masked_score)
    extra = jnp.where(lane == 0, masked0, jnp.where(lane == 1, masked1, 0.0))
    extra = extra.astype(bf16)[:, 0:EXTRA]
    for pair in range(n_heads // 2):
        b_scr[pair, :, 0:128] = k_ref[:, pair * 128 : pair * 128 + 128]
        b_scr[pair, :, 128:256] = x_hot
        b_scr[pair, :, 256:384] = y_hot
        b_scr[pair, :, 384 : 384 + EXTRA] = extra
    level = lax.broadcasted_iota(i32, (COORD, n_keys), 0)
    hot_scr[0:128, :] = (box_rows[0:1, :] == level).astype(bf16)
    hot_scr[128:256, :] = (box_rows[1:2, :] == level).astype(bf16)
    vec = jnp.dot(tab_ref[...], offset_hot(), precision=lax.Precision.HIGHEST, preferred_element_type=f32)
    n_strip = strip_scr.shape[1]
    for h in range(n_heads):
        for axis in range(2):
            at = n_heads * (1 + axis) + h
            table = toeplitz(vec[at : at + 1, :], 0)[:, 0:128]
            lut_scr[h, axis] = table.T.astype(bf16)
        row = vec[h : h + 1, :]
        near = toeplitz(row, -128)[:, 0:NEAR]
        mid = (n_strip - NEAR) // 2
        left = jnp.broadcast_to(row[:, 0:1], (mid, COORD))
        right = jnp.broadcast_to(row[:, 511:512], (mid, COORD))
        strip_scr[h, 0:mid, :] = left
        strip_scr[h, mid : mid + NEAR, :] = near.T
        strip_scr[h, mid + NEAR :, :] = right


def query_side(lens, block, qb, h, qt, hot_q, lut_scr):
    half = jnp.zeros((HEAD, qb), bf16)
    own = qt[(h % 2) * HEAD : (h % 2) * HEAD + HEAD, :]
    parts = [own, half] if h % 2 == 0 else [half, own]
    x_rows = dot(lut_scr[h, 0], hot_q[0:128, :]).astype(bf16)
    y_rows = dot(lut_scr[h, 1], hot_q[128:256, :]).astype(bf16)
    row = lax.broadcasted_iota(i32, (EXTRA, qb), 0)
    q_pos = block * qb + lax.broadcasted_iota(i32, (EXTRA, qb), 1)
    extra = jnp.where(row == jnp.where(q_pos >= SHORT, 1, 0), 1.0, 0.0)
    return jnp.concatenate(parts + [x_rows, y_rows, extra.astype(bf16)], axis=0)


def pieces(value):
    high = value.astype(bf16).astype(f32)
    rest = value - high
    mid = rest.astype(bf16).astype(f32)
    return high, mid, (rest - mid).astype(bf16).astype(f32)


def scores(block, qb, h, at, b_scr, strip_scr, key_at):
    s = dot(b_scr[h // 2, key_at : key_at + KEYS, :], at)
    blocks = qb // COORD
    top = b_scr.shape[1] // COORD - 1
    parts = []
    for t in range(blocks):
        off = pl.multiple_of((top - (block * blocks + t)) * COORD + key_at, COORD)
        parts.append(s[:, t * 128 : t * 128 + 128] + strip_scr[h, pl.ds(off, KEYS), :])
    return jnp.concatenate(parts, axis=1)


def lone(lens, block, qb):
    len0, len1 = lens[0, 0], lens[0, 1]
    start1, start1_len = start_of(len0, len1)
    in_second = block * qb >= SHORT
    begin = jnp.where(in_second, start1, 0) * SHORT
    limit = jnp.where(in_second, start1_len, len0)
    pos = block * qb + lax.broadcasted_iota(i32, (1, qb), 1) - begin
    return block * qb + qb - 1 - begin >= limit, pos >= limit


def own_score(h, qt, kt, strip_scr, lut_scr):
    mine = slice((h % 2) * HEAD, (h % 2) * HEAD + HEAD)
    product = qt[mine, :].astype(f32) * kt[mine, :].astype(f32)
    centre = (strip_scr.shape[1] - COORD) // 2
    bias = strip_scr[h, centre : centre + 1, 0:1] + lut_scr[h, 0, 0:1, 0:1].astype(f32) + lut_scr[h, 1, 0:1, 0:1].astype(f32)
    return jnp.sum(product, axis=0, keepdims=True) + bias


def fwd_kernel(n_heads, qb, base, lens, tab_ref, box_cols, box_rows, q_ref, k_ref, v_ref, *refs):
    ctx_ref, ctxt_ref, rows_ref, p_ref, out_ref, b_scr, hot_scr, lut_scr, strip_scr, vt_scr, s_scr, top_scr, log_scr = refs[-13:]
    n_keys = k_ref.shape[0]
    block = pl.program_id(0) + base

    @pl.when(pl.program_id(0) == 0)
    def _():
        build(lens, tab_ref, box_cols, box_rows, k_ref, b_scr, hot_scr, lut_scr, strip_scr, n_heads)
        for pair in range(n_heads // 2):
            vt_scr[pair, 0:128, :] = v_ref[:, pair * 128 : pair * 128 + 128].T
            vt_scr[pair, 128:144, :] = jnp.ones((16, n_keys), bf16)

    hot_q = hot_scr[:, pl.ds(pl.multiple_of(block * qb, qb), qb)]
    for pair in range(n_heads // 2):
        qt = q_ref[:, pair * 128 : pair * 128 + 128].T
        halves = []
        for h in (2 * pair, 2 * pair + 1):
            at = query_side(lens, block, qb, h, qt, hot_q, lut_scr)
            top = None
            for key_at in range(0, n_keys, KEYS):
                s = scores(block, qb, h, at, b_scr, strip_scr, key_at)
                s_scr[h % 2, key_at : key_at + KEYS, :] = s
                high = jnp.max(s, axis=0, keepdims=True)
                top = high if top is None else jnp.maximum(top, high)
            out = None
            for key_at in range(0, n_keys, KEYS):
                p = jnp.exp(s_scr[h % 2, key_at : key_at + KEYS, :] - top).astype(bf16)
                p_ref[h, key_at : key_at + KEYS, :] = p
                part = dot(vt_scr[pair, :, key_at : key_at + KEYS], p)
                out = part if out is None else out + part
            total = out[128:129, :]
            factor = 1.0 / total
            halves.append(out[(h % 2) * HEAD : (h % 2) * HEAD + HEAD, :] * factor)
            rows_ref[h : h + 1, :] = factor
            rows_ref[n_heads + h : n_heads + h + 1, :] = jnp.zeros((1, qb), f32)
            top_scr[h : h + 1, :] = top
            log_scr[h : h + 1, :] = top + jnp.log(total)
        ctxt = jnp.concatenate(halves, axis=0)
        ctxt_ref[pair * 128 : pair * 128 + 128, :] = ctxt
        ctx_ref[:, pair * 128 : pair * 128 + 128] = ctxt.T.astype(bf16)
    some, which = lone(lens, block, qb)

    @pl.when(some)
    def _():
        rows_q = pl.ds(pl.multiple_of(block * qb, qb), qb)
        for pair in range(n_heads // 2):
            cols = slice(pair * 128, pair * 128 + 128)
            qt, kt = q_ref[:, cols].T, k_ref[rows_q, cols].T
            for h in (2 * pair, 2 * pair + 1):
                own = own_score(h, qt, kt, strip_scr, lut_scr)
                log = log_scr[h : h + 1, :]
                high = jnp.maximum(own, log)
                new = high + jnp.log(jnp.exp(own - high) + jnp.exp(log - high))
                mine = slice(h * HEAD, h * HEAD + HEAD)
                value = vt_scr[pair, (h % 2) * HEAD : (h % 2) * HEAD + HEAD, rows_q].astype(f32)
                old = ctxt_ref[mine, :]
                alone = jnp.exp(own - new)
                ctxt_ref[mine, :] = jnp.where(which, old * jnp.exp(log - new) + value * alone, old)
                factor = rows_ref[h : h + 1, :]
                rows_ref[h : h + 1, :] = jnp.where(which, jnp.exp(top_scr[h : h + 1, :] - new), factor)
                rows_ref[n_heads + h : n_heads + h + 1, :] = jnp.where(which, alone, 0.0)
            ctx_ref[:, cols] = ctxt_ref[cols, :].T.astype(bf16)

    out_ref[...] = ctx_ref[...]


def scratch(n_keys, n_heads):
    return [
        pltpu.VMEM((n_heads // 2, n_keys, 384 + EXTRA), bf16),
        pltpu.VMEM((256, n_keys), bf16),
        pltpu.VMEM((n_heads, 2, COORD, COORD), bf16),
        pltpu.VMEM((n_heads, 2 * n_keys - COORD, COORD), f32),
    ]


def whole(shape):
    return pl.BlockSpec(shape, lambda *at: (0,) * len(shape))


def params():
    return pltpu.CompilerParams(dimension_semantics=("arbitrary",), vmem_limit_bytes=255 << 18)


def row_block(step, ids):
    return step // 2 * 2 + (step + ids[1]) % 2


def attend(chunk, q, k, v, tables, lengths, box_cols, box_rows, before):
    n_keys, width = k.shape
    qb = n_keys // 4
    n_heads = width // HEAD
    return pl.pallas_call(
        functools.partial(fwd_kernel, n_heads, qb, 2 * chunk),
        out_shape=(
            jax.ShapeDtypeStruct((n_keys, width), bf16),
            jax.ShapeDtypeStruct((width, n_keys), f32),
            jax.ShapeDtypeStruct((8, n_keys), f32),
            jax.ShapeDtypeStruct((n_heads, n_keys, n_keys), bf16),
            jax.ShapeDtypeStruct((2 * qb, width), bf16),
        ),
        grid=(2,),
        in_specs=[
            pl.BlockSpec(memory_space=pltpu.SMEM),
            whole(tables.shape), whole(box_cols.shape), whole(box_rows.shape),
            pl.BlockSpec((qb, width), lambda i: (i + 2 * chunk, 0)), whole(k.shape), whole(v.shape),
        ] + [anywhere()] * len(before),
        out_specs=(
            pl.BlockSpec((qb, width), lambda i: (i + 2 * chunk, 0)),
            pl.BlockSpec((width, qb), lambda i: (0, i + 2 * chunk)),
            pl.BlockSpec((8, qb), lambda i: (0, i + 2 * chunk)),
            pl.BlockSpec((n_heads, n_keys, qb), lambda i: (0, 0, i + 2 * chunk)),
            pl.BlockSpec((qb, width), lambda i: (i, 0)),
        ),
        scratch_shapes=scratch(n_keys, n_heads) + [
            pltpu.VMEM((n_heads // 2, 144, n_keys), bf16),
            pltpu.VMEM((2, n_keys, qb), f32),
            pltpu.VMEM((8, qb), f32),
            pltpu.VMEM((8, qb), f32),
        ],
        input_output_aliases={7 + i: i for i in range(len(before))},
        compiler_params=params(),
        cost_estimate=estimate(),
        name="attend",
    )(lengths, tables, box_cols, box_rows, q, k, v, *before)


def skew_sums(tile, base):
    width = tile.shape[1]
    wide = jnp.concatenate([tile, jnp.zeros((128, 512 - width), f32)], axis=1)
    wide = pltpu.roll(wide, (257 - width - base) % 512, 1, stride=1, stride_axis=0)
    return jnp.sum(wide, axis=0, keepdims=True)


def bwd_kernel(n_heads, qb, ids, lens, box_cols, box_rows, q_ref, k_ref, v_ref, d0_ref, d1_ref, d2_ref, d3_ref, wo_ref, ctxt_ref, rows_ref, p_ref,
               out_ref, dtab_ref, da_ref, v_scr, kt_scr, ds_scr, dk_scr, dv_scr, near_scr, part_scr, far_acc, self_acc):
    step = pl.program_id(0)
    block = row_block(step, ids)
    n_keys = k_ref.shape[0]
    blocks = qb // COORD

    @pl.when(step == 0)
    def _():
        lane = lax.broadcasted_iota(i32, (n_keys, 128), 1)
        level = COORD - 1 - lax.broadcasted_iota(i32, (COORD, n_keys), 0)
        kb = lax.broadcasted_iota(i32, (16, n_keys), 0)
        kp = lax.broadcasted_iota(i32, (16, n_keys), 1)
        for pair in range(n_heads // 2):
            cols = slice(pair * 128, pair * 128 + 128)
            v_scr[pair, :, 0:128] = v_ref[:, cols]
            v_scr[pair, :, 128 : 128 + EXTRA] = jnp.where(lane < 3, -1.0, 0.0).astype(bf16)[:, 0:EXTRA]
            kt_scr[pair, 0:128, :] = k_ref[:, cols].T
            for axis in range(2):
                kt_scr[pair, 128 + 128 * axis : 256 + 128 * axis, :] = (box_rows[axis : axis + 1, :] == level).astype(bf16)
            kt_scr[pair, 384:400, :] = (kp // COORD == kb).astype(bf16)
        dk_scr[...] = jnp.zeros_like(dk_scr)
        dv_scr[...] = jnp.zeros_like(dv_scr)
        near_scr[...] = jnp.zeros_like(near_scr)
        far_acc[...] = jnp.zeros_like(far_acc)
        self_acc[...] = jnp.zeros_like(self_acc)
        for h in range(n_heads):
            ds_scr[h, 0:128, :] = jnp.zeros((128, qb), bf16)
            ds_scr[h, 128 + n_keys :, :] = jnp.zeros((128, qb), bf16)

    rows_q = pl.ds(pl.multiple_of(block * qb, qb), qb)
    lane_half = lax.broadcasted_iota(i32, (qb, 128), 1) >= HEAD
    for at_step, piece in enumerate((d0_ref, d1_ref, d2_ref, d3_ref)):

        @pl.when(step == at_step)
        def _():
            da_ref[...] = piece[...]

    d_ctx = dot_nt(wo_ref[...], da_ref[...])
    prod = d_ctx * ctxt_ref[...]
    scaled = []
    operands = []
    for h in range(n_heads):
        mine = slice(h * HEAD, h * HEAD + HEAD)
        factor = rows_ref[h : h + 1, :]
        delta = jnp.sum(prod[mine, :], axis=0, keepdims=True) * factor
        row = lax.broadcasted_iota(i32, (EXTRA, qb), 0)
        extra = jnp.zeros((EXTRA, qb), f32)
        for piece, value in enumerate(pieces(delta)):
            extra = jnp.where(row == piece, value, extra)
        none = jnp.zeros((HEAD, qb), bf16)
        own = (d_ctx[mine, :] * factor).astype(bf16)
        scaled.append(own)
        operands.append(jnp.concatenate(([own, none] if h % 2 == 0 else [none, own]) + [extra.astype(bf16)], axis=0))
    for h, dat in enumerate(operands):
        for key_at in range(0, n_keys, KEYS):
            dp = dot(v_scr[h // 2, key_at : key_at + KEYS, :], dat)
            p = p_ref[h, key_at : key_at + KEYS, :].astype(f32)
            ds_scr[h, 128 + key_at : 128 + key_at + KEYS, :] = (p * dp).astype(bf16)
    key_block = lax.broadcasted_iota(i32, (8, qb), 0)
    q_block = block * blocks + lax.broadcasted_iota(i32, (8, qb), 1) // COORD

    def of_head(x, h):
        return jnp.where(lane_half, x if h else 0.0, 0.0 if h else x).astype(bf16)

    for pair in range(n_heads // 2):
        dq_halves = []
        for h in (2 * pair, 2 * pair + 1):
            got = dot(kt_scr[pair], ds_scr[h, 128 : 128 + n_keys, :])
            dq_halves.append(got[h % 2 * HEAD : h % 2 * HEAD + HEAD, :])
            part_scr[h, :, rows_q] = got[128:384, :].astype(bf16)
            by_block = got[384:392, :]
            far_acc[h, 0] += jnp.where(key_block + 1 < q_block, by_block, 0.0)
            far_acc[h, 1] += jnp.where(key_block > q_block + 1, by_block, 0.0)
        out_ref[rows_q, 384 * pair : 384 * pair + 128] = jnp.concatenate(dq_halves, axis=0).T.astype(bf16)
        do = jnp.concatenate(scaled[2 * pair : 2 * pair + 2], axis=0).T.astype(f32)
        q = q_ref[:, 128 * pair : 128 * pair + 128].astype(f32)
        dv_scr[pair] += dot(p_ref[2 * pair], of_head(do, 0)) + dot(p_ref[2 * pair + 1], of_head(do, 1))
        ds = [ds_scr[2 * pair + h, 128 : 128 + n_keys, :] for h in range(2)]
        dk_scr[pair] += dot(ds[0], of_head(q, 0)) + dot(ds[1], of_head(q, 1))
    for h in range(n_heads):
        for t in range(blocks):
            rows = pl.ds(pl.multiple_of((block * blocks + t) * COORD, COORD), NEAR)
            near_scr[h] += ds_scr[h, rows, t * 128 : t * 128 + 128].astype(f32)

    some, _ = lone(lens, block, qb)

    @pl.when(some)
    def _():
        d_out = dot_nt(wo_ref[...], da_ref[...])
        product = d_out * ctxt_ref[...]
        for pair in range(n_heads // 2):
            cols = slice(pair * 128, pair * 128 + 128)
            q_t, kt, vt = q_ref[:, cols].T, k_ref[rows_q, cols].T, v_ref[rows_q, cols].T
            add_q, add_k, add_v = [], [], []
            for h in (2 * pair, 2 * pair + 1):
                mine = slice(h % 2 * HEAD, h % 2 * HEAD + HEAD)
                d_own = d_out[h * HEAD : h * HEAD + HEAD, :]
                p = rows_ref[n_heads + h : n_heads + h + 1, :]
                dp = jnp.sum(d_own * vt[mine, :].astype(f32) - product[h * HEAD : h * HEAD + HEAD, :], axis=0, keepdims=True)
                ds = p * dp
                add_q.append(kt[mine, :].astype(f32) * ds)
                add_k.append(q_t[mine, :].astype(f32) * ds)
                add_v.append(d_own * p)
                self_acc[h : h + 1, :] += ds
            at = slice(384 * pair, 384 * pair + 128)
            out_ref[rows_q, at] = (out_ref[rows_q, at].astype(f32) + jnp.concatenate(add_q, axis=0).T).astype(bf16)
            dk_scr[pair, rows_q, :] += jnp.concatenate(add_k, axis=0).T
            dv_scr[pair, rows_q, :] += jnp.concatenate(add_v, axis=0).T

    @pl.when(step == pl.num_programs(0) - 1)
    def _():
        for pair in range(n_heads // 2):
            out_ref[:, 384 * pair + 128 : 384 * pair + 256] = dk_scr[pair].astype(bf16)
            out_ref[:, 384 * pair + 256 : 384 * pair + 384] = dv_scr[pair].astype(bf16)
        offset = 256 - lax.broadcasted_iota(i32, (1, 512), 1)
        row, column = (lax.broadcasted_iota(i32, (NEAR, NEAR), at) for at in (0, 1))
        mirror = (row + column == NEAR - 1).astype(bf16)
        lane = lax.broadcasted_iota(i32, (n_keys, 128), 1)
        hots = [(box_cols[:, axis : axis + 1] == lane).astype(bf16) for axis in range(2)]
        sums = [jnp.zeros((1, 512), f32)] * 16
        for h in range(n_heads):
            high, rest = pieces(near_scr[h])[0:2]
            near = skew_sums(dot_tn(high.astype(bf16), mirror) + dot_tn(rest.astype(bf16), mirror), -128)
            left = jnp.sum(far_acc[h, 0], keepdims=True)
            right = jnp.sum(far_acc[h, 1], keepdims=True)
            alone = jnp.where(offset == 0, jnp.sum(self_acc[h : h + 1, :], keepdims=True), 0.0)
            far = jnp.where(offset == -255, left, 0.0) + jnp.where(offset == 255, right, 0.0)
            sums[h] = near + far + alone
            for axis in range(2):
                pairs = dot(part_scr[h, 128 * axis : 128 * axis + 128, :], hots[axis])
                sums[n_heads * (1 + axis) + h] = skew_sums(pairs.T, 0) + alone
        sums = jnp.concatenate(sums, axis=0)
        dtab_ref[...] = lax.dot_general(offset_hot(-1), sums, (((1,), (1,)), ((), ())), precision=lax.Precision.HIGHEST, preferred_element_type=f32)


def attend_back(ids, q, k, v, d_own, d_core, w_out, ctxt, rows, probs, lengths, box_cols, box_rows):
    n_keys, width = k.shape
    n_heads = width // HEAD
    qb = n_keys // 4
    model = w_out.shape[1]
    n_pairs = n_heads // 2
    at_rows = lambda i, ids, lens: (row_block(i, ids), 0)
    at_columns = lambda i, ids, lens: (0, row_block(i, ids))
    pieces_in = [(d, at) for at in range(2) for d in (d_own, d_core)]
    return pl.pallas_call(
        functools.partial(bwd_kernel, n_heads, qb),
        out_shape=[
            jax.ShapeDtypeStruct((n_keys, 384 * n_pairs), bf16),
            jax.ShapeDtypeStruct((NB, 16), f32),
            jax.ShapeDtypeStruct((n_keys, model), bf16),
        ],
        grid_spec=pltpu.PrefetchScalarGridSpec(
            num_scalar_prefetch=2,
            grid=(4,),
            in_specs=[
                whole(box_cols.shape), whole(box_rows.shape),
                pl.BlockSpec((qb, width), at_rows), whole(k.shape), whole(v.shape),
                *[pl.BlockSpec((qb, model), lambda i, ids, lens, at=at: (at, 0)) for _, at in pieces_in],
                whole(w_out.shape),
                pl.BlockSpec((width, qb), at_columns),
                pl.BlockSpec((8, qb), at_columns),
                pl.BlockSpec((n_heads, n_keys, qb), lambda i, ids, lens: (0, 0, row_block(i, ids))),
            ],
            out_specs=[whole((n_keys, 384 * n_pairs)), whole((NB, 16)), pl.BlockSpec((qb, model), at_rows)],
            scratch_shapes=[
                pltpu.VMEM((n_pairs, n_keys, 128 + EXTRA), bf16),
                pltpu.VMEM((n_pairs, 400, n_keys), bf16),
                pltpu.VMEM((n_heads, n_keys + 256, qb), bf16),
                pltpu.VMEM((n_pairs, n_keys, 128), f32),
                pltpu.VMEM((n_pairs, n_keys, 128), f32),
                pltpu.VMEM((n_heads, NEAR, COORD), f32),
                pltpu.VMEM((n_heads, 256, n_keys), bf16),
                pltpu.VMEM((n_heads, 2, 8, qb), f32),
                pltpu.VMEM((8, qb), f32),
            ],
        ),
        compiler_params=params(),
        cost_estimate=estimate(),
        name="attend_back",
    )(ids, lengths, box_cols, box_rows, q, k, v, *(d for d, _ in pieces_in), w_out, ctxt, rows, probs)


norm_eps = 1e-06
gelu_scale = 0.7978845608028654
gelu_cube = 0.044715


def scale_of(values):
    return lax.rsqrt(jnp.mean(values * values, axis=-1, keepdims=True) + norm_eps)


def anywhere():
    return pl.BlockSpec(memory_space=pl.ANY)


def estimate():
    return pl.CostEstimate(flops=1_000, bytes_accessed=1_000, transcendentals=0)


def qkv_kernel(ids, xa_ref, xb_ref, g_ref, wq_ref, wk_ref, wv_ref, *refs):
    xo_ref, n_ref, q_ref, k_ref, v_ref = refs[-5:]
    for at_step, piece in enumerate((xa_ref, xb_ref)):

        @pl.when(pl.program_id(0) == at_step)
        def _():
            xo_ref[...] = piece[...]

    x = xo_ref[...].astype(f32)
    normed = (x * scale_of(x) * g_ref[...]).astype(bf16)
    n_ref[...] = normed
    q_ref[...] = dot(normed, wq_ref[...]).astype(bf16)
    k_ref[...] = dot(normed, wk_ref[...]).astype(bf16)
    v_ref[...] = dot(normed, wv_ref[...]).astype(bf16)


def project(ids, far, pair, gain, weights, before, n_blocks):
    rows, model = pair[0].shape
    width = weights[0].shape[1]

    def row(i, ids):
        chip = 1 - ids[2] if far else ids[2]
        return (2 * chip + (i + ids[1]) % 2, 0)

    shapes = [jax.ShapeDtypeStruct((n_blocks * rows, n), bf16) for n in (model, model, width, width, width)]
    return pl.pallas_call(
        qkv_kernel,
        out_shape=shapes,
        grid_spec=pltpu.PrefetchScalarGridSpec(
            num_scalar_prefetch=1,
            grid=(2,),
            in_specs=[whole(pair[0].shape)] * 2 + [whole(gain.shape)] + [whole(w.shape) for w in weights] + [anywhere()] * len(before),
            out_specs=[pl.BlockSpec((rows, s.shape[1]), row) for s in shapes],
        ),
        input_output_aliases={7 + i: i for i in range(len(before))},
        compiler_params=params(),
        cost_estimate=estimate(),
        name="project",
    )(ids, *pair, gain, *weights, *before)


def assemble_kernel(ids, *refs):
    for at_step in range(4):

        @pl.when(pl.program_id(0) == at_step)
        def _():
            refs[4][...] = refs[at_step][...]


def assemble(ids, blocks):
    rows, model = blocks[0].shape

    def row(i, ids):
        chip = i // 2
        core = i % 2
        return (2 * ((ids[2] + chip) % 2) + (ids[1] + core) % 2, 0)

    return pl.pallas_call(
        assemble_kernel,
        out_shape=jax.ShapeDtypeStruct((4 * rows, model), bf16),
        grid_spec=pltpu.PrefetchScalarGridSpec(
            num_scalar_prefetch=1,
            grid=(4,),
            in_specs=[whole((rows, model))] * 4,
            out_specs=pl.BlockSpec((rows, model), row),
        ),
        compiler_params=params(),
        cost_estimate=estimate(),
        name="assemble",
    )(ids, *blocks)


def ffn_kernel(ids, a0, a1, a2, a3, b0, b1, b2, b3, x_ref, cot_ref, o0, o1, o2, o3, g_ref, wg_ref, wu_ref, wd_ref,
               mixed_ref, nf_ref, hid_ref, dg_ref, du_ref, dsend, dkeep, rsend, rkeep):
    first = pl.program_id(0) == 0
    mixed = x_ref[...].astype(f32)
    for a, b, o in ((a0, b0, o0), (a1, b1, o1), (a2, b2, o2), (a3, b3, o3)):
        mixed = mixed + dot(jnp.where(first, a[...], b[...]), o[...])
    normed = (mixed * scale_of(mixed) * g_ref[...]).astype(bf16)
    nf_ref[...] = normed
    gate = dot_nt(wg_ref[...], normed)
    up = dot_nt(wu_ref[...], normed)
    d_hidden = dot_nt(wd_ref[...], cot_ref[...])
    square = gate * gate
    t = jnp.tanh(gelu_scale * gate * (1.0 + gelu_cube * square))
    half = 0.5 * (1.0 + t)
    unit = gate * half
    slope = half + 0.5 * gate * (1.0 - t * t) * (gelu_scale * (1.0 + 3.0 * gelu_cube * square))
    hidden = (unit * up).astype(bf16)
    d_gate = (d_hidden * up * slope).astype(bf16)
    d_up = (d_hidden * unit).astype(bf16)
    hid_ref[...] = hidden
    dg_ref[...] = d_gate
    du_ref[...] = d_up
    d_normed = (dot_tn(d_gate, wg_ref[...]) + dot_tn(d_up, wu_ref[...])).astype(bf16)
    down = dot_tn(hidden, wd_ref[...]).astype(bf16)
    rows = mixed.shape[0] // 2
    lower = ids[1] == 0
    for value, other, own in ((d_normed, dsend, dkeep), (down, rsend, rkeep)):
        other[...] = jnp.where(lower, value[rows:], value[:rows])
        own[...] = jnp.where(lower, value[:rows], value[rows:])
    mixed_ref[...] = jnp.where(lower, mixed[:rows], mixed[rows:])


def ffn(ids, contexts, x_all, cot_all, w_outs, gain, w_gate_t, w_up_t, w_down):
    total, model = x_all.shape
    rows = total // 4
    hidden = w_down.shape[0]
    rows_spec = pl.BlockSpec((2 * rows, model), lambda i, ids: (i, 0))
    units_spec = pl.BlockSpec((hidden, 2 * rows), lambda i, ids: (0, i))
    half_spec = pl.BlockSpec((rows, model), lambda i, ids: (i, 0))
    outs = [((2 * rows, model), f32, half_spec), ((total, model), bf16, rows_spec)]
    outs += [((hidden, total), bf16, units_spec)] * 3
    outs += [((2 * rows, model), bf16, half_spec)] * 4
    ins = [(a, whole(a.shape)) for chunk in range(2) for a in contexts[chunk]]
    ins += [(x_all, rows_spec), (cot_all, rows_spec)]
    ins += [(w, whole(w.shape)) for w in (*w_outs, gain, w_gate_t, w_up_t, w_down)]
    return call(ffn_kernel, ids, ins, outs, (2,), "ffn")


def norm_back(total, values, gain):
    r = scale_of(values)
    n = values * r
    e = gain * total
    return r * (e - n * jnp.mean(n * e, axis=-1, keepdims=True)), jnp.sum(total * n, axis=0, keepdims=True)


def mid_kernel(ids, a_ref, b_ref, mixed_ref, cot_ref, g_ref, dm_ref, da_ref, sum_ref):
    total = a_ref[...].astype(f32) + b_ref[...].astype(f32)
    grad, gain_sum = norm_back(total, mixed_ref[...], g_ref[...])
    d_mixed = cot_ref[...].astype(f32) + grad
    dm_ref[...] = d_mixed
    da_ref[...] = d_mixed.astype(bf16)
    step = pl.program_id(0)
    gain_sum = jnp.where(ids[2] == step // 2, gain_sum, 0.0)

    @pl.when(step == 0)
    def _():
        sum_ref[...] = gain_sum

    @pl.when(step > 0)
    def _():
        sum_ref[...] += gain_sum


def mid(ids, own, far, mixed, cot_all, gain):
    total, model = own.shape
    rows = total // 4
    spec = pl.BlockSpec((rows, model), lambda i, ids: (i, 0))
    cot_spec = pl.BlockSpec((rows, model), lambda i, ids: (i // 2 * 4 + 2 * ids[1] + i % 2, 0))
    ins = [(own, spec), (far, spec), (mixed, spec), (cot_all, cot_spec), (gain, whole(gain.shape))]
    outs = [((total, model), f32, spec), ((total, model), bf16, spec), ((1, model), f32, whole((1, model)))]
    return call(mid_kernel, ids, ins, outs, (4,), "mid")


def back_kernel(ids, a_ref, b_ref, wa_ref, wb_ref, *outs):
    total = dot_nt(a_ref[...], wa_ref[...]) + dot_nt(b_ref[...], wb_ref[...])
    rows = total.shape[0] // 2
    first = ids[1] == 0
    other = jnp.where(first, total[rows:], total[:rows]).astype(bf16)
    own = jnp.where(first, total[:rows], total[rows:])
    for at_step in range(2):

        @pl.when(pl.program_id(0) == at_step)
        def _():
            outs[2 * at_step][...] = other
            outs[2 * at_step + 1][...] = own


def project_back(ids, grads, weights):
    total = grads.shape[0]
    rows, (model, width) = total // 4, weights[0].shape
    ins = [(grads, pl.BlockSpec((2 * rows, width), lambda i, ids, at=at: ((1 - i + ids[2]) % 2, at))) for at in range(2)]
    ins += [(w, whole(w.shape)) for w in weights]
    outs = [((rows, model), kind, whole((rows, model))) for kind in (bf16, f32, bf16, f32)]
    return call(back_kernel, ids, ins, outs, (2,), "project_back")


def last_kernel(ids, keep_ref, core_ref, y_ref, x_ref, g_ref, dm_ref, out_ref, sum_ref):
    total = keep_ref[...] + core_ref[...].astype(f32) + y_ref[...].astype(f32)
    grad, gain_sum = norm_back(total, x_ref[...].astype(f32), g_ref[...])
    out_ref[...] = dm_ref[...] + grad
    sum_ref[...] = gain_sum


def last(ids, keep, core, far, x, gain, d_mixed):
    ins = [(a, whole(a.shape)) for a in (keep, core, far, x, gain)]
    ins.append((d_mixed, pl.BlockSpec(keep.shape, lambda i, ids: (ids[2], 0))))
    outs = [(shape, f32, whole(shape)) for shape in (keep.shape, (1, keep.shape[1]))]
    return call(last_kernel, ids, ins, outs, (1,), "last")


def bit_orders(shards):
    bits = list(range(shards.bit_length() - 1))
    return bits, bits[1:] + bits[:1]


def slot_of(flip, order):
    place = 0
    for bit in order[1:]:
        place = 2 * place + (flip >> bit) % 2
    return (flip >> order[0]) % 2, place


def unit_parts_kernel(ids, *refs):
    n = 3
    kept_a, sent_a, kept_b, sent_b = refs[2 * n :]
    step = pl.program_id(0)
    low, high = step % 2, step // 2
    even = ids[3] % 2 == 0
    nears, fars = [], []
    for i in range(n):
        out = dot(refs[i][...], refs[n + i][...]).astype(bf16)
        width, cut = out.shape[1] // 2, out.shape[0] // 2
        first, second = out[:, :width], out[:, width:]
        nears.append(jnp.where(even, first, second))
        fars.append(jnp.where(even, second, first))
        kept_a[2 * low + high, i] = nears[i][:cut]
        sent_a[2 * low + high, i] = fars[i][:cut]

    @pl.when(low == 0)
    def _():
        for i in range(n):
            kept_b[2 * high, i] = nears[i][cut:]
            kept_b[2 * high + 1, i] = fars[i][cut:]

    @pl.when(low == 1)
    def _():
        for i in range(n):
            sent_b[2 * high, i] = nears[i][cut:]
            sent_b[2 * high + 1, i] = fars[i][cut:]


def unit_parts(ids, lefts, rights):
    n = len(lefts)
    total, model = rights[0].shape
    hidden = lefts[0].shape[0]
    shape = (4, n, hidden // 2, model // 8)
    return pl.pallas_call(
        unit_parts_kernel,
        out_shape=[jax.ShapeDtypeStruct(shape, bf16)] * 4,
        grid_spec=pltpu.PrefetchScalarGridSpec(
            num_scalar_prefetch=1,
            grid=(4,),
            in_specs=[whole(a.shape) for a in lefts] + [pl.BlockSpec((total, model // 4), lambda i, ids: (0, i ^ (ids[3] // 2)))] * n,
            out_specs=[whole(shape)] * 4,
        ),
        compiler_params=params(),
        cost_estimate=estimate(),
        name="unit_parts",
    )(ids, *lefts, *rights)


def unit_sums_kernel(n, split, *refs):
    out_ref = refs[-1]
    for i in range(n):
        out = dot(refs[i][...], refs[n + i][...]).astype(bf16)
        width = out.shape[1] // split
        for part in range(split):
            out_ref[part, i] = out[:, part * width : part * width + width]


def unit_sums(lefts, rights, shards):
    n = len(lefts)
    total, model = rights[0].shape
    hidden = lefts[0].shape[0]
    cut = model // shards
    step = 256
    split = step // cut if cut % 128 == 0 else 1
    out = pl.pallas_call(
        functools.partial(unit_sums_kernel, n, split),
        out_shape=jax.ShapeDtypeStruct((model // step * split, n, hidden, step // split), bf16),
        grid=(model // step,),
        in_specs=[whole(a.shape) for a in lefts] + [pl.BlockSpec((total, step), lambda i: (0, i))] * n,
        out_specs=pl.BlockSpec((split, n, hidden, step // split), lambda i: (i, 0, 0, 0)),
        compiler_params=params(),
        cost_estimate=estimate(),
        name="unit_sums",
    )(*lefts, *rights)
    if split == 1:
        out = out.reshape(model // step, n, hidden, step // cut, cut)
        out = out.transpose(0, 3, 1, 2, 4).reshape(shards, n, hidden, cut)
    return out


def head_sums_kernel(shards, ids, normed_ref, da_ref, g_ref, ctx_ref, ka_ref, sa_ref, kb_ref, sb_ref, acc, turned):
    outs = ((ka_ref, sa_ref), (kb_ref, sb_ref))
    cut = acc.shape[0] // shards
    turned[...] = normed_ref[...].T
    acc[:, 0:768] = dot(turned[...], g_ref[...])
    turned[...] = da_ref[...].T
    acc[:, 768:] = dot(turned[...], ctx_ref[...])
    for group, order in enumerate(bit_orders(shards)):
        for flip in range(shards):
            sent, place = slot_of(flip, order)
            at = (ids[3] ^ flip) * cut + group * (cut // 2)
            rows = pl.ds(pl.multiple_of(at, cut // 2), cut // 2)
            outs[group][sent][place] = acc[rows, :].astype(bf16)


def head_sums(ids, normed, d_attn, grads, context, shards):
    total, model = normed.shape
    columns = grads.shape[1] + context.shape[1]
    shape = (shards // 2, model // shards // 2, columns)
    ins = [(a, whole(a.shape)) for a in (normed, d_attn, grads, context)]
    return pl.pallas_call(
        functools.partial(head_sums_kernel, shards),
        out_shape=[jax.ShapeDtypeStruct(shape, bf16)] * 4,
        grid_spec=pltpu.PrefetchScalarGridSpec(
            num_scalar_prefetch=1,
            grid=(1,),
            in_specs=[spec for _, spec in ins],
            out_specs=[whole(shape)] * 4,
            scratch_shapes=[pltpu.VMEM((model, columns), f32), pltpu.VMEM((model, total), bf16)],
        ),
        compiler_params=params(),
        cost_estimate=estimate(),
        name="head_sums",
    )(ids, *(a for a, _ in ins))


def swap(sent, bit, n_dp):
    return lax.ppermute(sent, "dp", [(i, i ^ (1 << bit)) for i in range(n_dp)])


def call(kernel, ids, ins, outs, grid, name):
    return pl.pallas_call(
        kernel,
        out_shape=[jax.ShapeDtypeStruct(shape, kind) for shape, kind, _ in outs],
        grid_spec=pltpu.PrefetchScalarGridSpec(
            num_scalar_prefetch=1,
            grid=grid,
            in_specs=[spec for _, spec in ins],
            out_specs=[spec for _, _, spec in outs],
        ),
        compiler_params=params(),
        cost_estimate=estimate(),
        name=name,
    )(ids, *(array for array, _ in ins))


def out_kernel(ids, ka_ref, ca_ref, kb_ref, cb_ref, send_ref, own_ref):
    sum_a = ka_ref[...].astype(f32) + ca_ref[...].astype(f32)
    sum_b = kb_ref[...].astype(f32) + cb_ref[...].astype(f32)
    first = ids[2] == 0
    send_ref[...] = jnp.where(first, sum_b, sum_a).astype(bf16)
    own_ref[...] = jnp.where(first, sum_a, sum_b)


def out_sums(ids, keep, core):
    rows, model = keep.shape[0] // 2, keep.shape[1]
    low = pl.BlockSpec((rows // 2, model), lambda i, ids: (i, 0))
    high = pl.BlockSpec((rows // 2, model), lambda i, ids: (2 + i, 0))
    ins = [(keep, low), (core, low), (keep, high), (core, high)]
    return call(out_kernel, ids, ins, [((rows, model), bf16, low), ((rows, model), f32, low)], (2,), "out_sums")


def result_kernel(ids, mixed_ref, own_ref, far_ref, out_ref):
    out_ref[...] = mixed_ref[...] + own_ref[...] + far_ref[...].astype(f32)


def result_of(ids, mixed, own, far):
    rows, model = own.shape
    spec = pl.BlockSpec((rows // 2, model), lambda i, ids: (i, 0))
    ins = [(mixed, pl.BlockSpec((rows // 2, model), lambda i, ids: (2 * ids[2] + i, 0))), (own, spec), (far, spec)]
    return call(result_kernel, ids, ins, [(own.shape, f32, spec)], (2,), "result_of")[0]


def onward_kernel(n, ids, *refs):
    for i in range(n):
        low, high, came_low, came_high = refs[4 * i : 4 * i + 4]
        keep, send = refs[4 * n + 2 * i : 4 * n + 2 * i + 2]
        keep[...] = (low[...].astype(f32) + came_low[...].astype(f32)).astype(bf16)
        send[...] = (high[...].astype(f32) + came_high[...].astype(f32)).astype(bf16)


def onward(ids, kept, came):
    ins, outs = [], []
    half = kept[0].shape[0] // 2
    for k, c in zip(kept, came, strict=True):
        block = (1,) + k.shape[1:]
        rest = (0,) * (k.ndim - 1)
        low = pl.BlockSpec(block, lambda i, ids, rest=rest: (i,) + rest)
        high = pl.BlockSpec(block, lambda i, ids, rest=rest: (half + i,) + rest)
        ins += [(k, low), (k, high), (c, low), (c, high)]
        outs += [((half,) + k.shape[1:], bf16, low)] * 2
    got = call(functools.partial(onward_kernel, len(kept)), ids, ins, outs, (half,), "onward")
    return got[0::2], got[1::2]


def unit_last_kernel(ids, ka, ca, kb, cb, *outs):
    cut = ka.shape[2]
    for i, out in enumerate(outs):
        out[0:cut, :] = ka[0, i].astype(f32) + ca[0, i].astype(f32)
        out[cut:, :] = kb[0, i].astype(f32) + cb[0, i].astype(f32)


def unit_last(ids, kept, came):
    _, n, cut, columns = kept[0].shape
    ins = [(a, whole(a.shape)) for a in (kept[0], came[0], kept[1], came[1])]
    outs = [((2 * cut, columns), f32, whole((2 * cut, columns)))] * n
    return call(unit_last_kernel, ids, ins, outs, (1,), "unit_last")


def head_last_kernel(ids, ka, ca, kb, cb, *outs):
    rows = ka.shape[1]
    both = jnp.concatenate([k[0].astype(f32) + c[0].astype(f32) for k, c in ((ka, ca), (kb, cb))], axis=0)
    for i, out in enumerate(outs[:3]):
        out[:, 0:128] = both[:, 128 * i : 128 * i + 128]
        out[:, 128:256] = both[:, 384 + 128 * i : 512 + 128 * i]
    outs[3][...] = both[:, 768:].T


def head_last(ids, kept, came):
    _, rows, columns = kept[0].shape
    ins = [(a, whole(a.shape)) for a in (kept[0], came[0], kept[1], came[1])]
    outs = [((2 * rows, 256), f32, whole((2 * rows, 256)))] * 3 + [((256, 2 * rows), f32, whole((256, 2 * rows)))]
    return call(head_last_kernel, ids, ins, outs, (1,), "head_last")


def local(
    tokens, w_query, w_key, w_value, w_attn_out, w_gate, w_up, w_down, norm_attn, norm_ffn,
    rel_table, x_table, y_table, lengths, boxes, cotangent,
):
    n_mp, n_dp = lax.axis_size("mp"), lax.axis_size("dp")
    me = lax.axis_index("mp")
    core, chip = me % 2, me // 2
    ids = jnp.stack([me, core, chip, lax.axis_index("dp")]).astype(i32)
    rows, model = tokens.shape

    def by_core(a):
        return lax.ppermute(a, "mp", [(i, i ^ 1) for i in range(n_mp)])

    def by_chip(a):
        return lax.ppermute(a, "mp", [(i, i ^ 2) for i in range(n_mp)])

    def together(*arrays):
        return lax.optimization_barrier(arrays)

    def after(a, *earlier):
        return lax.optimization_barrier((a, *earlier))[0]

    def exchange_small(a):
        return lax.all_to_all(a, ("dp", "mp"), split_axis=0, concat_axis=0, tiled=True)

    n_heads = w_query.shape[1] // HEAD
    tables = jnp.concatenate([rel_table.T, x_table.T, y_table.T, jnp.zeros((16 - 3 * n_heads, NB), f32)], axis=0)
    box_cols = boxes.T
    gain_attn, gain_ffn = norm_attn.reshape(1, model), norm_ffn.reshape(1, model)
    weights = (w_query, w_key, w_value)
    w_gate_t, w_up_t = w_gate.T, w_up.T

    x_chip = by_chip(tokens)
    group = project(ids, False, (tokens, by_core(tokens)), gain_attn, weights, [], n_mp)
    w_pairs = [jnp.concatenate([w[:, at : at + 128] for w in weights], axis=1) for at in (0, 128)]
    x_chip, _, box_cols, tables, *w_pairs = together(x_chip, group[0], box_cols, tables, *w_pairs)
    x_both = by_core(x_chip)
    w_chip = by_chip(after(w_attn_out, x_chip))
    c_chip = by_chip(after(cotangent, x_chip))
    group = project(ids, True, (x_chip, x_both), gain_attn, weights, group, n_mp)
    x_all, normed, queries, keys_all, values_all = group

    *kept, own_a = attend(0, queries, keys_all, values_all, tables, lengths, box_cols, boxes, [])
    core_a, far_a = by_core(own_a), by_chip(own_a)
    *kept, own_b = attend(1, after(queries, own_a), keys_all, values_all, tables, lengths, box_cols, boxes, kept)
    context, ctxt, factors, probs = kept
    own_b, core_a, far_a, w_chip, c_chip = together(own_b, core_a, far_a, w_chip, c_chip)
    core_b, far_b = by_core(own_b), by_chip(own_b)
    w_outs = (w_attn_out, by_core(w_attn_out), w_chip, by_core(w_chip))
    cot_all = assemble(ids, (cotangent, by_core(cotangent), c_chip, by_core(c_chip)))
    both_a = by_core(far_a)
    cot_all, far_b = together(cot_all, far_b)
    contexts = ((own_a, core_a, far_a, both_a), (own_b, core_b, far_b, by_core(far_b)))

    out = ffn(ids, contexts, x_all, cot_all, w_outs, gain_ffn, w_gate_t, w_up_t, w_down)
    mixed, normed_ffn, hidden, d_gate, d_up, d_send, d_keep, r_send, r_keep = out
    d_core = by_core(d_send)
    sums = (d_keep.astype(f32) + d_core.astype(f32)).astype(bf16)
    far_sums = by_chip(sums)
    r_core = by_core(after(r_send, sums))

    orders = bit_orders(n_dp)
    pairwise = n_dp == 8 and model == 1024
    unit_args = ((d_gate, d_up, hidden), (normed_ffn, normed_ffn, after(cot_all, sums)))
    if pairwise:
        unit = list(unit_parts(ids, *unit_args))
        r_out, r_own = out_sums(ids, r_keep, r_core)
        unit[0], unit[2], far_sums, r_out = together(unit[0], unit[2], far_sums, r_out)
        unit_came = [swap(unit[2 * i + 1], order[0], n_dp) for i, order in enumerate(orders)]
    else:
        unit = [unit_sums(*unit_args, n_dp)]
        r_out, r_own = out_sums(ids, r_keep, r_core)
        *unit, far_sums, r_out = together(*unit, far_sums, r_out)
        ffn_sums = lax.psum_scatter(unit[0], "dp", scatter_dimension=0, tiled=True)[0].astype(f32)
    d_mixed, d_own, gain_mid = mid(ids, sums, far_sums, mixed, cot_all, gain_ffn)
    d_core = by_core(d_own)

    r_far = by_chip(r_out)
    d_heads, d_tab, d_attn = attend_back(
        ids, queries, keys_all, values_all, d_own, d_core, w_attn_out, ctxt, factors, probs, lengths, box_cols, boxes
    )
    d_heads, r_far = together(d_heads, r_far)

    def swaps(sends, step):
        return [swap(send, order[step], n_dp) for send, order in zip(sends, orders, strict=True)]

    d_first = d_heads
    if pairwise:
        unit_came = together(*unit_came, d_heads)[:2]
        unit_kept, sends = onward(ids, unit[0::2], unit_came)
        unit_came = swaps(sends, 1)
        d_first = after(d_heads, *sends)
    f_send, f_keep, n_send, n_keep = project_back(ids, d_first, w_pairs)
    f_core, n_core = by_core(f_send), by_core(n_send)
    if pairwise:
        attn = head_sums(ids, normed, d_attn, after(d_heads, f_keep), context, n_dp)
        f_core, n_core, *attn = together(f_core, n_core, *attn)
        result = result_of(ids, mixed, r_own, after(r_far, attn[0]))
        *unit_came, result = together(*unit_came, result)
        unit_kept, sends = onward(ids, unit_kept, unit_came)
        unit_came = swaps(sends, 2)
        f_core = after(f_core, *sends)
        came = swaps(attn[1::2], 0)
    f_sum = (f_keep + f_core.astype(f32)).astype(bf16)
    far = by_chip(f_sum)
    if pairwise:
        came[0], came[1], f_sum = together(*came, f_sum)
        kept, sends = onward(ids, attn[0::2], came)
        came = swaps(sends, 1)
        far = after(far, *sends)
    d_tokens, gain_first = last(ids, n_keep, n_core, far, tokens, gain_attn, d_mixed)

    gains = jnp.concatenate([gain_first, gain_mid], axis=0).reshape(2, n_dp, n_mp, -1).transpose(1, 2, 0, 3)
    n_gain = gains.shape[3]
    tabs = d_tab[:, : 3 * n_heads].reshape(n_dp, 1, -1)
    tabs = jnp.where(lax.broadcasted_iota(i32, (1, n_mp, 1), 1) == me, tabs, 0.0)
    small = jnp.concatenate([gains.reshape(n_dp, n_mp, 2 * n_gain), tabs], axis=2).reshape(n_dp * n_mp, -1)
    if pairwise:
        unit_came[0], unit_came[1], small = together(*unit_came, small)
        small = exchange_small(small)
        ffn_sums = unit_last(ids, unit_kept, unit_came)
        came[0], came[1], *ffn_sums = together(*came, *ffn_sums)
        kept, sends = onward(ids, kept, came)
        came = swaps(sends, 2)
        small = after(small, *sends).sum(axis=0)
        attn_sums = head_last(ids, kept, came)
    else:
        result = result_of(ids, mixed, r_own, r_far)
        wide = dot_tn(normed, d_heads)
        parts = [wide[:, 384 * pair + 128 * i : 384 * pair + 128 * i + 128] for i in range(3) for pair in range(2)]
        wide = [*parts, dot_tn(d_attn, context)]
        wide = jnp.concatenate(wide, axis=1).astype(bf16)
        wide = lax.psum_scatter(wide, "dp", scatter_dimension=0, tiled=True).astype(f32)
        attn_sums = [wide[:, 256 * i : 256 * i + 256] for i in range(4)]
        attn_sums[3] = attn_sums[3].T
        small = exchange_small(small).sum(axis=0)
    tabs = small[2 * n_gain :].reshape(-1, 3, n_heads)
    return (
        result, d_tokens,
        *attn_sums,
        ffn_sums[0].T, ffn_sums[1].T, ffn_sums[2],
        small[:n_gain], small[n_gain : 2 * n_gain], tabs[:, 0], tabs[:, 1], tabs[:, 2],
    )


def solution(mesh):
    in_specs = (
        P(("dp", "mp"), None),
        P(None, "mp"),
        P(None, "mp"),
        P(None, "mp"),
        P("mp", None),
        P(None, "mp"),
        P(None, "mp"),
        P("mp", None),
        P(),
        P(),
        P(None, "mp"),
        P(None, "mp"),
        P(None, "mp"),
        P("dp", None),
        P(None, "dp"),
        P(("dp", "mp"), None),
    )
    out_specs = (
        P(("dp", "mp"), None),
        P(("dp", "mp"), None),
        P("dp", "mp"),
        P("dp", "mp"),
        P("dp", "mp"),
        P("mp", "dp"),
        P("dp", "mp"),
        P("dp", "mp"),
        P("mp", "dp"),
        P(("dp", "mp")),
        P(("dp", "mp")),
        P("dp", "mp"),
        P("dp", "mp"),
        P("dp", "mp"),
    )
    return jax.shard_map(local, mesh=mesh, in_specs=in_specs, out_specs=out_specs, check_vma=False)
```

```python
import functools

import jax
import jax.numpy as jnp
from jax import lax
from jax.experimental import pallas as pl
from jax.experimental.pallas import tpu as pltpu
from jax.sharding import PartitionSpec as P

f32, bf16, i32 = jnp.float32, jnp.bfloat16, jnp.int32
HEAD = 64
NB = 32
COORD = 128
SHORT = 512
NEAR = 3 * COORD
EXTRA = 16
KEYS = 512
thresholds = (1, 2, 3, 4, 5, 6, 7, 8, 12, 16, 23, 32, 46, 64, 91)
masked_score = -1000000000.0


def dot(a, b):
    return jnp.dot(a, b, preferred_element_type=f32)


def dot_nt(a, b):
    return lax.dot_general(a, b, (((1,), (1,)), ((), ())), preferred_element_type=f32)


def dot_tn(a, b):
    return lax.dot_general(a, b, (((0,), (0,)), ((), ())), preferred_element_type=f32)


def bucket_of(offsets):
    distance = jnp.abs(offsets)
    bucket_ids = jnp.where(offsets > 0, NB // 2, 0)
    for threshold in thresholds:
        bucket_ids = bucket_ids + jnp.where(distance >= threshold, 1, 0)
    return bucket_ids


def offset_hot(sign=1):
    offsets = sign * (lax.broadcasted_iota(i32, (NB, 512), 1) - 256)
    return (bucket_of(offsets) == lax.broadcasted_iota(i32, (NB, 512), 0)).astype(f32)


def toeplitz(row, base):
    wide = jnp.broadcast_to(row, (COORD, 512))
    return pltpu.roll(wide, (256 - base) % 512, 1, stride=1, stride_axis=0)


def start_of(len0, len1):
    return jnp.where(len1 > 0, 1, 0), jnp.where(len1 > 0, len1, len0)


def build(lens, tab_ref, box_cols, box_rows, k_ref, b_scr, hot_scr, lut_scr, strip_scr, n_heads):
    n_keys = k_ref.shape[0]
    len0, len1 = lens[0, 0], lens[0, 1]
    start1, start1_len = start_of(len0, len1)
    lane = lax.broadcasted_iota(i32, (n_keys, COORD), 1)
    pos = lax.broadcasted_iota(i32, (n_keys, COORD), 0)
    x_hot = (box_cols[:, 0:1] == lane).astype(bf16)
    y_hot = (box_cols[:, 1:2] == lane).astype(bf16)
    second = pos >= SHORT
    start_k = jnp.where(second, start1, 0)
    limit = jnp.where(second, start1_len, len0)
    valid = pos - start_k * SHORT < limit
    masked0 = jnp.where(valid & (start_k == 0), 0.0, masked_score)
    masked1 = jnp.where(valid & (start_k == start1), 0.0, masked_score)
    extra = jnp.where(lane == 0, masked0, jnp.where(lane == 1, masked1, 0.0))
    extra = extra.astype(bf16)[:, 0:EXTRA]
    for pair in range(n_heads // 2):
        b_scr[pair, :, 0:128] = k_ref[:, pair * 128 : pair * 128 + 128]
        b_scr[pair, :, 128:256] = x_hot
        b_scr[pair, :, 256:384] = y_hot
        b_scr[pair, :, 384 : 384 + EXTRA] = extra
    level = lax.broadcasted_iota(i32, (COORD, n_keys), 0)
    hot_scr[0:128, :] = (box_rows[0:1, :] == level).astype(bf16)
    hot_scr[128:256, :] = (box_rows[1:2, :] == level).astype(bf16)
    vec = jnp.dot(tab_ref[...], offset_hot(), precision=lax.Precision.HIGHEST, preferred_element_type=f32)
    n_strip = strip_scr.shape[1]
    for h in range(n_heads):
        for axis in range(2):
            at = n_heads * (1 + axis) + h
            table = toeplitz(vec[at : at + 1, :], 0)[:, 0:128]
            lut_scr[h, axis] = table.T.astype(bf16)
        row = vec[h : h + 1, :]
        near = toeplitz(row, -128)[:, 0:NEAR]
        mid = (n_strip - NEAR) // 2
        left = jnp.broadcast_to(row[:, 0:1], (mid, COORD))
        right = jnp.broadcast_to(row[:, 511:512], (mid, COORD))
        strip_scr[h, 0:mid, :] = left
        strip_scr[h, mid : mid + NEAR, :] = near.T
        strip_scr[h, mid + NEAR :, :] = right


def query_side(lens, block, qb, h, qt, hot_q, lut_scr):
    half = jnp.zeros((HEAD, qb), bf16)
    own = qt[(h % 2) * HEAD : (h % 2) * HEAD + HEAD, :]
    parts = [own, half] if h % 2 == 0 else [half, own]
    x_rows = dot(lut_scr[h, 0], hot_q[0:128, :]).astype(bf16)
    y_rows = dot(lut_scr[h, 1], hot_q[128:256, :]).astype(bf16)
    row = lax.broadcasted_iota(i32, (EXTRA, qb), 0)
    q_pos = block * qb + lax.broadcasted_iota(i32, (EXTRA, qb), 1)
    extra = jnp.where(row == jnp.where(q_pos >= SHORT, 1, 0), 1.0, 0.0)
    return jnp.concatenate(parts + [x_rows, y_rows, extra.astype(bf16)], axis=0)


def pieces(value):
    high = value.astype(bf16).astype(f32)
    rest = value - high
    mid = rest.astype(bf16).astype(f32)
    return high, mid, (rest - mid).astype(bf16).astype(f32)


def scores(block, qb, h, at, b_scr, strip_scr, key_at):
    s = dot(b_scr[h // 2, key_at : key_at + KEYS, :], at)
    blocks = qb // COORD
    top = b_scr.shape[1] // COORD - 1
    parts = []
    for t in range(blocks):
        off = pl.multiple_of((top - (block * blocks + t)) * COORD + key_at, COORD)
        parts.append(s[:, t * 128 : t * 128 + 128] + strip_scr[h, pl.ds(off, KEYS), :])
    return jnp.concatenate(parts, axis=1)


def lone(lens, block, qb):
    len0, len1 = lens[0, 0], lens[0, 1]
    start1, start1_len = start_of(len0, len1)
    in_second = block * qb >= SHORT
    begin = jnp.where(in_second, start1, 0) * SHORT
    limit = jnp.where(in_second, start1_len, len0)
    pos = block * qb + lax.broadcasted_iota(i32, (1, qb), 1) - begin
    return block * qb + qb - 1 - begin >= limit, pos >= limit


def own_score(h, qt, kt, strip_scr, lut_scr):
    mine = slice((h % 2) * HEAD, (h % 2) * HEAD + HEAD)
    product = qt[mine, :].astype(f32) * kt[mine, :].astype(f32)
    centre = (strip_scr.shape[1] - COORD) // 2
    bias = strip_scr[h, centre : centre + 1, 0:1] + lut_scr[h, 0, 0:1, 0:1].astype(f32) + lut_scr[h, 1, 0:1, 0:1].astype(f32)
    return jnp.sum(product, axis=0, keepdims=True) + bias


def fwd_kernel(n_heads, qb, base, lens, tab_ref, box_cols, box_rows, q_ref, k_ref, v_ref, *refs):
    ctx_ref, ctxt_ref, rows_ref, p_ref, out_ref, b_scr, hot_scr, lut_scr, strip_scr, vt_scr, s_scr, top_scr, log_scr = refs[-13:]
    n_keys = k_ref.shape[0]
    block = pl.program_id(0) + base

    @pl.when(pl.program_id(0) == 0)
    def _():
        build(lens, tab_ref, box_cols, box_rows, k_ref, b_scr, hot_scr, lut_scr, strip_scr, n_heads)
        for pair in range(n_heads // 2):
            vt_scr[pair, 0:128, :] = v_ref[:, pair * 128 : pair * 128 + 128].T
            vt_scr[pair, 128:144, :] = jnp.ones((16, n_keys), bf16)

    hot_q = hot_scr[:, pl.ds(pl.multiple_of(block * qb, qb), qb)]
    for pair in range(n_heads // 2):
        qt = q_ref[:, pair * 128 : pair * 128 + 128].T
        halves = []
        for h in (2 * pair, 2 * pair + 1):
            at = query_side(lens, block, qb, h, qt, hot_q, lut_scr)
            top = None
            for key_at in range(0, n_keys, KEYS):
                s = scores(block, qb, h, at, b_scr, strip_scr, key_at)
                s_scr[h % 2, key_at : key_at + KEYS, :] = s
                high = jnp.max(s, axis=0, keepdims=True)
                top = high if top is None else jnp.maximum(top, high)
            out = None
            for key_at in range(0, n_keys, KEYS):
                p = jnp.exp(s_scr[h % 2, key_at : key_at + KEYS, :] - top).astype(bf16)
                p_ref[h, key_at : key_at + KEYS, :] = p
                part = dot(vt_scr[pair, :, key_at : key_at + KEYS], p)
                out = part if out is None else out + part
            total = out[128:129, :]
            factor = 1.0 / total
            halves.append(out[(h % 2) * HEAD : (h % 2) * HEAD + HEAD, :] * factor)
            rows_ref[h : h + 1, :] = factor
            rows_ref[n_heads + h : n_heads + h + 1, :] = jnp.zeros((1, qb), f32)
            top_scr[h : h + 1, :] = top
            log_scr[h : h + 1, :] = top + jnp.log(total)
        ctxt = jnp.concatenate(halves, axis=0)
        ctxt_ref[pair * 128 : pair * 128 + 128, :] = ctxt
        ctx_ref[:, pair * 128 : pair * 128 + 128] = ctxt.T.astype(bf16)
    some, which = lone(lens, block, qb)

    @pl.when(some)
    def _():
        rows_q = pl.ds(pl.multiple_of(block * qb, qb), qb)
        for pair in range(n_heads // 2):
            cols = slice(pair * 128, pair * 128 + 128)
            qt, kt = q_ref[:, cols].T, k_ref[rows_q, cols].T
            for h in (2 * pair, 2 * pair + 1):
                own = own_score(h, qt, kt, strip_scr, lut_scr)
                log = log_scr[h : h + 1, :]
                high = jnp.maximum(own, log)
                new = high + jnp.log(jnp.exp(own - high) + jnp.exp(log - high))
                mine = slice(h * HEAD, h * HEAD + HEAD)
                value = vt_scr[pair, (h % 2) * HEAD : (h % 2) * HEAD + HEAD, rows_q].astype(f32)
                old = ctxt_ref[mine, :]
                alone = jnp.exp(own - new)
                ctxt_ref[mine, :] = jnp.where(which, old * jnp.exp(log - new) + value * alone, old)
                factor = rows_ref[h : h + 1, :]
                rows_ref[h : h + 1, :] = jnp.where(which, jnp.exp(top_scr[h : h + 1, :] - new), factor)
                rows_ref[n_heads + h : n_heads + h + 1, :] = jnp.where(which, alone, 0.0)
            ctx_ref[:, cols] = ctxt_ref[cols, :].T.astype(bf16)

    out_ref[...] = ctx_ref[...]


def scratch(n_keys, n_heads):
    return [
        pltpu.VMEM((n_heads // 2, n_keys, 384 + EXTRA), bf16),
        pltpu.VMEM((256, n_keys), bf16),
        pltpu.VMEM((n_heads, 2, COORD, COORD), bf16),
        pltpu.VMEM((n_heads, 2 * n_keys - COORD, COORD), f32),
    ]


def whole(shape):
    return pl.BlockSpec(shape, lambda *at: (0,) * len(shape))


def params():
    return pltpu.CompilerParams(dimension_semantics=("arbitrary",), vmem_limit_bytes=255 << 18)


def attend(chunk, q, k, v, tables, lengths, box_cols, box_rows, before):
    n_keys, width = k.shape
    qb = n_keys // 4
    n_heads = width // HEAD
    return pl.pallas_call(
        functools.partial(fwd_kernel, n_heads, qb, 2 * chunk),
        out_shape=(
            jax.ShapeDtypeStruct((n_keys, width), bf16),
            jax.ShapeDtypeStruct((width, n_keys), f32),
            jax.ShapeDtypeStruct((8, n_keys), f32),
            jax.ShapeDtypeStruct((n_heads, n_keys, n_keys), bf16),
            jax.ShapeDtypeStruct((2 * qb, width), bf16),
        ),
        grid=(2,),
        in_specs=[
            pl.BlockSpec(memory_space=pltpu.SMEM),
            whole(tables.shape), whole(box_cols.shape), whole(box_rows.shape),
            pl.BlockSpec((qb, width), lambda i: (i + 2 * chunk, 0)), whole(k.shape), whole(v.shape),
        ] + [anywhere()] * len(before),
        out_specs=(
            pl.BlockSpec((qb, width), lambda i: (i + 2 * chunk, 0)),
            pl.BlockSpec((width, qb), lambda i: (0, i + 2 * chunk)),
            pl.BlockSpec((8, qb), lambda i: (0, i + 2 * chunk)),
            pl.BlockSpec((n_heads, n_keys, qb), lambda i: (0, 0, i + 2 * chunk)),
            pl.BlockSpec((qb, width), lambda i: (i, 0)),
        ),
        scratch_shapes=scratch(n_keys, n_heads) + [
            pltpu.VMEM((n_heads // 2, 144, n_keys), bf16),
            pltpu.VMEM((2, n_keys, qb), f32),
            pltpu.VMEM((8, qb), f32),
            pltpu.VMEM((8, qb), f32),
        ],
        input_output_aliases={7 + i: i for i in range(len(before))},
        compiler_params=params(),
        cost_estimate=estimate(),
        name="attend",
    )(lengths, tables, box_cols, box_rows, q, k, v, *before)


def skew_sums(tile, base):
    width = tile.shape[1]
    wide = jnp.concatenate([tile, jnp.zeros((128, 512 - width), f32)], axis=1)
    wide = pltpu.roll(wide, (257 - width - base) % 512, 1, stride=1, stride_axis=0)
    return jnp.sum(wide, axis=0, keepdims=True)


def bwd_kernel(n_heads, qb, ids, lens, box_cols, box_rows, q_ref, k_ref, v_ref, own_ref, core_ref, wo_ref, ctxt_ref, rows_ref, p_ref,
               out_ref, dtab_ref, da_ref, v_scr, kt_scr, ds_scr, dk_scr, dv_scr, near_scr, part_scr, far_acc, self_acc, ctx_scr):
    step = block = pl.program_id(0)
    n_keys = k_ref.shape[0]
    blocks = qb // COORD

    @pl.when(step == 0)
    def _():
        lane = lax.broadcasted_iota(i32, (n_keys, 128), 1)
        level = COORD - 1 - lax.broadcasted_iota(i32, (COORD, n_keys), 0)
        kb = lax.broadcasted_iota(i32, (16, n_keys), 0)
        kp = lax.broadcasted_iota(i32, (16, n_keys), 1)
        for pair in range(n_heads // 2):
            cols = slice(pair * 128, pair * 128 + 128)
            v_scr[pair, :, 0:128] = v_ref[:, cols]
            v_scr[pair, :, 128 : 128 + EXTRA] = jnp.where(lane < 3, -1.0, 0.0).astype(bf16)[:, 0:EXTRA]
            kt_scr[pair, 0:128, :] = k_ref[:, cols].T
            for axis in range(2):
                kt_scr[pair, 128 + 128 * axis : 256 + 128 * axis, :] = (box_rows[axis : axis + 1, :] == level).astype(bf16)
            kt_scr[pair, 384:400, :] = (kp // COORD == kb).astype(bf16)
        dk_scr[...] = jnp.zeros_like(dk_scr)
        dv_scr[...] = jnp.zeros_like(dv_scr)
        near_scr[...] = jnp.zeros_like(near_scr)
        far_acc[...] = jnp.zeros_like(far_acc)
        self_acc[...] = jnp.zeros_like(self_acc)
        for h in range(n_heads):
            ds_scr[h, 0:128, :] = jnp.zeros((128, qb), bf16)
            ds_scr[h, 128 + n_keys :, :] = jnp.zeros((128, qb), bf16)

    rows_q = pl.ds(pl.multiple_of(block * qb, qb), qb)
    lane_half = lax.broadcasted_iota(i32, (qb, 128), 1) >= HEAD
    lower = ids[1] == 0
    da_ref[0 : qb // 2, :] = jnp.where(lower, own_ref[...], core_ref[...])
    da_ref[qb // 2 :, :] = jnp.where(lower, core_ref[...], own_ref[...])
    d_ctx = dot_nt(wo_ref[...], da_ref[...])
    ctx_scr[...] = d_ctx
    prod = d_ctx * ctxt_ref[...]
    scaled = []
    operands = []
    for h in range(n_heads):
        mine = slice(h * HEAD, h * HEAD + HEAD)
        factor = rows_ref[h : h + 1, :]
        delta = jnp.sum(prod[mine, :], axis=0, keepdims=True) * factor
        row = lax.broadcasted_iota(i32, (EXTRA, qb), 0)
        extra = jnp.zeros((EXTRA, qb), f32)
        for piece, value in enumerate(pieces(delta)):
            extra = jnp.where(row == piece, value, extra)
        none = jnp.zeros((HEAD, qb), bf16)
        own = (d_ctx[mine, :] * factor).astype(bf16)
        scaled.append(own)
        operands.append(jnp.concatenate(([own, none] if h % 2 == 0 else [none, own]) + [extra.astype(bf16)], axis=0))
    for h, dat in enumerate(operands):
        for key_at in range(0, n_keys, KEYS):
            dp = dot(v_scr[h // 2, key_at : key_at + KEYS, :], dat)
            p = p_ref[h, key_at : key_at + KEYS, :].astype(f32)
            ds_scr[h, 128 + key_at : 128 + key_at + KEYS, :] = (p * dp).astype(bf16)
    key_block = lax.broadcasted_iota(i32, (8, qb), 0)
    q_block = block * blocks + lax.broadcasted_iota(i32, (8, qb), 1) // COORD

    def of_head(x, h):
        return jnp.where(lane_half, x if h else 0.0, 0.0 if h else x).astype(bf16)

    for pair in range(n_heads // 2):
        dq_halves = []
        for h in (2 * pair, 2 * pair + 1):
            got = dot(kt_scr[pair], ds_scr[h, 128 : 128 + n_keys, :])
            dq_halves.append(got[h % 2 * HEAD : h % 2 * HEAD + HEAD, :])
            part_scr[h, :, rows_q] = got[128:384, :].astype(bf16)
            by_block = got[384:392, :]
            far_acc[h, 0] += jnp.where(key_block + 1 < q_block, by_block, 0.0)
            far_acc[h, 1] += jnp.where(key_block > q_block + 1, by_block, 0.0)
        out_ref[rows_q, 384 * pair : 384 * pair + 128] = jnp.concatenate(dq_halves, axis=0).T.astype(bf16)
        do = jnp.concatenate(scaled[2 * pair : 2 * pair + 2], axis=0).T.astype(f32)
        q = q_ref[:, 128 * pair : 128 * pair + 128].astype(f32)
        dv_scr[pair] += dot(p_ref[2 * pair], of_head(do, 0)) + dot(p_ref[2 * pair + 1], of_head(do, 1))
        ds = [ds_scr[2 * pair + h, 128 : 128 + n_keys, :] for h in range(2)]
        dk_scr[pair] += dot(ds[0], of_head(q, 0)) + dot(ds[1], of_head(q, 1))
    for h in range(n_heads):
        for t in range(blocks):
            rows = pl.ds(pl.multiple_of((block * blocks + t) * COORD, COORD), NEAR)
            near_scr[h] += ds_scr[h, rows, t * 128 : t * 128 + 128].astype(f32)

    some, _ = lone(lens, block, qb)

    @pl.when(some)
    def _():
        d_out = ctx_scr[...]
        product = d_out * ctxt_ref[...]
        for pair in range(n_heads // 2):
            cols = slice(pair * 128, pair * 128 + 128)
            q_t, kt, vt = q_ref[:, cols].T, k_ref[rows_q, cols].T, v_ref[rows_q, cols].T
            add_q, add_k, add_v = [], [], []
            for h in (2 * pair, 2 * pair + 1):
                mine = slice(h % 2 * HEAD, h % 2 * HEAD + HEAD)
                d_own = d_out[h * HEAD : h * HEAD + HEAD, :]
                p = rows_ref[n_heads + h : n_heads + h + 1, :]
                dp = jnp.sum(d_own * vt[mine, :].astype(f32) - product[h * HEAD : h * HEAD + HEAD, :], axis=0, keepdims=True)
                ds = p * dp
                add_q.append(kt[mine, :].astype(f32) * ds)
                add_k.append(q_t[mine, :].astype(f32) * ds)
                add_v.append(d_own * p)
                self_acc[h : h + 1, :] += ds
            at = slice(384 * pair, 384 * pair + 128)
            out_ref[rows_q, at] = (out_ref[rows_q, at].astype(f32) + jnp.concatenate(add_q, axis=0).T).astype(bf16)
            dk_scr[pair, rows_q, :] += jnp.concatenate(add_k, axis=0).T
            dv_scr[pair, rows_q, :] += jnp.concatenate(add_v, axis=0).T

    @pl.when(step == pl.num_programs(0) - 1)
    def _():
        for pair in range(n_heads // 2):
            out_ref[:, 384 * pair + 128 : 384 * pair + 256] = dk_scr[pair].astype(bf16)
            out_ref[:, 384 * pair + 256 : 384 * pair + 384] = dv_scr[pair].astype(bf16)
        offset = 256 - lax.broadcasted_iota(i32, (1, 512), 1)
        row, column = (lax.broadcasted_iota(i32, (NEAR, NEAR), at) for at in (0, 1))
        mirror = (row + column == NEAR - 1).astype(bf16)
        lane = lax.broadcasted_iota(i32, (n_keys, 128), 1)
        hots = [(box_cols[:, axis : axis + 1] == lane).astype(bf16) for axis in range(2)]
        sums = [jnp.zeros((1, 512), f32)] * 16
        for h in range(n_heads):
            high, rest = pieces(near_scr[h])[0:2]
            near = skew_sums(dot_tn(high.astype(bf16), mirror) + dot_tn(rest.astype(bf16), mirror), -128)
            left = jnp.sum(far_acc[h, 0], keepdims=True)
            right = jnp.sum(far_acc[h, 1], keepdims=True)
            alone = jnp.where(offset == 0, jnp.sum(self_acc[h : h + 1, :], keepdims=True), 0.0)
            far = jnp.where(offset == -255, left, 0.0) + jnp.where(offset == 255, right, 0.0)
            sums[h] = near + far + alone
            for axis in range(2):
                pairs = dot(part_scr[h, 128 * axis : 128 * axis + 128, :], hots[axis])
                sums[n_heads * (1 + axis) + h] = skew_sums(pairs.T, 0) + alone
        sums = jnp.concatenate(sums, axis=0)
        dtab_ref[...] = lax.dot_general(offset_hot(-1), sums, (((1,), (1,)), ((), ())), precision=lax.Precision.HIGHEST, preferred_element_type=f32)


def attend_back(ids, q, k, v, d_own, d_core, w_out, ctxt, rows, probs, lengths, box_cols, box_rows):
    n_keys, width = k.shape
    n_heads = width // HEAD
    qb = n_keys // 2
    model = w_out.shape[1]
    n_pairs = n_heads // 2
    at_rows = lambda i, ids, lens: (i, 0)
    at_columns = lambda i, ids, lens: (0, i)
    return pl.pallas_call(
        functools.partial(bwd_kernel, n_heads, qb),
        out_shape=[
            jax.ShapeDtypeStruct((n_keys, 384 * n_pairs), bf16),
            jax.ShapeDtypeStruct((NB, 16), f32),
            jax.ShapeDtypeStruct((n_keys, model), bf16),
        ],
        grid_spec=pltpu.PrefetchScalarGridSpec(
            num_scalar_prefetch=2,
            grid=(2,),
            in_specs=[
                whole(box_cols.shape), whole(box_rows.shape),
                pl.BlockSpec((qb, width), at_rows), whole(k.shape), whole(v.shape),
                *[pl.BlockSpec((qb // 2, model), at_rows)] * 2,
                whole(w_out.shape),
                pl.BlockSpec((width, qb), at_columns),
                pl.BlockSpec((8, qb), at_columns),
                pl.BlockSpec((n_heads, n_keys, qb), lambda i, ids, lens: (0, 0, i)),
            ],
            out_specs=[whole((n_keys, 384 * n_pairs)), whole((NB, 16)), pl.BlockSpec((qb, model), at_rows)],
            scratch_shapes=[
                pltpu.VMEM((n_pairs, n_keys, 128 + EXTRA), bf16),
                pltpu.VMEM((n_pairs, 400, n_keys), bf16),
                pltpu.VMEM((n_heads, n_keys + 256, qb), bf16),
                pltpu.VMEM((n_pairs, n_keys, 128), f32),
                pltpu.VMEM((n_pairs, n_keys, 128), f32),
                pltpu.VMEM((n_heads, NEAR, COORD), f32),
                pltpu.VMEM((n_heads, 256, n_keys), bf16),
                pltpu.VMEM((n_heads, 2, 8, qb), f32),
                pltpu.VMEM((8, qb), f32),
                pltpu.VMEM((width, qb), f32),
            ],
        ),
        compiler_params=params(),
        cost_estimate=estimate(),
        name="attend_back",
    )(ids, lengths, box_cols, box_rows, q, k, v, d_own, d_core, w_out, ctxt, rows, probs)


norm_eps = 1e-06
gelu_scale = 0.7978845608028654
gelu_cube = 0.044715


def scale_of(values):
    return lax.rsqrt(jnp.mean(values * values, axis=-1, keepdims=True) + norm_eps)


def anywhere():
    return pl.BlockSpec(memory_space=pl.ANY)


def estimate():
    return pl.CostEstimate(flops=1_000, bytes_accessed=1_000, transcendentals=0)


def qkv_kernel(ids, xa_ref, xb_ref, g_ref, wq_ref, wk_ref, wv_ref, *refs):
    xo_ref, n_ref, q_ref, k_ref, v_ref = refs[-5:]
    rows = xa_ref.shape[0]
    lower = ids[1] == 0
    xo_ref[0:rows, :] = jnp.where(lower, xa_ref[...], xb_ref[...])
    xo_ref[rows:, :] = jnp.where(lower, xb_ref[...], xa_ref[...])
    x = xo_ref[...].astype(f32)
    normed = (x * scale_of(x) * g_ref[...]).astype(bf16)
    n_ref[...] = normed
    q_ref[...] = dot(normed, wq_ref[...]).astype(bf16)
    k_ref[...] = dot(normed, wk_ref[...]).astype(bf16)
    v_ref[...] = dot(normed, wv_ref[...]).astype(bf16)


def project(ids, far, pair, gain, weights, before, n_blocks):
    rows, model = pair[0].shape
    width = weights[0].shape[1]
    shapes = [jax.ShapeDtypeStruct((n_blocks * rows, n), bf16) for n in (model, model, width, width, width)]
    return pl.pallas_call(
        qkv_kernel,
        out_shape=shapes,
        grid_spec=pltpu.PrefetchScalarGridSpec(
            num_scalar_prefetch=1,
            grid=(1,),
            in_specs=[whole(pair[0].shape)] * 2 + [whole(gain.shape)] + [whole(w.shape) for w in weights] + [anywhere()] * len(before),
            out_specs=[pl.BlockSpec((2 * rows, s.shape[1]), lambda i, ids: (1 - ids[2] if far else ids[2], 0)) for s in shapes],
        ),
        input_output_aliases={7 + i: i for i in range(len(before))},
        compiler_params=params(),
        cost_estimate=estimate(),
        name="project",
    )(ids, *pair, gain, *weights, *before)


def assemble_kernel(ids, *refs):
    for at_step in range(4):

        @pl.when(pl.program_id(0) == at_step)
        def _():
            refs[4][...] = refs[at_step][...]


def assemble(ids, blocks):
    rows, model = blocks[0].shape

    def row(i, ids):
        chip = i // 2
        core = i % 2
        return (2 * ((ids[2] + chip) % 2) + (ids[1] + core) % 2, 0)

    return pl.pallas_call(
        assemble_kernel,
        out_shape=jax.ShapeDtypeStruct((4 * rows, model), bf16),
        grid_spec=pltpu.PrefetchScalarGridSpec(
            num_scalar_prefetch=1,
            grid=(4,),
            in_specs=[whole((rows, model))] * 4,
            out_specs=pl.BlockSpec((rows, model), row),
        ),
        compiler_params=params(),
        cost_estimate=estimate(),
        name="assemble",
    )(ids, *blocks)


def ffn_kernel(ids, a0, a1, a2, a3, b0, b1, b2, b3, x_ref, cot_ref, o0, o1, o2, o3, g_ref, wg_ref, wu_ref, wd_ref,
               mixed_ref, nf_ref, hid_ref, dg_ref, du_ref, dsend, dkeep, rsend, rkeep):
    first = pl.program_id(0) == 0
    mixed = x_ref[...].astype(f32)
    for a, b, o in ((a0, b0, o0), (a1, b1, o1), (a2, b2, o2), (a3, b3, o3)):
        mixed = mixed + dot(jnp.where(first, a[...], b[...]), o[...])
    normed = (mixed * scale_of(mixed) * g_ref[...]).astype(bf16)
    nf_ref[...] = normed
    gate = dot_nt(wg_ref[...], normed)
    up = dot_nt(wu_ref[...], normed)
    d_hidden = dot_nt(wd_ref[...], cot_ref[...])
    square = gate * gate
    t = jnp.tanh(gelu_scale * gate * (1.0 + gelu_cube * square))
    half = 0.5 * (1.0 + t)
    unit = gate * half
    slope = half + 0.5 * gate * (1.0 - t * t) * (gelu_scale * (1.0 + 3.0 * gelu_cube * square))
    hidden = (unit * up).astype(bf16)
    d_gate = (d_hidden * up * slope).astype(bf16)
    d_up = (d_hidden * unit).astype(bf16)
    hid_ref[...] = hidden
    dg_ref[...] = d_gate
    du_ref[...] = d_up
    d_normed = (dot_tn(d_gate, wg_ref[...]) + dot_tn(d_up, wu_ref[...])).astype(bf16)
    down = dot_tn(hidden, wd_ref[...]).astype(bf16)
    rows = mixed.shape[0] // 2
    lower = ids[1] == 0
    for value, other, own in ((d_normed, dsend, dkeep), (down, rsend, rkeep)):
        other[...] = jnp.where(lower, value[rows:], value[:rows])
        own[...] = jnp.where(lower, value[:rows], value[rows:])
    mixed_ref[...] = jnp.where(lower, mixed[:rows], mixed[rows:])


def ffn(ids, contexts, x_all, cot_all, w_outs, gain, w_gate_t, w_up_t, w_down):
    total, model = x_all.shape
    rows = total // 4
    hidden = w_down.shape[0]
    rows_spec = pl.BlockSpec((2 * rows, model), lambda i, ids: (i, 0))
    units_spec = pl.BlockSpec((hidden, 2 * rows), lambda i, ids: (0, i))
    half_spec = pl.BlockSpec((rows, model), lambda i, ids: (i, 0))
    outs = [((2 * rows, model), f32, half_spec), ((total, model), bf16, rows_spec)]
    outs += [((hidden, total), bf16, units_spec)] * 3
    outs += [((2 * rows, model), bf16, half_spec)] * 4
    ins = [(a, whole(a.shape)) for chunk in range(2) for a in contexts[chunk]]
    ins += [(x_all, rows_spec), (cot_all, rows_spec)]
    ins += [(w, whole(w.shape)) for w in (*w_outs, gain, w_gate_t, w_up_t, w_down)]
    return call(ffn_kernel, ids, ins, outs, (2,), "ffn")


def norm_back(total, values, gain):
    r = scale_of(values)
    n = values * r
    e = gain * total
    return r * (e - n * jnp.mean(n * e, axis=-1, keepdims=True)), jnp.sum(total * n, axis=0, keepdims=True)


def mid_kernel(ids, a_ref, b_ref, mixed_ref, cot_ref, g_ref, dm_ref, da_ref, sum_ref):
    total = a_ref[...].astype(f32) + b_ref[...].astype(f32)
    grad, gain_sum = norm_back(total, mixed_ref[...], g_ref[...])
    d_mixed = cot_ref[...].astype(f32) + grad
    dm_ref[...] = d_mixed
    da_ref[...] = d_mixed.astype(bf16)
    step = pl.program_id(0)
    gain_sum = jnp.where(ids[2] == step, gain_sum, 0.0)

    @pl.when(step == 0)
    def _():
        sum_ref[...] = gain_sum

    @pl.when(step > 0)
    def _():
        sum_ref[...] += gain_sum


def mid(ids, own, far, mixed, cot_all, gain):
    total, model = own.shape
    rows = total // 2
    spec = pl.BlockSpec((rows, model), lambda i, ids: (i, 0))
    cot_spec = pl.BlockSpec((rows, model), lambda i, ids: (2 * i + ids[1], 0))
    ins = [(own, spec), (far, spec), (mixed, spec), (cot_all, cot_spec), (gain, whole(gain.shape))]
    outs = [((total, model), f32, spec), ((total, model), bf16, spec), ((1, model), f32, whole((1, model)))]
    return call(mid_kernel, ids, ins, outs, (2,), "mid")


def back_kernel(ids, a_ref, b_ref, wa_ref, wb_ref, *outs):
    total = dot_nt(a_ref[...], wa_ref[...]) + dot_nt(b_ref[...], wb_ref[...])
    rows = total.shape[0] // 2
    first = ids[1] == 0
    other = jnp.where(first, total[rows:], total[:rows]).astype(bf16)
    own = jnp.where(first, total[:rows], total[rows:])
    for at_step in range(2):

        @pl.when(pl.program_id(0) == at_step)
        def _():
            outs[2 * at_step][...] = other
            outs[2 * at_step + 1][...] = own


def project_back(ids, grads, weights):
    total = grads.shape[0]
    rows, (model, width) = total // 4, weights[0].shape
    ins = [(grads, pl.BlockSpec((2 * rows, width), lambda i, ids, at=at: ((1 - i + ids[2]) % 2, at))) for at in range(2)]
    ins += [(w, whole(w.shape)) for w in weights]
    outs = [((rows, model), kind, whole((rows, model))) for kind in (bf16, f32, bf16, f32)]
    return call(back_kernel, ids, ins, outs, (2,), "project_back")


def last_kernel(ids, keep_ref, core_ref, y_ref, x_ref, g_ref, dm_ref, out_ref, sum_ref):
    total = keep_ref[...] + core_ref[...].astype(f32) + y_ref[...].astype(f32)
    grad, gain_sum = norm_back(total, x_ref[...].astype(f32), g_ref[...])
    out_ref[...] = dm_ref[...] + grad
    sum_ref[...] = gain_sum


def last(ids, keep, core, far, x, gain, d_mixed):
    ins = [(a, whole(a.shape)) for a in (keep, core, far, x, gain)]
    ins.append((d_mixed, pl.BlockSpec(keep.shape, lambda i, ids: (ids[2], 0))))
    outs = [(shape, f32, whole(shape)) for shape in (keep.shape, (1, keep.shape[1]))]
    return call(last_kernel, ids, ins, outs, (1,), "last")


def bit_orders(shards):
    bits = list(range(shards.bit_length() - 1))
    return bits, bits[1:] + bits[:1]


def slot_of(flip, order):
    place = 0
    for bit in order[1:]:
        place = 2 * place + (flip >> bit) % 2
    return (flip >> order[0]) % 2, place


def unit_parts_kernel(ids, *refs):
    n = 3
    kept_a, sent_a, kept_b, sent_b = refs[2 * n :]
    step = pl.program_id(0)
    low, high = step % 2, step // 2
    even = ids[3] % 2 == 0
    nears, fars = [], []
    for i in range(n):
        out = dot(refs[i][...], refs[n + i][...]).astype(bf16)
        width, cut = out.shape[1] // 2, out.shape[0] // 2
        first, second = out[:, :width], out[:, width:]
        nears.append(jnp.where(even, first, second))
        fars.append(jnp.where(even, second, first))
        kept_a[2 * low + high, i] = nears[i][:cut]
        sent_a[2 * low + high, i] = fars[i][:cut]

    @pl.when(low == 0)
    def _():
        for i in range(n):
            kept_b[2 * high, i] = nears[i][cut:]
            kept_b[2 * high + 1, i] = fars[i][cut:]

    @pl.when(low == 1)
    def _():
        for i in range(n):
            sent_b[2 * high, i] = nears[i][cut:]
            sent_b[2 * high + 1, i] = fars[i][cut:]


def unit_parts(ids, lefts, rights):
    n = len(lefts)
    total, model = rights[0].shape
    hidden = lefts[0].shape[0]
    shape = (4, n, hidden // 2, model // 8)
    return pl.pallas_call(
        unit_parts_kernel,
        out_shape=[jax.ShapeDtypeStruct(shape, bf16)] * 4,
        grid_spec=pltpu.PrefetchScalarGridSpec(
            num_scalar_prefetch=1,
            grid=(4,),
            in_specs=[whole(a.shape) for a in lefts] + [pl.BlockSpec((total, model // 4), lambda i, ids: (0, i ^ (ids[3] // 2)))] * n,
            out_specs=[whole(shape)] * 4,
        ),
        compiler_params=params(),
        cost_estimate=estimate(),
        name="unit_parts",
    )(ids, *lefts, *rights)


def unit_sums_kernel(n, split, *refs):
    out_ref = refs[-1]
    for i in range(n):
        out = dot(refs[i][...], refs[n + i][...]).astype(bf16)
        width = out.shape[1] // split
        for part in range(split):
            out_ref[part, i] = out[:, part * width : part * width + width]


def unit_sums(lefts, rights, shards):
    n = len(lefts)
    total, model = rights[0].shape
    hidden = lefts[0].shape[0]
    cut = model // shards
    step = 256
    split = step // cut if cut % 128 == 0 else 1
    out = pl.pallas_call(
        functools.partial(unit_sums_kernel, n, split),
        out_shape=jax.ShapeDtypeStruct((model // step * split, n, hidden, step // split), bf16),
        grid=(model // step,),
        in_specs=[whole(a.shape) for a in lefts] + [pl.BlockSpec((total, step), lambda i: (0, i))] * n,
        out_specs=pl.BlockSpec((split, n, hidden, step // split), lambda i: (i, 0, 0, 0)),
        compiler_params=params(),
        cost_estimate=estimate(),
        name="unit_sums",
    )(*lefts, *rights)
    if split == 1:
        out = out.reshape(model // step, n, hidden, step // cut, cut)
        out = out.transpose(0, 3, 1, 2, 4).reshape(shards, n, hidden, cut)
    return out


def head_sums_kernel(shards, ids, normed_ref, da_ref, g_ref, ctx_ref, ka_ref, sa_ref, kb_ref, sb_ref, acc, turned):
    outs = ((ka_ref, sa_ref), (kb_ref, sb_ref))
    cut = acc.shape[0] // shards
    turned[...] = normed_ref[...].T
    acc[:, 0:768] = dot(turned[...], g_ref[...])
    turned[...] = da_ref[...].T
    acc[:, 768:] = dot(turned[...], ctx_ref[...])
    for group, order in enumerate(bit_orders(shards)):
        for flip in range(shards):
            sent, place = slot_of(flip, order)
            at = (ids[3] ^ flip) * cut + group * (cut // 2)
            rows = pl.ds(pl.multiple_of(at, cut // 2), cut // 2)
            outs[group][sent][place] = acc[rows, :].astype(bf16)


def head_sums(ids, normed, d_attn, grads, context, shards):
    total, model = normed.shape
    columns = grads.shape[1] + context.shape[1]
    shape = (shards // 2, model // shards // 2, columns)
    ins = [(a, whole(a.shape)) for a in (normed, d_attn, grads, context)]
    return pl.pallas_call(
        functools.partial(head_sums_kernel, shards),
        out_shape=[jax.ShapeDtypeStruct(shape, bf16)] * 4,
        grid_spec=pltpu.PrefetchScalarGridSpec(
            num_scalar_prefetch=1,
            grid=(1,),
            in_specs=[spec for _, spec in ins],
            out_specs=[whole(shape)] * 4,
            scratch_shapes=[pltpu.VMEM((model, columns), f32), pltpu.VMEM((model, total), bf16)],
        ),
        compiler_params=params(),
        cost_estimate=estimate(),
        name="head_sums",
    )(ids, *(a for a, _ in ins))


def swap(sent, bit, n_dp):
    return lax.ppermute(sent, "dp", [(i, i ^ (1 << bit)) for i in range(n_dp)])


def call(kernel, ids, ins, outs, grid, name):
    return pl.pallas_call(
        kernel,
        out_shape=[jax.ShapeDtypeStruct(shape, kind) for shape, kind, _ in outs],
        grid_spec=pltpu.PrefetchScalarGridSpec(
            num_scalar_prefetch=1,
            grid=grid,
            in_specs=[spec for _, spec in ins],
            out_specs=[spec for _, _, spec in outs],
        ),
        compiler_params=params(),
        cost_estimate=estimate(),
        name=name,
    )(ids, *(array for array, _ in ins))


def out_kernel(ids, ka_ref, ca_ref, kb_ref, cb_ref, send_ref, own_ref):
    sum_a = ka_ref[...].astype(f32) + ca_ref[...].astype(f32)
    sum_b = kb_ref[...].astype(f32) + cb_ref[...].astype(f32)
    first = ids[2] == 0
    send_ref[...] = jnp.where(first, sum_b, sum_a).astype(bf16)
    own_ref[...] = jnp.where(first, sum_a, sum_b)


def out_sums(ids, keep, core):
    rows, model = keep.shape[0] // 2, keep.shape[1]
    low = pl.BlockSpec((rows // 2, model), lambda i, ids: (i, 0))
    high = pl.BlockSpec((rows // 2, model), lambda i, ids: (2 + i, 0))
    ins = [(keep, low), (core, low), (keep, high), (core, high)]
    return call(out_kernel, ids, ins, [((rows, model), bf16, low), ((rows, model), f32, low)], (2,), "out_sums")


def result_kernel(ids, mixed_ref, own_ref, far_ref, out_ref):
    out_ref[...] = mixed_ref[...] + own_ref[...] + far_ref[...].astype(f32)


def result_of(ids, mixed, own, far):
    rows, model = own.shape
    spec = pl.BlockSpec((rows // 2, model), lambda i, ids: (i, 0))
    ins = [(mixed, pl.BlockSpec((rows // 2, model), lambda i, ids: (2 * ids[2] + i, 0))), (own, spec), (far, spec)]
    return call(result_kernel, ids, ins, [(own.shape, f32, spec)], (2,), "result_of")[0]


def onward_kernel(n, ids, *refs):
    for i in range(n):
        low, high, came_low, came_high = refs[4 * i : 4 * i + 4]
        keep, send = refs[4 * n + 2 * i : 4 * n + 2 * i + 2]
        keep[...] = (low[...].astype(f32) + came_low[...].astype(f32)).astype(bf16)
        send[...] = (high[...].astype(f32) + came_high[...].astype(f32)).astype(bf16)


def onward(ids, kept, came):
    ins, outs = [], []
    half = kept[0].shape[0] // 2
    for k, c in zip(kept, came, strict=True):
        block = (1,) + k.shape[1:]
        rest = (0,) * (k.ndim - 1)
        low = pl.BlockSpec(block, lambda i, ids, rest=rest: (i,) + rest)
        high = pl.BlockSpec(block, lambda i, ids, rest=rest: (half + i,) + rest)
        ins += [(k, low), (k, high), (c, low), (c, high)]
        outs += [((half,) + k.shape[1:], bf16, low)] * 2
    got = call(functools.partial(onward_kernel, len(kept)), ids, ins, outs, (half,), "onward")
    return got[0::2], got[1::2]


def unit_last_kernel(ids, ka, ca, kb, cb, *outs):
    cut = ka.shape[2]
    for i, out in enumerate(outs):
        out[0:cut, :] = ka[0, i].astype(f32) + ca[0, i].astype(f32)
        out[cut:, :] = kb[0, i].astype(f32) + cb[0, i].astype(f32)


def unit_last(ids, kept, came):
    _, n, cut, columns = kept[0].shape
    ins = [(a, whole(a.shape)) for a in (kept[0], came[0], kept[1], came[1])]
    outs = [((2 * cut, columns), f32, whole((2 * cut, columns)))] * n
    return call(unit_last_kernel, ids, ins, outs, (1,), "unit_last")


def head_last_kernel(ids, ka, ca, kb, cb, *outs):
    rows = ka.shape[1]
    both = jnp.concatenate([k[0].astype(f32) + c[0].astype(f32) for k, c in ((ka, ca), (kb, cb))], axis=0)
    for i, out in enumerate(outs[:3]):
        out[:, 0:128] = both[:, 128 * i : 128 * i + 128]
        out[:, 128:256] = both[:, 384 + 128 * i : 512 + 128 * i]
    outs[3][...] = both[:, 768:].T


def head_last(ids, kept, came):
    _, rows, columns = kept[0].shape
    ins = [(a, whole(a.shape)) for a in (kept[0], came[0], kept[1], came[1])]
    outs = [((2 * rows, 256), f32, whole((2 * rows, 256)))] * 3 + [((256, 2 * rows), f32, whole((256, 2 * rows)))]
    return call(head_last_kernel, ids, ins, outs, (1,), "head_last")


def local(
    tokens, w_query, w_key, w_value, w_attn_out, w_gate, w_up, w_down, norm_attn, norm_ffn,
    rel_table, x_table, y_table, lengths, boxes, cotangent,
):
    n_mp, n_dp = lax.axis_size("mp"), lax.axis_size("dp")
    me = lax.axis_index("mp")
    core, chip = me % 2, me // 2
    ids = jnp.stack([me, core, chip, lax.axis_index("dp")]).astype(i32)
    rows, model = tokens.shape

    def by_core(a):
        return lax.ppermute(a, "mp", [(i, i ^ 1) for i in range(n_mp)])

    def by_chip(a):
        return lax.ppermute(a, "mp", [(i, i ^ 2) for i in range(n_mp)])

    def together(*arrays):
        return lax.optimization_barrier(arrays)

    def after(a, *earlier):
        return lax.optimization_barrier((a, *earlier))[0]

    def exchange_small(a):
        return lax.all_to_all(a, ("dp", "mp"), split_axis=0, concat_axis=0, tiled=True)

    n_heads = w_query.shape[1] // HEAD
    tables = jnp.concatenate([rel_table.T, x_table.T, y_table.T, jnp.zeros((16 - 3 * n_heads, NB), f32)], axis=0)
    box_cols = boxes.T
    gain_attn, gain_ffn = norm_attn.reshape(1, model), norm_ffn.reshape(1, model)
    weights = (w_query, w_key, w_value)
    w_gate_t, w_up_t = w_gate.T, w_up.T

    x_chip = by_chip(tokens)
    group = project(ids, False, (tokens, by_core(tokens)), gain_attn, weights, [], n_mp)
    w_pairs = [jnp.concatenate([w[:, at : at + 128] for w in weights], axis=1) for at in (0, 128)]
    x_chip, _, box_cols, tables, *w_pairs = together(x_chip, group[0], box_cols, tables, *w_pairs)
    x_both = by_core(x_chip)
    w_chip = by_chip(after(w_attn_out, x_chip))
    c_chip = by_chip(after(cotangent, x_chip))
    group = project(ids, True, (x_chip, x_both), gain_attn, weights, group, n_mp)
    x_all, normed, queries, keys_all, values_all = group

    *kept, own_a = attend(0, queries, keys_all, values_all, tables, lengths, box_cols, boxes, [])
    core_a, far_a = by_core(own_a), by_chip(own_a)
    *kept, own_b = attend(1, after(queries, own_a), keys_all, values_all, tables, lengths, box_cols, boxes, kept)
    context, ctxt, factors, probs = kept
    own_b, core_a, far_a, w_chip, c_chip = together(own_b, core_a, far_a, w_chip, c_chip)
    core_b, far_b = by_core(own_b), by_chip(own_b)
    w_outs = (w_attn_out, by_core(w_attn_out), w_chip, by_core(w_chip))
    cot_all = assemble(ids, (cotangent, by_core(cotangent), c_chip, by_core(c_chip)))
    both_a = by_core(far_a)
    cot_all, far_b = together(cot_all, far_b)
    contexts = ((own_a, core_a, far_a, both_a), (own_b, core_b, far_b, by_core(far_b)))

    out = ffn(ids, contexts, x_all, cot_all, w_outs, gain_ffn, w_gate_t, w_up_t, w_down)
    mixed, normed_ffn, hidden, d_gate, d_up, d_send, d_keep, r_send, r_keep = out
    d_core = by_core(d_send)
    sums = (d_keep.astype(f32) + d_core.astype(f32)).astype(bf16)
    far_sums = by_chip(sums)
    r_core = by_core(after(r_send, sums))

    orders = bit_orders(n_dp)
    pairwise = n_dp == 8 and model == 1024
    unit_args = ((d_gate, d_up, hidden), (normed_ffn, normed_ffn, after(cot_all, sums)))
    if pairwise:
        unit = list(unit_parts(ids, *unit_args))
        r_out, r_own = out_sums(ids, r_keep, r_core)
        unit[0], unit[2], far_sums, r_out = together(unit[0], unit[2], far_sums, r_out)
        unit_came = [swap(unit[2 * i + 1], order[0], n_dp) for i, order in enumerate(orders)]
    else:
        unit = [unit_sums(*unit_args, n_dp)]
        r_out, r_own = out_sums(ids, r_keep, r_core)
        *unit, far_sums, r_out = together(*unit, far_sums, r_out)
        ffn_sums = lax.psum_scatter(unit[0], "dp", scatter_dimension=0, tiled=True)[0].astype(f32)
    d_mixed, d_own, gain_mid = mid(ids, sums, far_sums, mixed, cot_all, gain_ffn)
    d_core = by_core(d_own)

    r_far = by_chip(r_out)
    d_heads, d_tab, d_attn = attend_back(
        ids, queries, keys_all, values_all, d_own, d_core, w_attn_out, ctxt, factors, probs, lengths, box_cols, boxes
    )
    d_heads, r_far = together(d_heads, r_far)

    def swaps(sends, step):
        return [swap(send, order[step], n_dp) for send, order in zip(sends, orders, strict=True)]

    d_first = d_heads
    if pairwise:
        unit_came = together(*unit_came, d_heads)[:2]
        unit_kept, sends = onward(ids, unit[0::2], unit_came)
        unit_came = swaps(sends, 1)
        d_first = after(d_heads, *sends)
    f_send, f_keep, n_send, n_keep = project_back(ids, d_first, w_pairs)
    f_core, n_core = by_core(f_send), by_core(n_send)
    if pairwise:
        attn = head_sums(ids, normed, d_attn, after(d_heads, f_keep), context, n_dp)
        f_core, n_core, *attn = together(f_core, n_core, *attn)
        result = result_of(ids, mixed, r_own, after(r_far, attn[0]))
        *unit_came, result = together(*unit_came, result)
        unit_kept, sends = onward(ids, unit_kept, unit_came)
        unit_came = swaps(sends, 2)
        f_core = after(f_core, *sends)
        came = swaps(attn[1::2], 0)
    f_sum = (f_keep + f_core.astype(f32)).astype(bf16)
    far = by_chip(f_sum)
    if pairwise:
        came[0], came[1], f_sum = together(*came, f_sum)
        kept, sends = onward(ids, attn[0::2], came)
        came = swaps(sends, 1)
        far = after(far, *sends)
    d_tokens, gain_first = last(ids, n_keep, n_core, far, tokens, gain_attn, d_mixed)

    gains = jnp.concatenate([gain_first, gain_mid], axis=0).reshape(2, n_dp, n_mp, -1).transpose(1, 2, 0, 3)
    n_gain = gains.shape[3]
    tabs = d_tab[:, : 3 * n_heads].reshape(n_dp, 1, -1)
    tabs = jnp.where(lax.broadcasted_iota(i32, (1, n_mp, 1), 1) == me, tabs, 0.0)
    small = jnp.concatenate([gains.reshape(n_dp, n_mp, 2 * n_gain), tabs], axis=2).reshape(n_dp * n_mp, -1)
    if pairwise:
        small = exchange_small(small)
        kept, sends = onward(ids, kept, came)
        came = swaps(sends, 2)
        small = after(small, *sends).sum(axis=0)
        unit_came[0] = after(unit_came[0], small)
        ffn_sums = unit_last(ids, unit_kept, unit_came)
        came[0], came[1], *ffn_sums = together(*came, *ffn_sums)
        attn_sums = head_last(ids, kept, came)
    else:
        result = result_of(ids, mixed, r_own, r_far)
        wide = dot_tn(normed, d_heads)
        parts = [wide[:, 384 * pair + 128 * i : 384 * pair + 128 * i + 128] for i in range(3) for pair in range(2)]
        wide = [*parts, dot_tn(d_attn, context)]
        wide = jnp.concatenate(wide, axis=1).astype(bf16)
        wide = lax.psum_scatter(wide, "dp", scatter_dimension=0, tiled=True).astype(f32)
        attn_sums = [wide[:, 256 * i : 256 * i + 256] for i in range(4)]
        attn_sums[3] = attn_sums[3].T
        small = exchange_small(small).sum(axis=0)
    tabs = small[2 * n_gain :].reshape(-1, 3, n_heads)
    return (
        result, d_tokens,
        *attn_sums,
        ffn_sums[0].T, ffn_sums[1].T, ffn_sums[2],
        small[:n_gain], small[n_gain : 2 * n_gain], tabs[:, 0], tabs[:, 1], tabs[:, 2],
    )


def solution(mesh):
    in_specs = (
        P(("dp", "mp"), None),
        P(None, "mp"),
        P(None, "mp"),
        P(None, "mp"),
        P("mp", None),
        P(None, "mp"),
        P(None, "mp"),
        P("mp", None),
        P(),
        P(),
        P(None, "mp"),
        P(None, "mp"),
        P(None, "mp"),
        P("dp", None),
        P(None, "dp"),
        P(("dp", "mp"), None),
    )
    out_specs = (
        P(("dp", "mp"), None),
        P(("dp", "mp"), None),
        P("dp", "mp"),
        P("dp", "mp"),
        P("dp", "mp"),
        P("mp", "dp"),
        P("dp", "mp"),
        P("dp", "mp"),
        P("mp", "dp"),
        P(("dp", "mp")),
        P(("dp", "mp")),
        P("dp", "mp"),
        P("dp", "mp"),
        P("dp", "mp"),
    )
    return jax.shard_map(local, mesh=mesh, in_specs=in_specs, out_specs=out_specs, check_vma=False)
```

```python
import functools

import jax
import jax.numpy as jnp
from jax import lax
from jax.experimental import pallas as pl
from jax.experimental.pallas import tpu as pltpu
from jax.sharding import PartitionSpec as P

f32, bf16, i32 = jnp.float32, jnp.bfloat16, jnp.int32
HEAD = 64
NB = 32
COORD = 128
SHORT = 512
NEAR = 3 * COORD
EXTRA = 16
KEYS = 512
thresholds = (1, 2, 3, 4, 5, 6, 7, 8, 12, 16, 23, 32, 46, 64, 91)
masked_score = -1000000000.0


def dot(a, b):
    return jnp.dot(a, b, preferred_element_type=f32)


def dot_nt(a, b):
    return lax.dot_general(a, b, (((1,), (1,)), ((), ())), preferred_element_type=f32)


def dot_tn(a, b):
    return lax.dot_general(a, b, (((0,), (0,)), ((), ())), preferred_element_type=f32)


def bucket_of(offsets):
    distance = jnp.abs(offsets)
    bucket_ids = jnp.where(offsets > 0, NB // 2, 0)
    for threshold in thresholds:
        bucket_ids = bucket_ids + jnp.where(distance >= threshold, 1, 0)
    return bucket_ids


def offset_hot(sign=1):
    offsets = sign * (lax.broadcasted_iota(i32, (NB, 512), 1) - 256)
    return (bucket_of(offsets) == lax.broadcasted_iota(i32, (NB, 512), 0)).astype(f32)


def toeplitz(row, base):
    wide = jnp.broadcast_to(row, (COORD, 512))
    return pltpu.roll(wide, (256 - base) % 512, 1, stride=1, stride_axis=0)


def start_of(len0, len1):
    return jnp.where(len1 > 0, 1, 0), jnp.where(len1 > 0, len1, len0)


def build(lens, tab_ref, box_cols, box_rows, k_ref, b_scr, hot_scr, lut_scr, strip_scr, n_heads):
    n_keys = k_ref.shape[0]
    len0, len1 = lens[0, 0], lens[0, 1]
    start1, start1_len = start_of(len0, len1)
    lane = lax.broadcasted_iota(i32, (n_keys, COORD), 1)
    pos = lax.broadcasted_iota(i32, (n_keys, COORD), 0)
    x_hot = (box_cols[:, 0:1] == lane).astype(bf16)
    y_hot = (box_cols[:, 1:2] == lane).astype(bf16)
    second = pos >= SHORT
    start_k = jnp.where(second, start1, 0)
    limit = jnp.where(second, start1_len, len0)
    valid = pos - start_k * SHORT < limit
    masked0 = jnp.where(valid & (start_k == 0), 0.0, masked_score)
    masked1 = jnp.where(valid & (start_k == start1), 0.0, masked_score)
    extra = jnp.where(lane == 0, masked0, jnp.where(lane == 1, masked1, 0.0))
    extra = extra.astype(bf16)[:, 0:EXTRA]
    for pair in range(n_heads // 2):
        b_scr[pair, :, 0:128] = k_ref[:, pair * 128 : pair * 128 + 128]
        b_scr[pair, :, 128:256] = x_hot
        b_scr[pair, :, 256:384] = y_hot
        b_scr[pair, :, 384 : 384 + EXTRA] = extra
    level = lax.broadcasted_iota(i32, (COORD, n_keys), 0)
    hot_scr[0:128, :] = (box_rows[0:1, :] == level).astype(bf16)
    hot_scr[128:256, :] = (box_rows[1:2, :] == level).astype(bf16)
    vec = jnp.dot(tab_ref[...], offset_hot(), precision=lax.Precision.HIGHEST, preferred_element_type=f32)
    n_strip = strip_scr.shape[1]
    for h in range(n_heads):
        for axis in range(2):
            at = n_heads * (1 + axis) + h
            table = toeplitz(vec[at : at + 1, :], 0)[:, 0:128]
            lut_scr[h, axis] = table.T.astype(bf16)
        row = vec[h : h + 1, :]
        near = toeplitz(row, -128)[:, 0:NEAR]
        mid = (n_strip - NEAR) // 2
        left = jnp.broadcast_to(row[:, 0:1], (mid, COORD))
        right = jnp.broadcast_to(row[:, 511:512], (mid, COORD))
        strip_scr[h, 0:mid, :] = left
        strip_scr[h, mid : mid + NEAR, :] = near.T
        strip_scr[h, mid + NEAR :, :] = right


def query_side(lens, block, qb, h, qt, hot_q, lut_scr):
    half = jnp.zeros((HEAD, qb), bf16)
    own = qt[(h % 2) * HEAD : (h % 2) * HEAD + HEAD, :]
    parts = [own, half] if h % 2 == 0 else [half, own]
    x_rows = dot(lut_scr[h, 0], hot_q[0:128, :]).astype(bf16)
    y_rows = dot(lut_scr[h, 1], hot_q[128:256, :]).astype(bf16)
    row = lax.broadcasted_iota(i32, (EXTRA, qb), 0)
    q_pos = block * qb + lax.broadcasted_iota(i32, (EXTRA, qb), 1)
    extra = jnp.where(row == jnp.where(q_pos >= SHORT, 1, 0), 1.0, 0.0)
    return jnp.concatenate(parts + [x_rows, y_rows, extra.astype(bf16)], axis=0)


def pieces(value):
    high = value.astype(bf16).astype(f32)
    rest = value - high
    mid = rest.astype(bf16).astype(f32)
    return high, mid, (rest - mid).astype(bf16).astype(f32)


def scores(block, qb, h, at, b_scr, strip_scr, key_at):
    s = dot(b_scr[h // 2, key_at : key_at + KEYS, :], at)
    blocks = qb // COORD
    top = b_scr.shape[1] // COORD - 1
    parts = []
    for t in range(blocks):
        off = pl.multiple_of((top - (block * blocks + t)) * COORD + key_at, COORD)
        parts.append(s[:, t * 128 : t * 128 + 128] + strip_scr[h, pl.ds(off, KEYS), :])
    return jnp.concatenate(parts, axis=1)


def lone(lens, block, qb):
    len0, len1 = lens[0, 0], lens[0, 1]
    start1, start1_len = start_of(len0, len1)
    in_second = block * qb >= SHORT
    begin = jnp.where(in_second, start1, 0) * SHORT
    limit = jnp.where(in_second, start1_len, len0)
    pos = block * qb + lax.broadcasted_iota(i32, (1, qb), 1) - begin
    return block * qb + qb - 1 - begin >= limit, pos >= limit


def own_score(h, qt, kt, strip_scr, lut_scr):
    mine = slice((h % 2) * HEAD, (h % 2) * HEAD + HEAD)
    product = qt[mine, :].astype(f32) * kt[mine, :].astype(f32)
    centre = (strip_scr.shape[1] - COORD) // 2
    bias = strip_scr[h, centre : centre + 1, 0:1] + lut_scr[h, 0, 0:1, 0:1].astype(f32) + lut_scr[h, 1, 0:1, 0:1].astype(f32)
    return jnp.sum(product, axis=0, keepdims=True) + bias


def fwd_kernel(n_heads, qb, base, lens, tab_ref, box_cols, box_rows, q_ref, k_ref, v_ref, *refs):
    ctx_ref, ctxt_ref, rows_ref, p_ref, out_ref, b_scr, hot_scr, lut_scr, strip_scr, vt_scr, s_scr, top_scr, log_scr = refs[-13:]
    n_keys = k_ref.shape[0]
    block = pl.program_id(0) + base

    @pl.when(pl.program_id(0) == 0)
    def _():
        build(lens, tab_ref, box_cols, box_rows, k_ref, b_scr, hot_scr, lut_scr, strip_scr, n_heads)
        for pair in range(n_heads // 2):
            vt_scr[pair, 0:128, :] = v_ref[:, pair * 128 : pair * 128 + 128].T
            vt_scr[pair, 128:144, :] = jnp.ones((16, n_keys), bf16)

    hot_q = hot_scr[:, pl.ds(pl.multiple_of(block * qb, qb), qb)]
    for pair in range(n_heads // 2):
        qt = q_ref[:, pair * 128 : pair * 128 + 128].T
        halves = []
        for h in (2 * pair, 2 * pair + 1):
            at = query_side(lens, block, qb, h, qt, hot_q, lut_scr)
            top = None
            for key_at in range(0, n_keys, KEYS):
                s = scores(block, qb, h, at, b_scr, strip_scr, key_at)
                s_scr[h % 2, key_at : key_at + KEYS, :] = s
                high = jnp.max(s, axis=0, keepdims=True)
                top = high if top is None else jnp.maximum(top, high)
            out = None
            for key_at in range(0, n_keys, KEYS):
                p = jnp.exp(s_scr[h % 2, key_at : key_at + KEYS, :] - top).astype(bf16)
                p_ref[h, key_at : key_at + KEYS, :] = p
                part = dot(vt_scr[pair, :, key_at : key_at + KEYS], p)
                out = part if out is None else out + part
            total = out[128:129, :]
            factor = 1.0 / total
            halves.append(out[(h % 2) * HEAD : (h % 2) * HEAD + HEAD, :] * factor)
            rows_ref[h : h + 1, :] = factor
            rows_ref[n_heads + h : n_heads + h + 1, :] = jnp.zeros((1, qb), f32)
            top_scr[h : h + 1, :] = top
            log_scr[h : h + 1, :] = top + jnp.log(total)
        ctxt = jnp.concatenate(halves, axis=0)
        ctxt_ref[pair * 128 : pair * 128 + 128, :] = ctxt
        ctx_ref[:, pair * 128 : pair * 128 + 128] = ctxt.T.astype(bf16)
    some, which = lone(lens, block, qb)

    @pl.when(some)
    def _():
        rows_q = pl.ds(pl.multiple_of(block * qb, qb), qb)
        for pair in range(n_heads // 2):
            cols = slice(pair * 128, pair * 128 + 128)
            qt, kt = q_ref[:, cols].T, k_ref[rows_q, cols].T
            for h in (2 * pair, 2 * pair + 1):
                own = own_score(h, qt, kt, strip_scr, lut_scr)
                log = log_scr[h : h + 1, :]
                high = jnp.maximum(own, log)
                new = high + jnp.log(jnp.exp(own - high) + jnp.exp(log - high))
                mine = slice(h * HEAD, h * HEAD + HEAD)
                value = vt_scr[pair, (h % 2) * HEAD : (h % 2) * HEAD + HEAD, rows_q].astype(f32)
                old = ctxt_ref[mine, :]
                alone = jnp.exp(own - new)
                ctxt_ref[mine, :] = jnp.where(which, old * jnp.exp(log - new) + value * alone, old)
                factor = rows_ref[h : h + 1, :]
                rows_ref[h : h + 1, :] = jnp.where(which, jnp.exp(top_scr[h : h + 1, :] - new), factor)
                rows_ref[n_heads + h : n_heads + h + 1, :] = jnp.where(which, alone, 0.0)
            ctx_ref[:, cols] = ctxt_ref[cols, :].T.astype(bf16)

    out_ref[...] = ctx_ref[...]


def scratch(n_keys, n_heads):
    return [
        pltpu.VMEM((n_heads // 2, n_keys, 384 + EXTRA), bf16),
        pltpu.VMEM((256, n_keys), bf16),
        pltpu.VMEM((n_heads, 2, COORD, COORD), bf16),
        pltpu.VMEM((n_heads, 2 * n_keys - COORD, COORD), f32),
    ]


def whole(shape):
    return pl.BlockSpec(shape, lambda *at: (0,) * len(shape))


def params():
    return pltpu.CompilerParams(dimension_semantics=("arbitrary",), vmem_limit_bytes=255 << 18)


def attend(chunk, q, k, v, tables, lengths, box_cols, box_rows, before):
    n_keys, width = k.shape
    qb = n_keys // 4
    n_heads = width // HEAD
    return pl.pallas_call(
        functools.partial(fwd_kernel, n_heads, qb, 2 * chunk),
        out_shape=(
            jax.ShapeDtypeStruct((n_keys, width), bf16),
            jax.ShapeDtypeStruct((width, n_keys), f32),
            jax.ShapeDtypeStruct((8, n_keys), f32),
            jax.ShapeDtypeStruct((n_heads, n_keys, n_keys), bf16),
            jax.ShapeDtypeStruct((2 * qb, width), bf16),
        ),
        grid=(2,),
        in_specs=[
            pl.BlockSpec(memory_space=pltpu.SMEM),
            whole(tables.shape), whole(box_cols.shape), whole(box_rows.shape),
            pl.BlockSpec((qb, width), lambda i: (i + 2 * chunk, 0)), whole(k.shape), whole(v.shape),
        ] + [anywhere()] * len(before),
        out_specs=(
            pl.BlockSpec((qb, width), lambda i: (i + 2 * chunk, 0)),
            pl.BlockSpec((width, qb), lambda i: (0, i + 2 * chunk)),
            pl.BlockSpec((8, qb), lambda i: (0, i + 2 * chunk)),
            pl.BlockSpec((n_heads, n_keys, qb), lambda i: (0, 0, i + 2 * chunk)),
            pl.BlockSpec((qb, width), lambda i: (i, 0)),
        ),
        scratch_shapes=scratch(n_keys, n_heads) + [
            pltpu.VMEM((n_heads // 2, 144, n_keys), bf16),
            pltpu.VMEM((2, n_keys, qb), f32),
            pltpu.VMEM((8, qb), f32),
            pltpu.VMEM((8, qb), f32),
        ],
        input_output_aliases={7 + i: i for i in range(len(before))},
        compiler_params=params(),
        cost_estimate=estimate(),
        name="attend",
    )(lengths, tables, box_cols, box_rows, q, k, v, *before)


def skew_sums(tile, base):
    width = tile.shape[1]
    wide = jnp.concatenate([tile, jnp.zeros((128, 512 - width), f32)], axis=1)
    wide = pltpu.roll(wide, (257 - width - base) % 512, 1, stride=1, stride_axis=0)
    return jnp.sum(wide, axis=0, keepdims=True)


def bwd_kernel(n_heads, qb, ids, lens, box_cols, box_rows, q_ref, k_ref, v_ref, own_ref, core_ref, wo_ref, ctxt_ref, rows_ref, p_ref,
               out_ref, dtab_ref, da_ref, v_scr, kt_scr, ds_scr, dk_scr, dv_scr, near_scr, part_scr, far_acc, self_acc, ctx_scr):
    step = block = pl.program_id(0)
    n_keys = k_ref.shape[0]
    blocks = qb // COORD

    @pl.when(step == 0)
    def _():
        lane = lax.broadcasted_iota(i32, (n_keys, 128), 1)
        level = COORD - 1 - lax.broadcasted_iota(i32, (COORD, n_keys), 0)
        kb = lax.broadcasted_iota(i32, (16, n_keys), 0)
        kp = lax.broadcasted_iota(i32, (16, n_keys), 1)
        for pair in range(n_heads // 2):
            cols = slice(pair * 128, pair * 128 + 128)
            v_scr[pair, :, 0:128] = v_ref[:, cols]
            v_scr[pair, :, 128 : 128 + EXTRA] = jnp.where(lane < 3, -1.0, 0.0).astype(bf16)[:, 0:EXTRA]
            kt_scr[pair, 0:128, :] = k_ref[:, cols].T
            for axis in range(2):
                kt_scr[pair, 128 + 128 * axis : 256 + 128 * axis, :] = (box_rows[axis : axis + 1, :] == level).astype(bf16)
            kt_scr[pair, 384:400, :] = (kp // COORD == kb).astype(bf16)
        dk_scr[...] = jnp.zeros_like(dk_scr)
        dv_scr[...] = jnp.zeros_like(dv_scr)
        near_scr[...] = jnp.zeros_like(near_scr)
        far_acc[...] = jnp.zeros_like(far_acc)
        self_acc[...] = jnp.zeros_like(self_acc)
        for h in range(n_heads):
            ds_scr[h, 0:128, :] = jnp.zeros((128, qb), bf16)
            ds_scr[h, 128 + n_keys :, :] = jnp.zeros((128, qb), bf16)

    rows_q = pl.ds(pl.multiple_of(block * qb, qb), qb)
    lane_half = lax.broadcasted_iota(i32, (qb, 128), 1) >= HEAD
    lower = ids[1] == 0
    da_ref[0 : qb // 2, :] = jnp.where(lower, own_ref[...], core_ref[...])
    da_ref[qb // 2 :, :] = jnp.where(lower, core_ref[...], own_ref[...])
    d_ctx = dot_nt(wo_ref[...], da_ref[...])
    ctx_scr[...] = d_ctx
    prod = d_ctx * ctxt_ref[...]
    scaled = []
    operands = []
    for h in range(n_heads):
        mine = slice(h * HEAD, h * HEAD + HEAD)
        factor = rows_ref[h : h + 1, :]
        delta = jnp.sum(prod[mine, :], axis=0, keepdims=True) * factor
        row = lax.broadcasted_iota(i32, (EXTRA, qb), 0)
        extra = jnp.zeros((EXTRA, qb), f32)
        for piece, value in enumerate(pieces(delta)):
            extra = jnp.where(row == piece, value, extra)
        none = jnp.zeros((HEAD, qb), bf16)
        own = (d_ctx[mine, :] * factor).astype(bf16)
        scaled.append(own)
        operands.append(jnp.concatenate(([own, none] if h % 2 == 0 else [none, own]) + [extra.astype(bf16)], axis=0))
    for h, dat in enumerate(operands):
        for key_at in range(0, n_keys, KEYS):
            dp = dot(v_scr[h // 2, key_at : key_at + KEYS, :], dat)
            p = p_ref[h, key_at : key_at + KEYS, :].astype(f32)
            ds_scr[h, 128 + key_at : 128 + key_at + KEYS, :] = (p * dp).astype(bf16)
    key_block = lax.broadcasted_iota(i32, (8, qb), 0)
    q_block = block * blocks + lax.broadcasted_iota(i32, (8, qb), 1) // COORD

    def of_head(x, h):
        return jnp.where(lane_half, x if h else 0.0, 0.0 if h else x).astype(bf16)

    for pair in range(n_heads // 2):
        dq_halves = []
        for h in (2 * pair, 2 * pair + 1):
            got = dot(kt_scr[pair], ds_scr[h, 128 : 128 + n_keys, :])
            dq_halves.append(got[h % 2 * HEAD : h % 2 * HEAD + HEAD, :])
            part_scr[h, :, rows_q] = got[128:384, :].astype(bf16)
            by_block = got[384:392, :]
            far_acc[h, 0] += jnp.where(key_block + 1 < q_block, by_block, 0.0)
            far_acc[h, 1] += jnp.where(key_block > q_block + 1, by_block, 0.0)
        out_ref[rows_q, 384 * pair : 384 * pair + 128] = jnp.concatenate(dq_halves, axis=0).T.astype(bf16)
        do = jnp.concatenate(scaled[2 * pair : 2 * pair + 2], axis=0).T.astype(f32)
        q = q_ref[:, 128 * pair : 128 * pair + 128].astype(f32)
        dv_scr[pair] += dot(p_ref[2 * pair], of_head(do, 0)) + dot(p_ref[2 * pair + 1], of_head(do, 1))
        ds = [ds_scr[2 * pair + h, 128 : 128 + n_keys, :] for h in range(2)]
        dk_scr[pair] += dot(ds[0], of_head(q, 0)) + dot(ds[1], of_head(q, 1))
    for h in range(n_heads):
        for t in range(blocks):
            rows = pl.ds(pl.multiple_of((block * blocks + t) * COORD, COORD), NEAR)
            near_scr[h] += ds_scr[h, rows, t * 128 : t * 128 + 128].astype(f32)

    some, _ = lone(lens, block, qb)

    @pl.when(some)
    def _():
        d_out = ctx_scr[...]
        product = d_out * ctxt_ref[...]
        for pair in range(n_heads // 2):
            cols = slice(pair * 128, pair * 128 + 128)
            q_t, kt, vt = q_ref[:, cols].T, k_ref[rows_q, cols].T, v_ref[rows_q, cols].T
            add_q, add_k, add_v = [], [], []
            for h in (2 * pair, 2 * pair + 1):
                mine = slice(h % 2 * HEAD, h % 2 * HEAD + HEAD)
                d_own = d_out[h * HEAD : h * HEAD + HEAD, :]
                p = rows_ref[n_heads + h : n_heads + h + 1, :]
                dp = jnp.sum(d_own * vt[mine, :].astype(f32) - product[h * HEAD : h * HEAD + HEAD, :], axis=0, keepdims=True)
                ds = p * dp
                add_q.append(kt[mine, :].astype(f32) * ds)
                add_k.append(q_t[mine, :].astype(f32) * ds)
                add_v.append(d_own * p)
                self_acc[h : h + 1, :] += ds
            at = slice(384 * pair, 384 * pair + 128)
            out_ref[rows_q, at] = (out_ref[rows_q, at].astype(f32) + jnp.concatenate(add_q, axis=0).T).astype(bf16)
            dk_scr[pair, rows_q, :] += jnp.concatenate(add_k, axis=0).T
            dv_scr[pair, rows_q, :] += jnp.concatenate(add_v, axis=0).T

    @pl.when(step == pl.num_programs(0) - 1)
    def _():
        for pair in range(n_heads // 2):
            out_ref[:, 384 * pair + 128 : 384 * pair + 256] = dk_scr[pair].astype(bf16)
            out_ref[:, 384 * pair + 256 : 384 * pair + 384] = dv_scr[pair].astype(bf16)
        offset = 256 - lax.broadcasted_iota(i32, (1, 512), 1)
        row, column = (lax.broadcasted_iota(i32, (NEAR, NEAR), at) for at in (0, 1))
        mirror = (row + column == NEAR - 1).astype(bf16)
        lane = lax.broadcasted_iota(i32, (n_keys, 128), 1)
        hots = [(box_cols[:, axis : axis + 1] == lane).astype(bf16) for axis in range(2)]
        sums = [jnp.zeros((1, 512), f32)] * 16
        for h in range(n_heads):
            high, rest = pieces(near_scr[h])[0:2]
            near = skew_sums(dot_tn(high.astype(bf16), mirror) + dot_tn(rest.astype(bf16), mirror), -128)
            left = jnp.sum(far_acc[h, 0], keepdims=True)
            right = jnp.sum(far_acc[h, 1], keepdims=True)
            alone = jnp.where(offset == 0, jnp.sum(self_acc[h : h + 1, :], keepdims=True), 0.0)
            far = jnp.where(offset == -255, left, 0.0) + jnp.where(offset == 255, right, 0.0)
            sums[h] = near + far + alone
            for axis in range(2):
                pairs = dot(part_scr[h, 128 * axis : 128 * axis + 128, :], hots[axis])
                sums[n_heads * (1 + axis) + h] = skew_sums(pairs.T, 0) + alone
        sums = jnp.concatenate(sums, axis=0)
        dtab_ref[...] = lax.dot_general(offset_hot(-1), sums, (((1,), (1,)), ((), ())), precision=lax.Precision.HIGHEST, preferred_element_type=f32)


def attend_back(ids, q, k, v, d_own, d_core, w_out, ctxt, rows, probs, lengths, box_cols, box_rows):
    n_keys, width = k.shape
    n_heads = width // HEAD
    qb = n_keys // 2
    model = w_out.shape[1]
    n_pairs = n_heads // 2
    at_rows = lambda i, ids, lens: (i, 0)
    at_columns = lambda i, ids, lens: (0, i)
    return pl.pallas_call(
        functools.partial(bwd_kernel, n_heads, qb),
        out_shape=[
            jax.ShapeDtypeStruct((n_keys, 384 * n_pairs), bf16),
            jax.ShapeDtypeStruct((NB, 16), f32),
            jax.ShapeDtypeStruct((n_keys, model), bf16),
        ],
        grid_spec=pltpu.PrefetchScalarGridSpec(
            num_scalar_prefetch=2,
            grid=(2,),
            in_specs=[
                whole(box_cols.shape), whole(box_rows.shape),
                pl.BlockSpec((qb, width), at_rows), whole(k.shape), whole(v.shape),
                *[pl.BlockSpec((qb // 2, model), at_rows)] * 2,
                whole(w_out.shape),
                pl.BlockSpec((width, qb), at_columns),
                pl.BlockSpec((8, qb), at_columns),
                pl.BlockSpec((n_heads, n_keys, qb), lambda i, ids, lens: (0, 0, i)),
            ],
            out_specs=[whole((n_keys, 384 * n_pairs)), whole((NB, 16)), pl.BlockSpec((qb, model), at_rows)],
            scratch_shapes=[
                pltpu.VMEM((n_pairs, n_keys, 128 + EXTRA), bf16),
                pltpu.VMEM((n_pairs, 400, n_keys), bf16),
                pltpu.VMEM((n_heads, n_keys + 256, qb), bf16),
                pltpu.VMEM((n_pairs, n_keys, 128), f32),
                pltpu.VMEM((n_pairs, n_keys, 128), f32),
                pltpu.VMEM((n_heads, NEAR, COORD), f32),
                pltpu.VMEM((n_heads, 256, n_keys), bf16),
                pltpu.VMEM((n_heads, 2, 8, qb), f32),
                pltpu.VMEM((8, qb), f32),
                pltpu.VMEM((width, qb), f32),
            ],
        ),
        compiler_params=params(),
        cost_estimate=estimate(),
        name="attend_back",
    )(ids, lengths, box_cols, box_rows, q, k, v, d_own, d_core, w_out, ctxt, rows, probs)


norm_eps = 1e-06
gelu_scale = 0.7978845608028654
gelu_cube = 0.044715


def scale_of(values):
    return lax.rsqrt(jnp.mean(values * values, axis=-1, keepdims=True) + norm_eps)


def anywhere():
    return pl.BlockSpec(memory_space=pl.ANY)


def estimate():
    return pl.CostEstimate(flops=1_000, bytes_accessed=1_000, transcendentals=0)


def qkv_kernel(ids, xa_ref, xb_ref, g_ref, wq_ref, wk_ref, wv_ref, *refs):
    xo_ref, n_ref, q_ref, k_ref, v_ref = refs[-5:]
    rows = xa_ref.shape[0]
    lower = ids[1] == 0
    xo_ref[0:rows, :] = jnp.where(lower, xa_ref[...], xb_ref[...])
    xo_ref[rows:, :] = jnp.where(lower, xb_ref[...], xa_ref[...])
    x = xo_ref[...].astype(f32)
    normed = (x * scale_of(x) * g_ref[...]).astype(bf16)
    n_ref[...] = normed
    q_ref[...] = dot(normed, wq_ref[...]).astype(bf16)
    k_ref[...] = dot(normed, wk_ref[...]).astype(bf16)
    v_ref[...] = dot(normed, wv_ref[...]).astype(bf16)


def project(ids, far, pair, gain, weights, before, n_blocks):
    rows, model = pair[0].shape
    width = weights[0].shape[1]
    shapes = [jax.ShapeDtypeStruct((n_blocks * rows, n), bf16) for n in (model, model, width, width, width)]
    return pl.pallas_call(
        qkv_kernel,
        out_shape=shapes,
        grid_spec=pltpu.PrefetchScalarGridSpec(
            num_scalar_prefetch=1,
            grid=(1,),
            in_specs=[whole(pair[0].shape)] * 2 + [whole(gain.shape)] + [whole(w.shape) for w in weights] + [anywhere()] * len(before),
            out_specs=[pl.BlockSpec((2 * rows, s.shape[1]), lambda i, ids: (1 - ids[2] if far else ids[2], 0)) for s in shapes],
        ),
        input_output_aliases={7 + i: i for i in range(len(before))},
        compiler_params=params(),
        cost_estimate=estimate(),
        name="project",
    )(ids, *pair, gain, *weights, *before)


def assemble_kernel(ids, *refs):
    for at_step in range(4):

        @pl.when(pl.program_id(0) == at_step)
        def _():
            refs[4][...] = refs[at_step][...]


def assemble(ids, blocks):
    rows, model = blocks[0].shape

    def row(i, ids):
        chip = i // 2
        core = i % 2
        return (2 * ((ids[2] + chip) % 2) + (ids[1] + core) % 2, 0)

    return pl.pallas_call(
        assemble_kernel,
        out_shape=jax.ShapeDtypeStruct((4 * rows, model), bf16),
        grid_spec=pltpu.PrefetchScalarGridSpec(
            num_scalar_prefetch=1,
            grid=(4,),
            in_specs=[whole((rows, model))] * 4,
            out_specs=pl.BlockSpec((rows, model), row),
        ),
        compiler_params=params(),
        cost_estimate=estimate(),
        name="assemble",
    )(ids, *blocks)


def ffn_kernel(ids, a0, a1, a2, a3, b0, b1, b2, b3, x_ref, cot_ref, o0, o1, o2, o3, g_ref, wg_ref, wu_ref, wd_ref,
               mixed_ref, nf_ref, hid_ref, dg_ref, du_ref, dsend, dkeep, rsend, rkeep):
    first = pl.program_id(0) == 0
    mixed = x_ref[...].astype(f32)
    for a, b, o in ((a0, b0, o0), (a1, b1, o1), (a2, b2, o2), (a3, b3, o3)):
        mixed = mixed + dot(jnp.where(first, a[...], b[...]), o[...])
    normed = (mixed * scale_of(mixed) * g_ref[...]).astype(bf16)
    nf_ref[...] = normed
    gate = dot_nt(wg_ref[...], normed)
    up = dot_nt(wu_ref[...], normed)
    d_hidden = dot_nt(wd_ref[...], cot_ref[...])
    square = gate * gate
    t = jnp.tanh(gelu_scale * gate * (1.0 + gelu_cube * square))
    half = 0.5 * (1.0 + t)
    unit = gate * half
    slope = half + 0.5 * gate * (1.0 - t * t) * (gelu_scale * (1.0 + 3.0 * gelu_cube * square))
    hidden = (unit * up).astype(bf16)
    d_gate = (d_hidden * up * slope).astype(bf16)
    d_up = (d_hidden * unit).astype(bf16)
    hid_ref[...] = hidden
    dg_ref[...] = d_gate
    du_ref[...] = d_up
    d_normed = (dot_tn(d_gate, wg_ref[...]) + dot_tn(d_up, wu_ref[...])).astype(bf16)
    down = dot_tn(hidden, wd_ref[...]).astype(bf16)
    rows = mixed.shape[0] // 2
    lower = ids[1] == 0
    for value, other, own in ((d_normed, dsend, dkeep), (down, rsend, rkeep)):
        other[...] = jnp.where(lower, value[rows:], value[:rows])
        own[...] = jnp.where(lower, value[:rows], value[rows:])
    mixed_ref[...] = jnp.where(lower, mixed[:rows], mixed[rows:])


def ffn(ids, contexts, x_all, cot_all, w_outs, gain, w_gate_t, w_up_t, w_down):
    total, model = x_all.shape
    rows = total // 4
    hidden = w_down.shape[0]
    rows_spec = pl.BlockSpec((2 * rows, model), lambda i, ids: (i, 0))
    units_spec = pl.BlockSpec((hidden, 2 * rows), lambda i, ids: (0, i))
    half_spec = pl.BlockSpec((rows, model), lambda i, ids: (i, 0))
    outs = [((2 * rows, model), f32, half_spec), ((total, model), bf16, rows_spec)]
    outs += [((hidden, total), bf16, units_spec)] * 3
    outs += [((2 * rows, model), bf16, half_spec)] * 4
    ins = [(a, whole(a.shape)) for chunk in range(2) for a in contexts[chunk]]
    ins += [(x_all, rows_spec), (cot_all, rows_spec)]
    ins += [(w, whole(w.shape)) for w in (*w_outs, gain, w_gate_t, w_up_t, w_down)]
    return call(ffn_kernel, ids, ins, outs, (2,), "ffn")


def norm_back(total, values, gain):
    r = scale_of(values)
    n = values * r
    e = gain * total
    return r * (e - n * jnp.mean(n * e, axis=-1, keepdims=True)), jnp.sum(total * n, axis=0, keepdims=True)


def mid_kernel(ids, a_ref, b_ref, mixed_ref, cot_ref, g_ref, dm_ref, da_ref, sum_ref):
    total = a_ref[...].astype(f32) + b_ref[...].astype(f32)
    grad, gain_sum = norm_back(total, mixed_ref[...], g_ref[...])
    d_mixed = cot_ref[...].astype(f32) + grad
    dm_ref[...] = d_mixed
    da_ref[...] = d_mixed.astype(bf16)
    step = pl.program_id(0)
    gain_sum = jnp.where(ids[2] == step, gain_sum, 0.0)

    @pl.when(step == 0)
    def _():
        sum_ref[...] = gain_sum

    @pl.when(step > 0)
    def _():
        sum_ref[...] += gain_sum


def mid(ids, own, far, mixed, cot_all, gain):
    total, model = own.shape
    rows = total // 2
    spec = pl.BlockSpec((rows, model), lambda i, ids: (i, 0))
    cot_spec = pl.BlockSpec((rows, model), lambda i, ids: (2 * i + ids[1], 0))
    ins = [(own, spec), (far, spec), (mixed, spec), (cot_all, cot_spec), (gain, whole(gain.shape))]
    outs = [((total, model), f32, spec), ((total, model), bf16, spec), ((1, model), f32, whole((1, model)))]
    return call(mid_kernel, ids, ins, outs, (2,), "mid")


def back_kernel(ids, a_ref, b_ref, wa_ref, wb_ref, *outs):
    total = dot_nt(a_ref[...], wa_ref[...]) + dot_nt(b_ref[...], wb_ref[...])
    rows = total.shape[0] // 2
    first = ids[1] == 0
    other = jnp.where(first, total[rows:], total[:rows]).astype(bf16)
    own = jnp.where(first, total[:rows], total[rows:])
    for at_step in range(2):

        @pl.when(pl.program_id(0) == at_step)
        def _():
            outs[2 * at_step][...] = other
            outs[2 * at_step + 1][...] = own


def project_back(ids, grads, weights):
    total = grads.shape[0]
    rows, (model, width) = total // 4, weights[0].shape
    ins = [(grads, pl.BlockSpec((2 * rows, width), lambda i, ids, at=at: ((1 - i + ids[2]) % 2, at))) for at in range(2)]
    ins += [(w, whole(w.shape)) for w in weights]
    outs = [((rows, model), kind, whole((rows, model))) for kind in (bf16, f32, bf16, f32)]
    return call(back_kernel, ids, ins, outs, (2,), "project_back")


def last_kernel(ids, keep_ref, core_ref, y_ref, x_ref, g_ref, dm_ref, out_ref, sum_ref):
    total = keep_ref[...] + core_ref[...].astype(f32) + y_ref[...].astype(f32)
    grad, gain_sum = norm_back(total, x_ref[...].astype(f32), g_ref[...])
    out_ref[...] = dm_ref[...] + grad
    sum_ref[...] = gain_sum


def last(ids, keep, core, far, x, gain, d_mixed):
    ins = [(a, whole(a.shape)) for a in (keep, core, far, x, gain)]
    ins.append((d_mixed, pl.BlockSpec(keep.shape, lambda i, ids: (ids[2], 0))))
    outs = [(shape, f32, whole(shape)) for shape in (keep.shape, (1, keep.shape[1]))]
    return call(last_kernel, ids, ins, outs, (1,), "last")


def bit_orders(shards):
    bits = list(range(shards.bit_length() - 1))
    return bits, bits[1:] + bits[:1]


def slot_of(flip, order):
    place = 0
    for bit in order[1:]:
        place = 2 * place + (flip >> bit) % 2
    return (flip >> order[0]) % 2, place


def unit_parts_kernel(ids, *refs):
    n = 3
    kept_a, sent_a, kept_b, sent_b = refs[2 * n :]
    step = pl.program_id(0)
    low, high = step % 2, step // 2
    even = ids[3] % 2 == 0
    nears, fars = [], []
    for i in range(n):
        out = dot(refs[i][...], refs[n + i][...]).astype(bf16)
        width, cut = out.shape[1] // 2, out.shape[0] // 2
        first, second = out[:, :width], out[:, width:]
        nears.append(jnp.where(even, first, second))
        fars.append(jnp.where(even, second, first))
        kept_a[2 * low + high, i] = nears[i][:cut]
        sent_a[2 * low + high, i] = fars[i][:cut]

    @pl.when(low == 0)
    def _():
        for i in range(n):
            kept_b[2 * high, i] = nears[i][cut:]
            kept_b[2 * high + 1, i] = fars[i][cut:]

    @pl.when(low == 1)
    def _():
        for i in range(n):
            sent_b[2 * high, i] = nears[i][cut:]
            sent_b[2 * high + 1, i] = fars[i][cut:]


def unit_parts(ids, lefts, rights):
    n = len(lefts)
    total, model = rights[0].shape
    hidden = lefts[0].shape[0]
    shape = (4, n, hidden // 2, model // 8)
    return pl.pallas_call(
        unit_parts_kernel,
        out_shape=[jax.ShapeDtypeStruct(shape, bf16)] * 4,
        grid_spec=pltpu.PrefetchScalarGridSpec(
            num_scalar_prefetch=1,
            grid=(4,),
            in_specs=[whole(a.shape) for a in lefts] + [pl.BlockSpec((total, model // 4), lambda i, ids: (0, i ^ (ids[3] // 2)))] * n,
            out_specs=[whole(shape)] * 4,
        ),
        compiler_params=params(),
        cost_estimate=estimate(),
        name="unit_parts",
    )(ids, *lefts, *rights)


def unit_sums_kernel(n, split, *refs):
    out_ref = refs[-1]
    for i in range(n):
        out = dot(refs[i][...], refs[n + i][...]).astype(bf16)
        width = out.shape[1] // split
        for part in range(split):
            out_ref[part, i] = out[:, part * width : part * width + width]


def unit_sums(lefts, rights, shards):
    n = len(lefts)
    total, model = rights[0].shape
    hidden = lefts[0].shape[0]
    cut = model // shards
    step = 256
    split = step // cut if cut % 128 == 0 else 1
    out = pl.pallas_call(
        functools.partial(unit_sums_kernel, n, split),
        out_shape=jax.ShapeDtypeStruct((model // step * split, n, hidden, step // split), bf16),
        grid=(model // step,),
        in_specs=[whole(a.shape) for a in lefts] + [pl.BlockSpec((total, step), lambda i: (0, i))] * n,
        out_specs=pl.BlockSpec((split, n, hidden, step // split), lambda i: (i, 0, 0, 0)),
        compiler_params=params(),
        cost_estimate=estimate(),
        name="unit_sums",
    )(*lefts, *rights)
    if split == 1:
        out = out.reshape(model // step, n, hidden, step // cut, cut)
        out = out.transpose(0, 3, 1, 2, 4).reshape(shards, n, hidden, cut)
    return out


def head_sums_kernel(shards, ids, normed_ref, da_ref, g_ref, ctx_ref, ka_ref, sa_ref, kb_ref, sb_ref, acc, turned):
    outs = ((ka_ref, sa_ref), (kb_ref, sb_ref))
    cut = acc.shape[0] // shards
    turned[...] = normed_ref[...].T
    acc[:, 0:768] = dot(turned[...], g_ref[...])
    turned[...] = da_ref[...].T
    acc[:, 768:] = dot(turned[...], ctx_ref[...])
    for group, order in enumerate(bit_orders(shards)):
        for flip in range(shards):
            sent, place = slot_of(flip, order)
            at = (ids[3] ^ flip) * cut + group * (cut // 2)
            rows = pl.ds(pl.multiple_of(at, cut // 2), cut // 2)
            outs[group][sent][place] = acc[rows, :].astype(bf16)


def head_sums(ids, normed, d_attn, grads, context, shards):
    total, model = normed.shape
    columns = grads.shape[1] + context.shape[1]
    shape = (shards // 2, model // shards // 2, columns)
    ins = [(a, whole(a.shape)) for a in (normed, d_attn, grads, context)]
    return pl.pallas_call(
        functools.partial(head_sums_kernel, shards),
        out_shape=[jax.ShapeDtypeStruct(shape, bf16)] * 4,
        grid_spec=pltpu.PrefetchScalarGridSpec(
            num_scalar_prefetch=1,
            grid=(1,),
            in_specs=[spec for _, spec in ins],
            out_specs=[whole(shape)] * 4,
            scratch_shapes=[pltpu.VMEM((model, columns), f32), pltpu.VMEM((model, total), bf16)],
        ),
        compiler_params=params(),
        cost_estimate=estimate(),
        name="head_sums",
    )(ids, *(a for a, _ in ins))


def heads_kernel(shards, ids, g_ref, wa_ref, wb_ref, normed_ref, da_ref, ctx_ref, fs_ref, fk_ref, ns_ref, nk_ref, ka_ref, sa_ref, kb_ref, sb_ref, acc, turned):
    step = pl.program_id(0)
    rows = fs_ref.shape[0]
    width = wa_ref.shape[1]
    for at_step, (send, keep) in enumerate(((fs_ref, fk_ref), (ns_ref, nk_ref))):

        @pl.when(step == at_step)
        def _():
            at = pl.ds(pl.multiple_of((1 - at_step + ids[2]) % 2 * 2 * rows, 2 * rows), 2 * rows)
            total = dot_nt(g_ref[at, 0:width], wa_ref[...]) + dot_nt(g_ref[at, width:], wb_ref[...])
            lower = ids[1] == 0
            send[...] = jnp.where(lower, total[rows:], total[:rows]).astype(bf16)
            keep[...] = jnp.where(lower, total[:rows], total[rows:])

    @pl.when(step == 2)
    def _():
        head_sums_kernel(shards, ids, normed_ref, da_ref, g_ref, ctx_ref, ka_ref, sa_ref, kb_ref, sb_ref, acc, turned)


def heads_back(ids, grads, weights, normed, d_attn, context, shards):
    total, model = normed.shape
    rows = total // 4
    columns = grads.shape[1] + context.shape[1]
    shape = (shards // 2, model // shards // 2, columns)
    ins = [(a, whole(a.shape)) for a in (grads, *weights, normed, d_attn, context)]
    outs = [((rows, model), kind) for kind in (bf16, f32, bf16, f32)] + [(shape, bf16)] * 4
    return pl.pallas_call(
        functools.partial(heads_kernel, shards),
        out_shape=[jax.ShapeDtypeStruct(*out) for out in outs],
        grid_spec=pltpu.PrefetchScalarGridSpec(
            num_scalar_prefetch=1,
            grid=(3,),
            in_specs=[spec for _, spec in ins],
            out_specs=[whole(out[0]) for out in outs],
            scratch_shapes=[pltpu.VMEM((model, columns), f32), pltpu.VMEM((model, total), bf16)],
        ),
        compiler_params=params(),
        cost_estimate=estimate(),
        name="heads_back",
    )(ids, *(a for a, _ in ins))


def swap(sent, bit, n_dp):
    return lax.ppermute(sent, "dp", [(i, i ^ (1 << bit)) for i in range(n_dp)])


def call(kernel, ids, ins, outs, grid, name):
    return pl.pallas_call(
        kernel,
        out_shape=[jax.ShapeDtypeStruct(shape, kind) for shape, kind, _ in outs],
        grid_spec=pltpu.PrefetchScalarGridSpec(
            num_scalar_prefetch=1,
            grid=grid,
            in_specs=[spec for _, spec in ins],
            out_specs=[spec for _, _, spec in outs],
        ),
        compiler_params=params(),
        cost_estimate=estimate(),
        name=name,
    )(ids, *(array for array, _ in ins))


def out_kernel(ids, ka_ref, ca_ref, kb_ref, cb_ref, send_ref, own_ref):
    sum_a = ka_ref[...].astype(f32) + ca_ref[...].astype(f32)
    sum_b = kb_ref[...].astype(f32) + cb_ref[...].astype(f32)
    first = ids[2] == 0
    send_ref[...] = jnp.where(first, sum_b, sum_a).astype(bf16)
    own_ref[...] = jnp.where(first, sum_a, sum_b)


def out_sums(ids, keep, core):
    rows, model = keep.shape[0] // 2, keep.shape[1]
    low = pl.BlockSpec((rows // 2, model), lambda i, ids: (i, 0))
    high = pl.BlockSpec((rows // 2, model), lambda i, ids: (2 + i, 0))
    ins = [(keep, low), (core, low), (keep, high), (core, high)]
    return call(out_kernel, ids, ins, [((rows, model), bf16, low), ((rows, model), f32, low)], (2,), "out_sums")


def result_kernel(ids, mixed_ref, own_ref, far_ref, out_ref):
    out_ref[...] = mixed_ref[...] + own_ref[...] + far_ref[...].astype(f32)


def result_of(ids, mixed, own, far):
    rows, model = own.shape
    spec = pl.BlockSpec((rows // 2, model), lambda i, ids: (i, 0))
    ins = [(mixed, pl.BlockSpec((rows // 2, model), lambda i, ids: (2 * ids[2] + i, 0))), (own, spec), (far, spec)]
    return call(result_kernel, ids, ins, [(own.shape, f32, spec)], (2,), "result_of")[0]


def onward_kernel(n, ids, *refs):
    for i in range(n):
        low, high, came_low, came_high = refs[4 * i : 4 * i + 4]
        keep, send = refs[4 * n + 2 * i : 4 * n + 2 * i + 2]
        keep[...] = (low[...].astype(f32) + came_low[...].astype(f32)).astype(bf16)
        send[...] = (high[...].astype(f32) + came_high[...].astype(f32)).astype(bf16)


def onward(ids, kept, came):
    ins, outs = [], []
    half = kept[0].shape[0] // 2
    for k, c in zip(kept, came, strict=True):
        block = (1,) + k.shape[1:]
        rest = (0,) * (k.ndim - 1)
        low = pl.BlockSpec(block, lambda i, ids, rest=rest: (i,) + rest)
        high = pl.BlockSpec(block, lambda i, ids, rest=rest: (half + i,) + rest)
        ins += [(k, low), (k, high), (c, low), (c, high)]
        outs += [((half,) + k.shape[1:], bf16, low)] * 2
    got = call(functools.partial(onward_kernel, len(kept)), ids, ins, outs, (half,), "onward")
    return got[0::2], got[1::2]


def unit_last_kernel(ids, ka, ca, kb, cb, *outs):
    cut = ka.shape[2]
    for i, out in enumerate(outs):
        out[0:cut, :] = ka[0, i].astype(f32) + ca[0, i].astype(f32)
        out[cut:, :] = kb[0, i].astype(f32) + cb[0, i].astype(f32)


def unit_last(ids, kept, came):
    _, n, cut, columns = kept[0].shape
    ins = [(a, whole(a.shape)) for a in (kept[0], came[0], kept[1], came[1])]
    outs = [((2 * cut, columns), f32, whole((2 * cut, columns)))] * n
    return call(unit_last_kernel, ids, ins, outs, (1,), "unit_last")


def head_last_kernel(ids, ka, ca, kb, cb, *outs):
    rows = ka.shape[1]
    both = jnp.concatenate([k[0].astype(f32) + c[0].astype(f32) for k, c in ((ka, ca), (kb, cb))], axis=0)
    for i, out in enumerate(outs[:3]):
        out[:, 0:128] = both[:, 128 * i : 128 * i + 128]
        out[:, 128:256] = both[:, 384 + 128 * i : 512 + 128 * i]
    outs[3][...] = both[:, 768:].T


def head_last(ids, kept, came):
    _, rows, columns = kept[0].shape
    ins = [(a, whole(a.shape)) for a in (kept[0], came[0], kept[1], came[1])]
    outs = [((2 * rows, 256), f32, whole((2 * rows, 256)))] * 3 + [((256, 2 * rows), f32, whole((256, 2 * rows)))]
    return call(head_last_kernel, ids, ins, outs, (1,), "head_last")


def local(
    tokens, w_query, w_key, w_value, w_attn_out, w_gate, w_up, w_down, norm_attn, norm_ffn,
    rel_table, x_table, y_table, lengths, boxes, cotangent,
):
    n_mp, n_dp = lax.axis_size("mp"), lax.axis_size("dp")
    me = lax.axis_index("mp")
    core, chip = me % 2, me // 2
    ids = jnp.stack([me, core, chip, lax.axis_index("dp")]).astype(i32)
    rows, model = tokens.shape

    def by_core(a):
        return lax.ppermute(a, "mp", [(i, i ^ 1) for i in range(n_mp)])

    def by_chip(a):
        return lax.ppermute(a, "mp", [(i, i ^ 2) for i in range(n_mp)])

    def together(*arrays):
        return lax.optimization_barrier(arrays)

    def after(a, *earlier):
        return lax.optimization_barrier((a, *earlier))[0]

    def exchange_small(a):
        return lax.all_to_all(a, ("dp", "mp"), split_axis=0, concat_axis=0, tiled=True)

    n_heads = w_query.shape[1] // HEAD
    tables = jnp.concatenate([rel_table.T, x_table.T, y_table.T, jnp.zeros((16 - 3 * n_heads, NB), f32)], axis=0)
    box_cols = boxes.T
    gain_attn, gain_ffn = norm_attn.reshape(1, model), norm_ffn.reshape(1, model)
    weights = (w_query, w_key, w_value)
    w_gate_t, w_up_t = w_gate.T, w_up.T

    x_chip = by_chip(tokens)
    group = project(ids, False, (tokens, by_core(tokens)), gain_attn, weights, [], n_mp)
    w_pairs = [jnp.concatenate([w[:, at : at + 128] for w in weights], axis=1) for at in (0, 128)]
    x_chip, _, box_cols, tables, *w_pairs = together(x_chip, group[0], box_cols, tables, *w_pairs)
    x_both = by_core(x_chip)
    w_chip = by_chip(after(w_attn_out, x_chip))
    c_chip = by_chip(after(cotangent, x_chip))
    group = project(ids, True, (x_chip, x_both), gain_attn, weights, group, n_mp)
    x_all, normed, queries, keys_all, values_all = group

    *kept, own_a = attend(0, queries, keys_all, values_all, tables, lengths, box_cols, boxes, [])
    core_a, far_a = by_core(own_a), by_chip(own_a)
    *kept, own_b = attend(1, after(queries, own_a), keys_all, values_all, tables, lengths, box_cols, boxes, kept)
    context, ctxt, factors, probs = kept
    own_b, core_a, far_a, w_chip, c_chip = together(own_b, core_a, far_a, w_chip, c_chip)
    core_b, far_b = by_core(own_b), by_chip(own_b)
    w_outs = (w_attn_out, by_core(w_attn_out), w_chip, by_core(w_chip))
    cot_all = assemble(ids, (cotangent, by_core(cotangent), c_chip, by_core(c_chip)))
    both_a = by_core(far_a)
    cot_all, far_b = together(cot_all, far_b)
    contexts = ((own_a, core_a, far_a, both_a), (own_b, core_b, far_b, by_core(far_b)))

    out = ffn(ids, contexts, x_all, cot_all, w_outs, gain_ffn, w_gate_t, w_up_t, w_down)
    mixed, normed_ffn, hidden, d_gate, d_up, d_send, d_keep, r_send, r_keep = out
    d_core = by_core(d_send)
    sums = (d_keep.astype(f32) + d_core.astype(f32)).astype(bf16)
    far_sums = by_chip(sums)
    r_core = by_core(after(r_send, sums))

    orders = bit_orders(n_dp)
    pairwise = n_dp == 8 and model == 1024
    unit_args = ((d_gate, d_up, hidden), (normed_ffn, normed_ffn, after(cot_all, sums)))
    if pairwise:
        unit = list(unit_parts(ids, *unit_args))
        r_out, r_own = out_sums(ids, r_keep, r_core)
        unit[0], unit[2], far_sums, r_out = together(unit[0], unit[2], far_sums, r_out)
        unit_came = [swap(unit[2 * i + 1], order[0], n_dp) for i, order in enumerate(orders)]
    else:
        unit = [unit_sums(*unit_args, n_dp)]
        r_out, r_own = out_sums(ids, r_keep, r_core)
        *unit, far_sums, r_out = together(*unit, far_sums, r_out)
        ffn_sums = lax.psum_scatter(unit[0], "dp", scatter_dimension=0, tiled=True)[0].astype(f32)
    d_mixed, d_own, gain_mid = mid(ids, sums, far_sums, mixed, cot_all, gain_ffn)
    d_core = by_core(d_own)

    r_far = by_chip(r_out)
    d_heads, d_tab, d_attn = attend_back(
        ids, queries, keys_all, values_all, d_own, d_core, w_attn_out, ctxt, factors, probs, lengths, box_cols, boxes
    )
    d_heads, r_far = together(d_heads, r_far)

    def swaps(sends, step):
        return [swap(send, order[step], n_dp) for send, order in zip(sends, orders, strict=True)]

    d_first = d_heads
    if pairwise:
        unit_came = together(*unit_came, d_heads)[:2]
        unit_kept, sends = onward(ids, unit[0::2], unit_came)
        unit_came = swaps(sends, 1)
        d_first = after(d_heads, *sends)
    if pairwise:
        f_send, f_keep, n_send, n_keep, *attn = heads_back(ids, d_first, w_pairs, normed, d_attn, context, n_dp)
    else:
        f_send, f_keep, n_send, n_keep = project_back(ids, d_first, w_pairs)
    f_core, n_core = by_core(f_send), by_core(n_send)
    if pairwise:
        result = result_of(ids, mixed, r_own, after(r_far, attn[0]))
        *unit_came, result = together(*unit_came, result)
        unit_kept, sends = onward(ids, unit_kept, unit_came)
        unit_came = swaps(sends, 2)
        f_core, n_core = together(f_core, n_core, *sends)[:2]
        came = swaps(attn[1::2], 0)
    f_sum = (f_keep + f_core.astype(f32)).astype(bf16)
    far = by_chip(f_sum)
    if pairwise:
        came[0], came[1], f_sum = together(*came, f_sum)
        kept, sends = onward(ids, attn[0::2], came)
        came = swaps(sends, 1)
        far = after(far, *sends)
    d_tokens, gain_first = last(ids, n_keep, n_core, far, tokens, gain_attn, d_mixed)

    gains = jnp.concatenate([gain_first, gain_mid], axis=0).reshape(2, n_dp, n_mp, -1).transpose(1, 2, 0, 3)
    n_gain = gains.shape[3]
    tabs = d_tab[:, : 3 * n_heads].reshape(n_dp, 1, -1)
    tabs = jnp.where(lax.broadcasted_iota(i32, (1, n_mp, 1), 1) == me, tabs, 0.0)
    small = jnp.concatenate([gains.reshape(n_dp, n_mp, 2 * n_gain), tabs], axis=2).reshape(n_dp * n_mp, -1)
    if pairwise:
        small = exchange_small(small)
        kept, sends = onward(ids, kept, came)
        came = swaps(sends, 2)
        small = after(small, *sends).sum(axis=0)
        unit_came[0] = after(unit_came[0], small)
        ffn_sums = unit_last(ids, unit_kept, unit_came)
        came[0], came[1], *ffn_sums = together(*came, *ffn_sums)
        attn_sums = head_last(ids, kept, came)
    else:
        result = result_of(ids, mixed, r_own, r_far)
        wide = dot_tn(normed, d_heads)
        parts = [wide[:, 384 * pair + 128 * i : 384 * pair + 128 * i + 128] for i in range(3) for pair in range(2)]
        wide = [*parts, dot_tn(d_attn, context)]
        wide = jnp.concatenate(wide, axis=1).astype(bf16)
        wide = lax.psum_scatter(wide, "dp", scatter_dimension=0, tiled=True).astype(f32)
        attn_sums = [wide[:, 256 * i : 256 * i + 256] for i in range(4)]
        attn_sums[3] = attn_sums[3].T
        small = exchange_small(small).sum(axis=0)
    tabs = small[2 * n_gain :].reshape(-1, 3, n_heads)
    return (
        result, d_tokens,
        *attn_sums,
        ffn_sums[0].T, ffn_sums[1].T, ffn_sums[2],
        small[:n_gain], small[n_gain : 2 * n_gain], tabs[:, 0], tabs[:, 1], tabs[:, 2],
    )


def solution(mesh):
    in_specs = (
        P(("dp", "mp"), None),
        P(None, "mp"),
        P(None, "mp"),
        P(None, "mp"),
        P("mp", None),
        P(None, "mp"),
        P(None, "mp"),
        P("mp", None),
        P(),
        P(),
        P(None, "mp"),
        P(None, "mp"),
        P(None, "mp"),
        P("dp", None),
        P(None, "dp"),
        P(("dp", "mp"), None),
    )
    out_specs = (
        P(("dp", "mp"), None),
        P(("dp", "mp"), None),
        P("dp", "mp"),
        P("dp", "mp"),
        P("dp", "mp"),
        P("mp", "dp"),
        P("dp", "mp"),
        P("dp", "mp"),
        P("mp", "dp"),
        P(("dp", "mp")),
        P(("dp", "mp")),
        P("dp", "mp"),
        P("dp", "mp"),
        P("dp", "mp"),
    )
    return jax.shard_map(local, mesh=mesh, in_specs=in_specs, out_specs=out_specs, check_vma=False)
```
